768 devices in a mesh: gx: 24 (over z, core), gy: 8 (over x, y_lo), gz: 4 (over y_hi).
Axes of the slice: x: 4, y: 8 (y_hi: 4, y_lo: 2; y = y_hi * 2 + y_lo), z: 12, core: 2. Of those that a mesh axis runs over, the one named last changes fastest.
Arguments:
- positions: float32 [24, 8, 8, 192], P('gx', 'gy', 'gz'), may hold values from 0 to 1, as said below
- species: int32 [24, 8, 8, 64], P('gx', 'gy', 'gz'), may hold values from 0 to 4
- neighbors: int32 [24, 8, 8, 512], P('gx', 'gy', 'gz'), may hold values from 0 to 1727, as said below
- center_table: bfloat16 [5, 128], replicated, may hold values from -4 to 4
- neighbor_table: bfloat16 [5, 128], replicated, may hold values from -4 to 4
- radial_weight: bfloat16 [8, 128], replicated, may hold values from -2 to 2
- mix_weight: bfloat16 [128, 128], replicated, may hold values from -0.5 to 0.5
- env_weight: bfloat16 [128, 128], replicated, may hold values from -0.5 to 0.5
- update_weight: bfloat16 [384, 128], replicated, may hold values from -0.3125 to 0.3125
- second_weight: bfloat16 [128, 128], replicated, may hold values from -0.5 to 0.5
- readout: float32 [128], replicated, may hold values from -0.5 to 0.5
Outputs:
- atom_energy: float32 [24, 8, 8, 64], P('gx', 'gy', 'gz')
- forces: float32 [24, 8, 8, 192], P('gx', 'gy', 'gz')
The draws below stay inside these ranges and needn't reach their ends.
Inputs may be any that keep to these rules, and one draw needn't show every extreme that they name: `positions`: every coordinate lies inside its block; atoms of a block sit on a jittered sublattice, so any two atoms are at least 0.4 / cube root of 64 apart. `neighbors`: each atom lists 8 different atoms of the 27 blocks around and including its own, never itself; a code is offset index times 64 plus slot.
All inputs are finite; a program needn't handle non-finite values.
Results may differ from the reference program's by a relative error of at most 0.011.
Values may be sent and summed in bfloat16 or wider, within the bound.
A program may use at most 32 MiB of HBM per device.

```python
import math
import jax
import jax.numpy as jnp
from jax import lax

SLOTS = 64
NEIGH = 8
WIDTH = 128
NBASIS = 8
NSPEC = 5
NX = 24
NY = 8
NZ = 8


def draw_positions(key, part):
    side = 2 if SLOTS == 8 else 3 if SLOTS == 27 else 4
    lattice_ids = jnp.arange(SLOTS, dtype=jnp.int32)
    lattice = jnp.stack([lattice_ids // (side * side), lattice_ids // side % side, lattice_ids % side]).astype(jnp.float32)
    jitter = jax.random.uniform(key, (NX, NY, NZ, 3, SLOTS), jnp.float32, -0.3, 0.3)
    placed = (lattice + 0.5 + jitter) / side
    return placed.reshape(NX, NY, NZ, 3 * SLOTS)


def draw_neighbors(key, part):
    span = 27 * SLOTS - 1
    start_key = jax.random.fold_in(key, 11)
    stride_key = jax.random.fold_in(key, 23)
    starting = jax.random.randint(start_key, (NX, NY, NZ, SLOTS, 1), 0, span, jnp.int32)
    stride = jax.random.randint(stride_key, (NX, NY, NZ, SLOTS, 1), 1, (span - 1) // (NEIGH - 1) + 1, jnp.int32)
    ranks = jnp.arange(NEIGH, dtype=jnp.int32)
    candidate = (starting + ranks * stride) % span
    self_code = 13 * SLOTS + jnp.arange(SLOTS, dtype=jnp.int32)[:, None]
    codes = candidate + (candidate >= self_code).astype(jnp.int32)
    return codes.reshape(NX, NY, NZ, SLOTS * NEIGH)


def place_ends(entries, own_key, low, high):
    spot = [jax.random.randint(jax.random.fold_in(own_key, axis), (), 0, length) for axis, length in enumerate(entries.shape)]
    longest = entries.shape.index(max(entries.shape))
    next_to = spot[:longest] + [(spot[longest] + 1) % entries.shape[longest]] + spot[longest + 1:]
    return entries.at[tuple(spot)].set(low).at[tuple(next_to)].set(high)


def gaussian(own_key, shape, spread, bound, kind=jnp.bfloat16):
    array = jax.random.normal(own_key, shape, jnp.float32) * spread
    return jnp.minimum(jnp.maximum(array, -bound), bound).astype(kind)


def setup_inputs(seed: int = 0) -> dict:
    key_of = jax.random.split(jax.random.key(seed), 12)
    return {
        "positions": draw_positions(jax.random.fold_in(key_of[11], 71), 0),
        "species": place_ends(jax.random.randint(key_of[1], (NX, NY, NZ, SLOTS), 0, NSPEC), jax.random.fold_in(key_of[1], 1), 0, NSPEC - 1).astype(jnp.int32),
        "neighbors": draw_neighbors(jax.random.fold_in(key_of[11], 71), 0),
        "center_table": gaussian(key_of[3], (NSPEC, WIDTH), 1.0, 4.0),
        "neighbor_table": gaussian(key_of[4], (NSPEC, WIDTH), 1.0, 4.0),
        "radial_weight": gaussian(key_of[5], (NBASIS, WIDTH), NBASIS ** -0.5, 2.0),
        "mix_weight": gaussian(key_of[6], (WIDTH, WIDTH), WIDTH ** -0.5, 0.5),
        "env_weight": gaussian(key_of[7], (WIDTH, WIDTH), WIDTH ** -0.5, 0.5),
        "update_weight": gaussian(key_of[8], (3 * WIDTH, WIDTH), (3 * WIDTH) ** -0.5, 0.3125),
        "second_weight": gaussian(key_of[9], (WIDTH, WIDTH), WIDTH ** -0.5, 0.5),
        "readout": gaussian(key_of[10], (WIDTH,), WIDTH ** -0.5, 0.5, jnp.float32),
    }


CUTOFF = 4.0
SHARPNESS = 2.0
HIGH = lax.Precision.HIGHEST

def harmonics(displacement):
    distance = jnp.sqrt(lax.optimization_barrier(jnp.sum(displacement * displacement, axis=0)))
    unit_vec = displacement / distance
    unit_x, unit_y, unit_z = (unit_vec[0], unit_vec[1], unit_vec[2])
    root_three = math.sqrt(3.0)
    angular = jnp.stack([jnp.ones_like(unit_x), unit_x, unit_y, unit_z, root_three * unit_x * unit_y, root_three * unit_y * unit_z, 0.5 * (3.0 * unit_z * unit_z - 1.0), root_three * unit_x * unit_z, 0.5 * root_three * (unit_x * unit_x - unit_y * unit_y)], axis=0)
    return (distance, angular)

def layer_one(displacement, onehot_center, onehot_other, params):
    radial_weight, center_table, neighbor_table, mix_weight, env_weight, update_weight = params
    distance, angular = harmonics(displacement)
    nbasis = radial_weight.shape[0]
    centers = CUTOFF * (jnp.arange(nbasis, dtype=jnp.float32) + 0.5) / nbasis
    cut_ratio = distance / CUTOFF
    envelope = (1.0 - cut_ratio * cut_ratio) ** 2
    radial_basis = jnp.exp(-SHARPNESS * (distance[:, None] - centers[None, :]) ** 2) * envelope[:, None]
    before = jnp.dot(radial_basis.astype(jnp.bfloat16), radial_weight, preferred_element_type=jnp.float32)
    before = before + jnp.dot(onehot_center, center_table, preferred_element_type=jnp.float32)
    before = before + jnp.dot(onehot_other, neighbor_table, preferred_element_type=jnp.float32)
    activated = jax.nn.silu(before).astype(jnp.bfloat16)
    latent = jax.nn.silu(jnp.dot(activated, mix_weight, preferred_element_type=jnp.float32))
    env_terms = jnp.dot(latent.astype(jnp.bfloat16), env_weight, preferred_element_type=jnp.float32)
    channels = latent.shape[1]
    center_count = latent.shape[0] // NEIGH
    env_terms = env_terms.reshape(center_count, NEIGH, channels)
    harmonic_grid = angular.reshape(9, center_count, NEIGH)
    environment = jnp.einsum('akc,mak->amc', env_terms, harmonic_grid, precision=HIGH) / NEIGH
    pieces = []
    for start_m, stop_m in ((0, 1), (1, 4), (4, 9)):
        pieces.append(jnp.einsum('amc,mak->akc', environment[:, start_m:stop_m], harmonic_grid[start_m:stop_m], precision=HIGH))
    invariants = jnp.concatenate(pieces, axis=2).reshape(center_count * NEIGH, 3 * channels)
    invariants = invariants.astype(jnp.bfloat16)
    update = jnp.dot(invariants, update_weight, preferred_element_type=jnp.float32)
    edge_latent = jax.nn.silu(latent + update)
    atom_latent = lax.optimization_barrier(jnp.mean(edge_latent.reshape(center_count, NEIGH, channels), axis=1))
    return (atom_latent, edge_latent)

def layer_two(edge_latent, other_latent, second_weight, readout):
    product = (edge_latent * other_latent).astype(jnp.bfloat16)
    hidden = jax.nn.silu(jnp.dot(product, second_weight, preferred_element_type=jnp.float32))
    edge_energy = jnp.dot(hidden, readout, precision=HIGH)
    return lax.optimization_barrier(jnp.sum(edge_energy.reshape(-1, NEIGH), axis=1))

def edge_model(rel_center, rel_other, offsets, onehot_center, onehot_other, params):
    displacement = (offsets + (rel_other - rel_center[:, :, None])).reshape(3, -1)
    return layer_one(displacement, onehot_center, onehot_other, params)

def one_hot(labels, count):
    return (labels[:, None] == jnp.arange(count, dtype=jnp.int32)[None, :]).astype(jnp.bfloat16)

def slab_lists(neighbors, species_flat, slab):
    codes = lax.dynamic_index_in_dim(neighbors, slab, 0, keepdims=False).reshape(NY, NZ, SLOTS, NEIGH)
    offset_code = codes // SLOTS
    slot_other = codes % SLOTS
    step_x = offset_code // 9 - 1
    step_y = offset_code // 3 % 3 - 1
    step_z = offset_code % 3 - 1
    index_y = jnp.arange(NY, dtype=jnp.int32).reshape(NY, 1, 1, 1)
    index_z = jnp.arange(NZ, dtype=jnp.int32).reshape(1, NZ, 1, 1)
    cell_other = ((slab + step_x) % NX * NY + (index_y + step_y) % NY) * NZ + (index_z + step_z) % NZ
    per_slab = NY * NZ * SLOTS
    other_index = (cell_other * SLOTS + slot_other).reshape(per_slab, NEIGH).astype(jnp.int32)
    own_index = (slab * per_slab + jnp.arange(per_slab, dtype=jnp.int32)).astype(jnp.int32)
    offsets = jnp.stack([step_x, step_y, step_z]).astype(jnp.float32).reshape(3, per_slab, NEIGH)
    center_species = jnp.broadcast_to(species_flat[own_index][:, None], (per_slab, NEIGH)).reshape(-1)
    onehot_center = one_hot(center_species, NSPEC)
    onehot_other = one_hot(species_flat[other_index.reshape(-1)], NSPEC)
    return (own_index, other_index, offsets, onehot_center, onehot_other)

def reference(positions, species, neighbors, center_table, neighbor_table, radial_weight, mix_weight, env_weight, update_weight, second_weight, readout):
    params = (radial_weight, center_table, neighbor_table, mix_weight, env_weight, update_weight)
    total = NX * NY * NZ * SLOTS
    flat_pos = positions.reshape(NX, NY, NZ, 3, SLOTS).transpose(3, 0, 1, 2, 4).reshape(3, total)
    species_flat = species.reshape(total)
    slabs = jnp.arange(NX, dtype=jnp.int32)

    def prepare(slab):
        lists = slab_lists(neighbors, species_flat, slab)
        rel_center = flat_pos[:, lists[0]]
        rel_other = flat_pos[:, lists[1]]
        return (lists, rel_center, rel_other)

    def first_pass(slab):
        lists, rel_center, rel_other = prepare(slab)
        return edge_model(rel_center, rel_other, lists[2], lists[3], lists[4], params)[0]
    atom_latent = lax.map(first_pass, slabs).reshape(total, WIDTH)
    coarse_latent = lax.optimization_barrier(atom_latent.astype(jnp.bfloat16)).astype(jnp.float32)

    def both_layers(slab):
        lists, rel_center, rel_other = prepare(slab)

        def first(center_pos, other_pos):
            return edge_model(center_pos, other_pos, lists[2], lists[3], lists[4], params)
        outputs, back_one = jax.vjp(first, rel_center, rel_other)
        other_latent = coarse_latent[lists[1].reshape(-1)]

        def second(edge_latent, neighbor_latent):
            return layer_two(edge_latent, neighbor_latent, second_weight, readout)
        energy, back_two = jax.vjp(second, outputs[1], other_latent)
        grad_edge, grad_other = back_two(jnp.ones_like(energy))
        return (lists, energy, grad_edge, grad_other, back_one)

    def gather_step(carry, slab):
        lists, energy, grad_edge, grad_other, back_one = both_layers(slab)
        carry = carry.at[lists[1].reshape(-1)].add(grad_other)
        return (carry, energy)
    latent_grad, energies = lax.scan(gather_step, jnp.zeros((total, WIDTH), jnp.float32), slabs)

    def force_step(carry, slab):
        lists, energy, grad_edge, grad_other, back_one = both_layers(slab)
        grad_center, grad_other_pos = back_one((latent_grad[lists[0]], grad_edge))
        carry = carry.at[:, lists[0]].add(grad_center)
        carry = carry.at[:, lists[1].reshape(-1)].add(grad_other_pos.reshape(3, -1))
        return (carry, None)
    motion, unused = lax.scan(force_step, jnp.zeros((3, total), jnp.float32), slabs)
    forces = -motion.reshape(3, NX, NY, NZ, SLOTS).transpose(1, 2, 3, 0, 4).reshape(NX, NY, NZ, 3 * SLOTS)
    atom_energy = energies.reshape(NX, NY, NZ, SLOTS)
    return (atom_energy, forces)
```

```python
import math

import jax
import jax.numpy as jnp
from jax import lax
from jax.experimental import pallas as pl
from jax.experimental.pallas import tpu as pltpu
from jax.sharding import PartitionSpec as P

MESH = pl.DeviceIdType.MESH
F32 = jnp.float32
BF16 = jnp.bfloat16
HIGH = lax.Precision.HIGHEST

NEIGH = 8
SLOTS = 64
CUTOFF = 4.0
SHARPNESS = 2.0
NBASIS = 8
CELLS_Z = 2
ATOMS = CELLS_Z * SLOTS
EDGES = ATOMS * NEIGH
WIDTH = 128
PLANE = 256
HALO = 9 * PLANE
GROUP = 16
GROUPS = ATOMS // GROUP
ROOT3 = math.sqrt(3.0)

PARTNERS = ((1, -1), (-1, 1), (1, 1), (-1, -1), (0, 1), (0, -1), (1, 0), (-1, 0))
PART = {0: 0, 1: 1, -1: 2}
ROWS = {0: (0, 128), 1: (128, 64), -1: (192, 64)}
OWN_ROWS = {0: (0, 128), 1: (0, 64), -1: (64, 64)}


def split_bf16(value):
    high = value.astype(BF16)
    return high, (value - high.astype(F32)).astype(BF16)


def dot(a, b, dims=((1,), (0,)), precision=None):
    return lax.dot_general(a, b, (dims, ((), ())), preferred_element_type=F32, precision=precision)


NT = ((1,), (1,))


def sigmoid(value):
    return 0.5 + 0.5 * jnp.tanh(0.5 * value)


def kernel(
    pos_ref,
    spec_ref,
    nbr_ref,
    center_ref,
    neighbor_ref,
    radial_ref,
    mix_ref,
    env_ref,
    update_ref,
    second_ref,
    readout_ref,
    energy_ref,
    force_ref,
    tiles,
    onehot,
    onehot_t,
    table,
    weights,
    act_d,
    mix_d,
    upd_d,
    env_buf,
    diag_a,
    diag_at,
    diag_v,
    latent_buf,
    edge_buf,
    grad_send,
    grad_recv,
    plane_send,
    plane_recv,
    force_tab,
    force_recv,
    force_plane,
    force_plane_recv,
    send_a,
    recv_a,
    send_b,
    recv_b,
    send_c,
    recv_c,
    send_d,
    recv_d,
    send_e,
    recv_e,
    send_f,
    recv_f,
):
    size_x, size_y, size_z = lax.axis_size("gx"), lax.axis_size("gy"), lax.axis_size("gz")
    my_x, my_y, my_z = lax.axis_index("gx"), lax.axis_index("gy"), lax.axis_index("gz")

    def device(dx, dy, dz):
        return (
            lax.rem(my_x + (dx + size_x), size_x),
            lax.rem(my_y + (dy + size_y), size_y),
            lax.rem(my_z + (dz + size_z), size_z),
        )

    def remote(src, dst, send, recv, target):
        return pltpu.make_async_remote_copy(
            src_ref=src, dst_ref=dst, send_sem=send, recv_sem=recv, device_id=target, device_id_type=MESH
        )

    barrier = pltpu.get_barrier_semaphore()
    for dy, dz in PARTNERS:
        pl.semaphore_signal(barrier, inc=1, device_id=device(0, dy, dz), device_id_type=MESH)
    for dx in (-1, 1):
        pl.semaphore_signal(barrier, inc=1, device_id=device(dx, 0, 0), device_id_type=MESH)

    coords = pos_ref[0, 0]
    kinds = spec_ref[0, 0].astype(F32)
    rows = [
        jnp.concatenate([coords[z : z + 1, SLOTS * c : SLOTS * (c + 1)] for z in range(CELLS_Z)], axis=1)
        for c in range(3)
    ]
    rows.append(jnp.concatenate([kinds[z : z + 1, :] for z in range(CELLS_Z)], axis=1))
    own_tile = jnp.concatenate(rows, axis=0)
    tiles[4, 0] = own_tile

    pl.semaphore_wait(barrier, len(PARTNERS) + 2)

    sends = []

    def spread(own_source, yz_dest, columns, sems):
        send_yz, recv_yz, send_x, recv_x = sems
        yz = {}
        for k, (dy, dz) in enumerate(PARTNERS):
            copy = remote(
                own_source(dz), yz_dest(dy, dz), send_yz.at[k], recv_yz.at[k], device(0, -dy, -dz)
            )
            copy.start()
            yz[dy, dz] = copy
        own = forward(columns, 1, "own", send_x, recv_x, 0)
        return yz, own

    def forward(columns, e, part, send_x, recv_x, k):
        copies = []
        for side, dx in enumerate((-1, 1)):
            copy = remote(
                columns(1, e, part),
                columns(dx + 1, e, part),
                send_x.at[2 * k + side],
                recv_x.at[2 * k + side],
                device(-dx, 0, 0),
            )
            copy.start()
            copies.append(copy)
        return copies

    def relay(yz, own, columns, sems):
        send_x, recv_x = sems[2:]
        moved = list(own)
        yz[0, 1].wait_recv()
        yz[0, -1].wait_recv()
        moved += forward(columns, 1, "ends", send_x, recv_x, 1)
        for k, dy in ((2, 1), (3, -1)):
            for dz in (0, 1, -1):
                yz[dy, dz].wait_recv()
            moved += forward(columns, dy + 1, "all", send_x, recv_x, k)
        sends.extend(yz.values())
        sends.extend(moved)
        return moved

    def tile_columns(a, e, part):
        column = tiles.at[3 * a + e]
        return {"own": column.at[0], "ends": column.at[pl.ds(1, 2)], "all": column}[part]

    sems = (send_a, recv_a, send_b.at[0], recv_b.at[0])
    yz, own = spread(
        lambda dz: tiles.at[4, 0], lambda dy, dz: tiles.at[3 + dy + 1, PART[dz]], tile_columns, sems
    )

    codes = nbr_ref[0, 0]
    offset_code = lax.shift_right_logical(codes, 6)
    slot = jnp.bitwise_and(codes, SLOTS - 1)
    column_code = lax.shift_right_logical(offset_code * 171, 9)
    row_z = offset_code - 3 * column_code
    own_z = lax.broadcasted_iota(jnp.int32, codes.shape, 0)
    place = jnp.bitwise_and(row_z + own_z + 3, 3)
    target2 = (column_code * 4 + place) * SLOTS + slot
    step_a = lax.shift_right_logical(column_code * 171, 9)
    step_e = column_code - 3 * step_a

    def flat(value):
        return jnp.concatenate([value[z : z + 1, :] for z in range(CELLS_Z)], axis=1)

    target = flat(target2)
    offsets = [flat(step - 1).astype(F32) for step in (step_a, step_e, row_z)]

    def build_t(t, carry):
        first = pl.multiple_of(t * 128, 128)
        row = lax.broadcasted_iota(jnp.int32, (128, EDGES), 0) + first
        onehot_t[pl.ds(first, 128), :] = (row == target).astype(F32).astype(BF16)
        return carry

    lax.fori_loop(0, HALO // 128, build_t, 0)

    moved_a = relay(yz, own, tile_columns, sems)

    target_rows = jnp.concatenate([target[:, 128 * j : 128 * (j + 1)] for j in range(8)], axis=0)
    target_cols = jnp.transpose(
        jnp.concatenate([target_rows.astype(F32), jnp.zeros((120, 128), F32)], axis=0)
    )
    lane = lax.broadcasted_iota(jnp.int32, (128, 128), 1).astype(F32)
    for j in range(8):
        column = jnp.broadcast_to(target_cols[:, j : j + 1], (128, 128))
        for t in range(HALO // 128):
            onehot[128 * j : 128 * (j + 1), 128 * t : 128 * (t + 1)] = (
                (column == lane + float(128 * t)).astype(F32).astype(BF16)
            )

    weights[...] = jnp.zeros_like(weights)
    weights[0:NBASIS, :] = radial_ref[...].astype(F32)
    spec_count = center_ref.shape[0]
    weights[8 : 8 + spec_count, :] = center_ref[...].astype(F32)
    weights[16 : 16 + spec_count, :] = neighbor_ref[...].astype(F32)
    before_w = weights[...].astype(BF16)

    for copy in moved_a:
        copy.wait_recv()

    half_lane = lax.broadcasted_iota(jnp.int32, (4, 128), 1) < SLOTS
    halves = []
    for p in range(9):
        halves.append(tiles[p, 0])
        halves.append(jnp.where(half_lane, tiles[p, 1], tiles[p, 2]))
    packed = [jnp.concatenate([halves[t], halves[t + 9]], axis=0) for t in range(9)]
    own8 = jnp.concatenate([own_tile, own_tile], axis=0)
    lane8 = lax.broadcasted_iota(jnp.int32, (8, 128), 1)
    others, centers = [], []
    for j in range(8):
        goal = target[:, 128 * j : 128 * (j + 1)]
        spot = jnp.broadcast_to(jnp.bitwise_and(goal, 127), (8, 128))
        which = lax.shift_right_logical(goal, 7)
        late = which >= 9
        which = jnp.broadcast_to(jnp.where(late, which - 9, which), (8, 128))
        found = jnp.zeros((8, 128), F32)
        for t in range(9):
            picked = jnp.take_along_axis(packed[t], spot, axis=1)
            found = jnp.where(which == t, picked, found)
        others.append(jnp.where(jnp.broadcast_to(late, (4, 128)), found[4:8], found[0:4]))
        mine = jnp.take_along_axis(own8, lax.shift_right_logical(lane8, 3) + GROUP * j, axis=1)
        centers.append(mine[0:4])
    other = jnp.concatenate(others, axis=1)
    center = jnp.concatenate(centers, axis=1)

    d_x, d_y, d_z = (offsets[c] + (other[c : c + 1] - center[c : c + 1]) for c in range(3))
    distance = jnp.sqrt(d_x * d_x + d_y * d_y + d_z * d_z)
    inverse = 1.0 / distance
    u_x, u_y, u_z = d_x * inverse, d_y * inverse, d_z * inverse
    angular = [
        jnp.ones_like(u_x),
        u_x,
        u_y,
        u_z,
        ROOT3 * u_x * u_y,
        ROOT3 * u_y * u_z,
        0.5 * (3.0 * u_z * u_z - 1.0),
        ROOT3 * u_x * u_z,
        0.5 * ROOT3 * (u_x * u_x - u_y * u_y),
    ]
    ratio = distance * (1.0 / CUTOFF)
    inside = 1.0 - ratio * ratio
    index8 = lax.broadcasted_iota(jnp.int32, (8, EDGES), 0)
    mu = (index8.astype(F32) + 0.5) * (CUTOFF / NBASIS)
    apart = distance - mu
    bell = jnp.exp(-SHARPNESS * apart * apart)
    basis = bell * (inside * inside)
    basis_d = bell * (-2.0 * SHARPNESS * apart * (inside * inside) - ratio * inside)
    hot_center = (index8.astype(F32) == center[3:4]).astype(F32)
    hot_other = (index8.astype(F32) == other[3:4]).astype(F32)
    features = jnp.concatenate([basis, hot_center, hot_other], axis=0)
    features = jnp.transpose(features).astype(BF16)

    before = dot(features, before_w)
    gate = sigmoid(before)
    act = before * gate
    act_d[...] = gate + act * (1.0 - gate)
    mixed = dot(act.astype(BF16), mix_ref[...])
    gate = sigmoid(mixed)
    latent = mixed * gate
    mix_d[...] = gate + latent * (1.0 - gate)
    latent_buf[...] = latent
    env_buf[...] = dot(latent.astype(BF16), env_ref[...]).astype(BF16)

    group_mask = (
        lax.shift_right_logical(lax.broadcasted_iota(jnp.int32, (GROUP, 128), 1), 3)
        == lax.broadcasted_iota(jnp.int32, (GROUP, 128), 0)
    ).astype(F32)
    zero = {n: jnp.zeros((GROUP * n, WIDTH), BF16) for n in (1, 3, 5)}
    update_w = update_ref[...]
    for j in range(GROUPS):
        span = slice(128 * j, 128 * (j + 1))
        spread_y = jnp.concatenate([angular[m][:, span] * group_mask for m in range(9)], axis=0)
        diag_a[j] = spread_y.astype(BF16)
        diag_at[j] = jnp.transpose(spread_y).astype(BF16)
        value = (dot(diag_a[j], env_buf[span, :]) * (1.0 / NEIGH)).astype(BF16)
        diag_v[j] = jnp.concatenate(
            [
                jnp.concatenate([value[0:16], zero[1], zero[1]], axis=1),
                jnp.concatenate([zero[3], value[16:64], zero[3]], axis=1),
                jnp.concatenate([zero[5], zero[5], value[64:144]], axis=1),
            ],
            axis=0,
        )
        invariant = dot(diag_at[j], diag_v[j]).astype(BF16)
        summed = latent_buf[span, :] + dot(invariant, update_w)
        gate = sigmoid(summed)
        edge = summed * gate
        upd_d[span, :] = gate + edge * (1.0 - gate)
        edge_buf[span, :] = edge

    members = (
        lax.shift_right_logical(lax.broadcasted_iota(jnp.int32, (ATOMS, EDGES), 1), 3)
        == lax.broadcasted_iota(jnp.int32, (ATOMS, EDGES), 0)
    ).astype(F32).astype(BF16)
    high, low = split_bf16(edge_buf[...])
    table[4, 0:ATOMS, :] = ((dot(members, high) + dot(members, low)) * (1.0 / NEIGH)).astype(BF16)

    def table_columns(a, e, part):
        column = table.at[3 * a + e]
        return {"own": column.at[pl.ds(0, 128)], "ends": column.at[pl.ds(128, 128)], "all": column}[part]

    sems = (send_c, recv_c, send_b.at[1], recv_b.at[1])
    yz, own = spread(
        lambda dz: table.at[4, pl.ds(*OWN_ROWS[dz])],
        lambda dy, dz: table.at[3 + dy + 1, pl.ds(*ROWS[dz])],
        table_columns,
        sems,
    )
    moved_c = relay(yz, own, table_columns, sems)
    middle = jnp.concatenate([table[3], table[4], table[5]], axis=0)
    other_latent = dot(onehot[:, 768:1536], middle)
    for copy in moved_c:
        copy.wait_recv()
    before_plane = jnp.concatenate([table[0], table[1], table[2]], axis=0)
    after_plane = jnp.concatenate([table[6], table[7], table[8]], axis=0)
    other_latent = other_latent + dot(onehot[:, 0:768], before_plane) + dot(onehot[:, 1536:2304], after_plane)

    edge = edge_buf[...]
    product = (edge * other_latent).astype(BF16)
    second_w = second_ref[...]
    readout = readout_ref[...]
    hidden_in = dot(product, second_w)
    gate = sigmoid(hidden_in)
    hidden = hidden_in * gate
    hidden_g = (readout * (gate + hidden * (1.0 - gate))).astype(BF16)
    product_g = dot(hidden_g, second_w, NT).astype(BF16).astype(F32)
    other_g = (product_g * edge).astype(BF16)
    edge_buf[...] = product_g * other_latent

    moved_x = {}
    for side, dx in enumerate((-1, 1)):
        for e in (0, 2, 1):
            first = 256 * (3 * (dx + 1) + e)
            grad_send[side, e] = dot(onehot_t[first : first + 256, :], other_g).astype(BF16)
            copy = remote(
                grad_send.at[side, e],
                grad_recv.at[side, e],
                send_d.at[3 * side + e],
                recv_d.at[3 * side + e],
                device(dx, 0, 0),
            )
            copy.start()
            moved_x[side, e] = copy
    plane_sum = {e: dot(onehot_t[768 + 256 * e : 1024 + 256 * e, :], other_g) for e in range(3)}

    high, low = split_bf16(hidden * readout)
    atom_terms = dot(members, high) + dot(members, low)
    energy = dot(jnp.ones((8, WIDTH), F32), atom_terms, NT, HIGH)
    energy_ref[0, 0] = jnp.concatenate(
        [energy[0:1, SLOTS * z : SLOTS * (z + 1)] for z in range(CELLS_Z)], axis=0
    )

    moved_yz = {}
    for e in (0, 2, 1):
        moved_x[0, e].wait_recv()
        moved_x[1, e].wait_recv()
        plane_sum[e] = plane_sum[e] + grad_recv[0, e].astype(F32) + grad_recv[1, e].astype(F32)
        plane_send[e] = plane_sum[e].astype(BF16)
        for k, (dy, dz) in enumerate(PARTNERS):
            if dy == e - 1:
                rows_send = pl.ds(*ROWS[dz])
                copy = remote(
                    plane_send.at[e, rows_send],
                    plane_recv.at[k, pl.ds(0, ROWS[dz][1])],
                    send_c.at[8 + k],
                    recv_c.at[8 + k],
                    device(0, dy, dz),
                )
                copy.start()
                moved_yz[k] = copy
    for copy in moved_yz.values():
        copy.wait_recv()
    sends.extend(moved_x.values())
    sends.extend(moved_yz.values())
    parts = {0: plane_sum[1][0:128]}
    for k, (dy, dz) in enumerate(PARTNERS):
        got = plane_recv[k, 0 : ROWS[dz][1], :].astype(F32)
        parts[dz] = got if dz not in parts else parts[dz] + got
    owned = parts[0] + jnp.concatenate([parts[1], parts[-1]], axis=0)

    owned_edges = jnp.broadcast_to((owned * (1.0 / NEIGH))[:, None, :], (ATOMS, NEIGH, WIDTH)).reshape(EDGES, WIDTH)
    summed_g = (edge_buf[...] + owned_edges) * upd_d[...]
    edge_buf[...] = summed_g
    invariant_g = dot(summed_g.astype(BF16), update_w, NT).astype(BF16)
    angular_g = [[] for _ in range(9)]
    for j in range(GROUPS):
        span = slice(128 * j, 128 * (j + 1))
        inv_g = invariant_g[span, :]
        wide = dot(diag_a[j], inv_g)
        value_g = (
            jnp.concatenate([wide[0:16, 0:128], wide[16:64, 128:256], wide[64:144, 256:384]], axis=0)
            * (1.0 / NEIGH)
        ).astype(BF16)
        act_env = env_buf[span, :]
        all_g = dot(diag_v[j], inv_g, NT) + dot(value_g, act_env, NT)
        for m in range(9):
            angular_g[m].append(
                jnp.sum(all_g[GROUP * m : GROUP * (m + 1)] * group_mask, axis=0, keepdims=True)
            )
        latent_buf[span, :] = dot(diag_at[j], value_g)
    latent_g = dot(latent_buf[...].astype(BF16), env_ref[...], NT).astype(BF16).astype(F32)
    mixed_g = ((edge_buf[...] + latent_g) * mix_d[...]).astype(BF16)
    act_g = dot(mixed_g, mix_ref[...], NT).astype(BF16).astype(F32)
    before_g = (act_g * act_d[...]).astype(BF16)
    basis_g = dot(radial_ref[...], before_g, NT).astype(BF16).astype(F32)

    distance_g = jnp.sum(basis_g * basis_d, axis=0, keepdims=True)
    g = [jnp.concatenate(parts_m, axis=1) for parts_m in angular_g]
    gu_x = g[1] + ROOT3 * (u_y * g[4] + u_z * g[7] + u_x * g[8])
    gu_y = g[2] + ROOT3 * (u_x * g[4] + u_z * g[5] - u_y * g[8])
    gu_z = g[3] + ROOT3 * (u_y * g[5] + u_x * g[7]) + 3.0 * u_z * g[6]
    along = distance_g - inverse * (u_x * gu_x + u_y * gu_y + u_z * gu_z)
    pull = [-(gu * inverse + u * along) for gu, u in ((gu_x, u_x), (gu_y, u_y), (gu_z, u_z))]
    pull4 = jnp.concatenate(pull + [jnp.zeros_like(u_x)], axis=0)
    high = pull4.astype(BF16).astype(F32)
    pull8 = jnp.concatenate([high, pull4 - high], axis=0).astype(BF16)

    def scatter(first, count):
        both = dot(pull8, onehot_t[first : first + count, :], NT)
        return both[0:4] + both[4:8]

    moved_f = []
    for side, dx in enumerate((-1, 1)):
        a = dx + 1
        got = scatter(768 * a, 768)
        for i in range(6):
            force_tab[side, i] = got[:, 128 * i : 128 * (i + 1)]
        copy = remote(
            force_tab.at[side], force_recv.at[side], send_e.at[side], recv_e.at[side], device(dx, 0, 0)
        )
        copy.start()
        moved_f.append(copy)
    middle_f = scatter(768, 768)
    both = dot(pull8, members, NT)
    own_f = both[0:4] + both[4:8]
    for copy in moved_f:
        copy.wait_recv()
    for i in range(6):
        force_plane[i] = middle_f[:, 128 * i : 128 * (i + 1)] + force_recv[0, i] + force_recv[1, i]
    moved_g = []
    for k, (dy, dz) in enumerate(PARTNERS):
        copy = remote(
            force_plane.at[2 * (dy + 1) + (1 if dz else 0)],
            force_plane_recv.at[k],
            send_f.at[k],
            recv_f.at[k],
            device(0, dy, dz),
        )
        copy.start()
        moved_g.append(copy)
    for copy in moved_g:
        copy.wait_recv()
    sends.extend(moved_f)
    sends.extend(moved_g)
    total = force_plane[2] - own_f
    ends = {}
    for k, (dy, dz) in enumerate(PARTNERS):
        got = force_plane_recv[k]
        if dz == 0:
            total = total + got
        else:
            ends[dz] = got if dz not in ends else ends[dz] + got
    total = total + jnp.where(half_lane, ends[1], ends[-1])
    force_ref[0, 0] = jnp.concatenate(
        [
            jnp.concatenate([total[c : c + 1, SLOTS * z : SLOTS * (z + 1)] for c in range(3)], axis=1)
            for z in range(CELLS_Z)
        ],
        axis=0,
    )
    for copy in sends:
        copy.wait_send()


def on_device(
    positions,
    species,
    neighbors,
    center_table,
    neighbor_table,
    radial_weight,
    mix_weight,
    env_weight,
    update_weight,
    second_weight,
    readout,
):
    dma = pltpu.SemaphoreType.DMA
    vmem = pltpu.VMEM
    cells = positions.shape[:3]
    return pl.pallas_call(
        kernel,
        out_shape=(
            jax.ShapeDtypeStruct((*cells, SLOTS), F32),
            jax.ShapeDtypeStruct((*cells, 3 * SLOTS), F32),
        ),
        in_specs=[pl.BlockSpec(memory_space=pltpu.VMEM)] * 11,
        out_specs=[pl.BlockSpec(memory_space=pltpu.VMEM)] * 2,
        scratch_shapes=[
            vmem((9, 3, 4, 128), F32),
            vmem((EDGES, HALO), BF16),
            vmem((HALO, EDGES), BF16),
            vmem((9, PLANE, WIDTH), BF16),
            vmem((24, WIDTH), F32),
            vmem((EDGES, WIDTH), F32),
            vmem((EDGES, WIDTH), F32),
            vmem((EDGES, WIDTH), F32),
            vmem((EDGES, WIDTH), BF16),
            vmem((GROUPS, 9 * GROUP, 128), BF16),
            vmem((GROUPS, 128, 9 * GROUP), BF16),
            vmem((GROUPS, 9 * GROUP, 3 * WIDTH), BF16),
            vmem((EDGES, WIDTH), F32),
            vmem((EDGES, WIDTH), F32),
            vmem((2, 3, PLANE, WIDTH), BF16),
            vmem((2, 3, PLANE, WIDTH), BF16),
            vmem((3, PLANE, WIDTH), BF16),
            vmem((8, 128, WIDTH), BF16),
            vmem((2, 6, 4, 128), F32),
            vmem((2, 6, 4, 128), F32),
            vmem((6, 4, 128), F32),
            vmem((8, 4, 128), F32),
            dma((8,)),
            dma((8,)),
            dma((2, 8)),
            dma((2, 8)),
            dma((16,)),
            dma((16,)),
            dma((6,)),
            dma((6,)),
            dma((2,)),
            dma((2,)),
            dma((8,)),
            dma((8,)),
        ],
        compiler_params=pltpu.CompilerParams(collective_id=0, has_side_effects=True),
    )(
        positions,
        species,
        neighbors,
        center_table,
        neighbor_table,
        radial_weight,
        mix_weight,
        env_weight,
        update_weight,
        second_weight,
        readout.reshape(1, WIDTH),
    )


def solution(mesh):
    placed = (
        P("gx", "gy", "gz", None),
        P("gx", "gy", "gz", None),
        P("gx", "gy", "gz", None),
        P(),
        P(),
        P(),
        P(),
        P(),
        P(),
        P(),
        P(),
    )
    return jax.shard_map(
        on_device,
        mesh=mesh,
        in_specs=placed,
        out_specs=(P("gx", "gy", "gz", None), P("gx", "gy", "gz", None)),
        check_vma=False,
    )
```

```python
import itertools
import math

import jax
import jax.numpy as jnp
from jax import lax
from jax.experimental import pallas as pl
from jax.experimental.pallas import tpu as pltpu
from jax.sharding import PartitionSpec as P

MESH = pl.DeviceIdType.MESH
F32 = jnp.float32
BF16 = jnp.bfloat16
HIGH = lax.Precision.HIGHEST

NEIGH = 8
SLOTS = 64
CUTOFF = 4.0
SHARPNESS = 2.0
NBASIS = 8
CELLS_Z = 2
ATOMS = CELLS_Z * SLOTS
EDGES = ATOMS * NEIGH
WIDTH = 128
PLANE = 256
LEVEL = 3 * PLANE
GROUP = 16
GROUPS = ATOMS // GROUP
ROOT3 = math.sqrt(3.0)

PARTNERS = ((1, -1), (-1, 1), (1, 1), (-1, -1), (0, 1), (0, -1), (1, 0), (-1, 0))
AROUND = sorted(
    (d for d in itertools.product((-1, 0, 1), repeat=3) if any(d)), key=lambda d: -sum(abs(c) for c in d)
)
PART = {0: 0, 1: 1, -1: 2}
ROWS = {0: (0, 128), 1: (128, 64), -1: (192, 64)}
OWN_ROWS = {0: (0, 128), 1: (0, 64), -1: (64, 64)}


def split_bf16(value):
    high = value.astype(BF16)
    return high, (value - high.astype(F32)).astype(BF16)


def dot(a, b, dims=((1,), (0,)), precision=None):
    return lax.dot_general(a, b, (dims, ((), ())), preferred_element_type=F32, precision=precision)


NT = ((1,), (1,))


def sigmoid(value):
    return 0.5 + 0.5 * jnp.tanh(0.5 * value)


def kernel(
    pos_in,
    spec_in,
    nbr_in,
    center_in,
    neighbor_in,
    radial_in,
    mix_in,
    env_in,
    update_in,
    second_in,
    readout_in,
    out_ref,
    pos_ref,
    spec_ref,
    nbr_ref,
    center_ref,
    neighbor_ref,
    radial_ref,
    mix_ref,
    env_ref,
    update_ref,
    second_ref,
    readout_ref,
    load_sem,
    tiles,
    onehot,
    onehot_t,
    target_col,
    level_col,
    table,
    weights,
    act_d,
    mix_d,
    upd_d,
    env_buf,
    diag_a,
    diag_at,
    value_0,
    value_1,
    value_2,
    mixed_0,
    mixed_1,
    mixed_2,
    summed_b,
    latent_buf,
    edge_buf,
    grad_send,
    grad_recv,
    plane_send,
    plane_recv,
    force_tab,
    force_recv,
    send_a,
    recv_a,
    send_c,
    recv_c,
    send_x,
    recv_x,
    send_d,
    recv_d,
    send_f,
    recv_f,
):
    size_x, size_y, size_z = lax.axis_size("gx"), lax.axis_size("gy"), lax.axis_size("gz")
    my_x, my_y, my_z = lax.axis_index("gx"), lax.axis_index("gy"), lax.axis_index("gz")

    def device(dx, dy, dz):
        return (
            lax.rem(my_x + (dx + size_x), size_x),
            lax.rem(my_y + (dy + size_y), size_y),
            lax.rem(my_z + (dz + size_z), size_z),
        )

    def remote(src, dst, send, recv, target):
        return pltpu.make_async_remote_copy(
            src_ref=src, dst_ref=dst, send_sem=send, recv_sem=recv, device_id=target, device_id_type=MESH
        )

    barrier = pltpu.get_barrier_semaphore()
    for step in AROUND:
        pl.semaphore_signal(barrier, inc=1, device_id=device(*step), device_id_type=MESH)

    sources = (
        pos_in, spec_in, nbr_in, center_in, neighbor_in, radial_in, mix_in, env_in, update_in, second_in, readout_in
    )
    places = (
        pos_ref, spec_ref, nbr_ref, center_ref, neighbor_ref, radial_ref, mix_ref, env_ref, update_ref, second_ref,
        readout_ref,
    )
    loads = [pltpu.make_async_copy(src, dst, load_sem.at[k]) for k, (src, dst) in enumerate(zip(sources, places))]
    for load in loads:
        load.start()
    loads[0].wait()
    loads[1].wait()

    coords = pos_ref[0, 0]
    kinds = spec_ref[0, 0].astype(F32)
    rows = [
        jnp.concatenate([coords[z : z + 1, SLOTS * c : SLOTS * (c + 1)] for z in range(CELLS_Z)], axis=1)
        for c in range(3)
    ]
    rows.append(jnp.concatenate([kinds[z : z + 1, :] for z in range(CELLS_Z)], axis=1))
    own_tile = jnp.concatenate(rows, axis=0)
    tiles[4, 0] = own_tile

    pl.semaphore_wait(barrier, len(AROUND))

    sends = []

    far_side = lax.rem(my_x, 2)
    sides = (far_side, 1 - far_side)

    def forward(source, dest, send, recv, k):
        copies = []
        for side in sides[::-1]:
            copy = remote(
                source,
                dest(3 * (2 * side)),
                send.at[2 * k + side],
                recv.at[2 * k + side],
                device(1 - 2 * side, 0, 0),
            )
            copy.start()
            copies.append(copy)
        sends.extend(copies)
        return copies

    moved_a = []
    for k, (dx, dy, dz) in enumerate(AROUND):
        copy = remote(
            tiles.at[4, 0], tiles.at[3 * dx + dy + 4, PART[dz]], send_a.at[k], recv_a.at[k], device(-dx, -dy, -dz)
        )
        copy.start()
        moved_a.append(copy)
    sends.extend(moved_a)

    loads[2].wait()
    codes = nbr_ref[0, 0]
    offset_code = lax.shift_right_logical(codes, 6)
    slot = jnp.bitwise_and(codes, SLOTS - 1)
    column_code = lax.shift_right_logical(offset_code * 171, 9)
    row_z = offset_code - 3 * column_code
    own_z = lax.broadcasted_iota(jnp.int32, codes.shape, 0)
    place = jnp.bitwise_and(row_z + own_z + 3, 3)
    step_a = lax.shift_right_logical(column_code * 171, 9)
    step_e = column_code - 3 * step_a

    def flat(value):
        return jnp.concatenate([value[z : z + 1, :] for z in range(CELLS_Z)], axis=1)

    target = flat((step_e * 4 + place) * SLOTS + slot)
    level = flat(step_a)
    offsets = [flat(step - 1).astype(F32) for step in (step_a, step_e, row_z)]

    for load in loads[3:]:
        load.wait()
    weights[...] = jnp.zeros_like(weights)
    weights[0:NBASIS, :] = radial_ref[...].astype(F32)
    spec_count = center_ref.shape[0]
    weights[8 : 8 + spec_count, :] = center_ref[...].astype(F32)
    weights[16 : 16 + spec_count, :] = neighbor_ref[...].astype(F32)
    before_w = weights[...].astype(BF16)

    for copy in moved_a:
        copy.wait_recv()

    half_lane = lax.broadcasted_iota(jnp.int32, (4, 128), 1) < SLOTS
    halves = []
    for p in range(9):
        halves.append(tiles[p, 0])
        halves.append(jnp.where(half_lane, tiles[p, 1], tiles[p, 2]))
    packed = [jnp.concatenate([halves[t], halves[t + 9]], axis=0) for t in range(9)]
    own8 = jnp.concatenate([own_tile, own_tile], axis=0)
    lane8 = lax.broadcasted_iota(jnp.int32, (8, 128), 1)
    others, centers = [], []
    for j in range(8):
        goal = (target + LEVEL * level)[:, 128 * j : 128 * (j + 1)]
        spot = jnp.broadcast_to(jnp.bitwise_and(goal, 127), (8, 128))
        which = lax.shift_right_logical(goal, 7)
        late = which >= 9
        which = jnp.broadcast_to(jnp.where(late, which - 9, which), (8, 128))
        found = jnp.zeros((8, 128), F32)
        for t in range(9):
            picked = jnp.take_along_axis(packed[t], spot, axis=1)
            found = jnp.where(which == t, picked, found)
        others.append(jnp.where(jnp.broadcast_to(late, (4, 128)), found[4:8], found[0:4]))
        mine = jnp.take_along_axis(own8, lax.shift_right_logical(lane8, 3) + GROUP * j, axis=1)
        centers.append(mine[0:4])
    other = jnp.concatenate(others, axis=1)
    center = jnp.concatenate(centers, axis=1)

    d_x, d_y, d_z = (offsets[c] + (other[c : c + 1] - center[c : c + 1]) for c in range(3))
    distance = jnp.sqrt(d_x * d_x + d_y * d_y + d_z * d_z)
    inverse = 1.0 / distance
    u_x, u_y, u_z = d_x * inverse, d_y * inverse, d_z * inverse
    angular = [
        jnp.ones_like(u_x),
        u_x,
        u_y,
        u_z,
        ROOT3 * u_x * u_y,
        ROOT3 * u_y * u_z,
        0.5 * (3.0 * u_z * u_z - 1.0),
        ROOT3 * u_x * u_z,
        0.5 * ROOT3 * (u_x * u_x - u_y * u_y),
    ]
    ratio = distance * (1.0 / CUTOFF)
    inside = 1.0 - ratio * ratio
    index8 = lax.broadcasted_iota(jnp.int32, (8, EDGES), 0)
    mu = (index8.astype(F32) + 0.5) * (CUTOFF / NBASIS)
    apart = distance - mu
    bell = jnp.exp(-SHARPNESS * apart * apart)
    basis = bell * (inside * inside)
    basis_d = bell * (-2.0 * SHARPNESS * apart * (inside * inside) - ratio * inside)
    hot_center = (index8.astype(F32) == center[3:4]).astype(F32)
    hot_other = (index8.astype(F32) == other[3:4]).astype(F32)
    features = jnp.concatenate([basis, hot_center, hot_other], axis=0)
    features = jnp.transpose(features).astype(BF16)

    group_mask = (
        lax.shift_right_logical(lax.broadcasted_iota(jnp.int32, (GROUP, 128), 1), 3)
        == lax.broadcasted_iota(jnp.int32, (GROUP, 128), 0)
    ).astype(F32)
    members = (
        lax.shift_right_logical(lax.broadcasted_iota(jnp.int32, (ATOMS, EDGES), 1), 3)
        == lax.broadcasted_iota(jnp.int32, (ATOMS, EDGES), 0)
    ).astype(F32).astype(BF16)
    levels = ((0, 1), (1, 4), (4, 9))
    update_w = [update_ref[WIDTH * l : WIDTH * (l + 1), :] for l in range(3)]

    def gathered(buffers, j):
        return jnp.concatenate(
            [
                buffer[GROUP * (stop - start) * j : GROUP * (stop - start) * (j + 1), :]
                for buffer, (start, stop) in zip(buffers, levels)
            ],
            axis=0,
        )

    def placed(buffers, j, value):
        for buffer, (start, stop) in zip(buffers, levels):
            rows_l = GROUP * (stop - start)
            buffer[rows_l * j : rows_l * (j + 1), :] = value[GROUP * start : GROUP * stop]

    values = (value_0, value_1, value_2)
    mixes = (mixed_0, mixed_1, mixed_2)
    half_edges = EDGES // CELLS_Z
    half_groups = GROUPS // CELLS_Z
    yz = {}
    moved_c = []
    for z in range(CELLS_Z):
        block = slice(half_edges * z, half_edges * (z + 1))
        before = dot(features[block, :], before_w)
        gate = sigmoid(before)
        act = before * gate
        act_d[block, :] = gate + act * (1.0 - gate)
        mixed = dot(act.astype(BF16), mix_ref[...])
        gate = sigmoid(mixed)
        latent = mixed * gate
        mix_d[block, :] = gate + latent * (1.0 - gate)
        env_buf[block, :] = dot(latent.astype(BF16), env_ref[...]).astype(BF16)
        for j in range(half_groups * z, half_groups * (z + 1)):
            span = slice(128 * j, 128 * (j + 1))
            spread_y = jnp.concatenate([angular[m][:, span] * group_mask for m in range(9)], axis=0)
            diag_a[j] = spread_y.astype(BF16)
            diag_at[j] = jnp.transpose(spread_y).astype(BF16)
            placed(values, j, (dot(diag_a[j], env_buf[span, :]) * (1.0 / NEIGH)).astype(BF16))
        for value, mixed_l, weight, (start, stop) in zip(values, mixes, update_w, levels):
            rows_l = GROUP * (stop - start) * half_groups
            span = slice(rows_l * z, rows_l * (z + 1))
            mixed_l[span, :] = dot(value[span, :], weight).astype(BF16)
        update = jnp.concatenate(
            [dot(diag_at[j], gathered(mixes, j)) for j in range(half_groups * z, half_groups * (z + 1))], axis=0
        )
        summed = latent + update
        gate = sigmoid(summed)
        edge = summed * gate
        upd_d[block, :] = gate + edge * (1.0 - gate)
        edge_buf[block, :] = edge
        high, low = split_bf16(edge)
        mine = members[0:SLOTS, 0:half_edges]
        own_rows = pl.ds(SLOTS * z, SLOTS)
        table[4, SLOTS * z : SLOTS * (z + 1), :] = ((dot(mine, high) + dot(mine, low)) * (1.0 / NEIGH)).astype(BF16)
        for k, (dy, dz) in enumerate(PARTNERS):
            if dz == (-1 if z == 0 else 1):
                continue
            rows_there = own_rows if dz == 0 else pl.ds(*ROWS[dz])
            copy = remote(
                table.at[4, own_rows],
                table.at[4 + dy, rows_there],
                send_c.at[k + 8 * z],
                recv_c.at[k + 8 * z],
                device(0, -dy, -dz),
            )
            copy.start()
            yz[dy, dz, z] = copy
        moved_c.append(
            forward(
                table.at[4, own_rows], lambda a, own_rows=own_rows: table.at[a + 1, own_rows], send_x, recv_x, z
            )
        )
    sends.extend(yz.values())

    row_kinds = [target[:, 128 * j : 128 * (j + 1)].astype(F32) for j in range(8)]
    row_kinds += [level[:, 128 * j : 128 * (j + 1)].astype(F32) for j in range(8)]
    columns = jnp.transpose(jnp.concatenate(row_kinds + [jnp.zeros((112, 128), F32)], axis=0))
    for j in range(8):
        target_col[j] = jnp.broadcast_to(columns[:, j : j + 1], (128, 128))
        level_col[128 * j : 128 * (j + 1), :] = jnp.broadcast_to(columns[:, 8 + j : 9 + j], (128, 128))

    def build(j, carry):
        first = pl.multiple_of(j * 128, 128)
        lane = lax.broadcasted_iota(jnp.int32, (128, 128), 1).astype(F32)
        column = target_col[j]
        for t in range(LEVEL // 128):
            onehot[pl.ds(first, 128), 128 * t : 128 * (t + 1)] = (
                (column == lane + float(128 * t)).astype(F32).astype(BF16)
            )
        return carry

    lax.fori_loop(0, GROUPS, build, 0)

    def build_t(t, carry):
        first = pl.multiple_of(t * 128, 128)
        row = lax.broadcasted_iota(jnp.int32, (128, EDGES), 0) + first
        onehot_t[pl.ds(first, 128), :] = (row == target).astype(F32).astype(BF16)
        return carry

    lax.fori_loop(0, LEVEL // 128, build_t, 0)

    ends = pl.ds(128, 128)
    pair = pl.ds(0, 128)
    yz[0, 1, 0].wait_recv()
    yz[0, -1, 1].wait_recv()
    moved_c.append(forward(table.at[4, ends], lambda a: table.at[a + 1, ends], send_x, recv_x, 2))
    for k, dy in ((3, 1), (5, -1)):
        yz[dy, 0, 0].wait_recv()
        yz[dy, 0, 1].wait_recv()
        moved_c.append(forward(table.at[4 + dy, pair], lambda a, dy=dy: table.at[a + 1 + dy, pair], send_x, recv_x, k))
        yz[dy, 1, 0].wait_recv()
        yz[dy, -1, 1].wait_recv()
        moved_c.append(
            forward(table.at[4 + dy, ends], lambda a, dy=dy: table.at[a + 1 + dy, ends], send_x, recv_x, k + 1)
        )
    here = dot(onehot[...], jnp.concatenate([table[3], table[4], table[5]], axis=0))
    beside = jnp.zeros((EDGES, 2 * WIDTH), F32)
    for e, chunks in ((1, (0, 1, 2)), (2, (3, 4)), (0, (5, 6))):
        for c in chunks:
            for copy in moved_c[c]:
                copy.wait_recv()
        pair_e = jnp.concatenate([table[e], table[6 + e]], axis=1)
        beside = beside + dot(onehot[:, PLANE * e : PLANE * (e + 1)], pair_e)
    levels_e = level_col[...]
    other_latent = jnp.where(
        levels_e == 1.0, here, jnp.where(levels_e == 0.0, beside[:, 0:WIDTH], beside[:, WIDTH : 2 * WIDTH])
    )

    edge = edge_buf[...]
    product = (edge * other_latent).astype(BF16)
    second_w = second_ref[...]
    readout = readout_ref[...]
    hidden_in = dot(product, second_w)
    gate = sigmoid(hidden_in)
    hidden = hidden_in * gate
    hidden_g = (readout * (gate + hidden * (1.0 - gate))).astype(BF16)
    product_g = dot(hidden_g, second_w, NT).astype(BF16).astype(F32)
    other_g = product_g * edge
    none = jnp.zeros_like(other_g)
    beside_g = jnp.concatenate(
        [jnp.where(levels_e == 0.0, other_g, none), jnp.where(levels_e == 2.0, other_g, none)], axis=1
    ).astype(BF16)
    here_g = jnp.where(levels_e == 1.0, other_g, none).astype(BF16)
    edge_buf[...] = product_g * other_latent

    moved_x = {}
    for e in (0, 2, 1):
        grads = dot(onehot_t[PLANE * e : PLANE * (e + 1), :], beside_g).astype(BF16)
        grad_send[0, e] = grads[:, 0:WIDTH]
        grad_send[1, e] = grads[:, WIDTH : 2 * WIDTH]
        for order, side in enumerate(sides):
            copy = remote(
                grad_send.at[side, e],
                grad_recv.at[side, e],
                send_d.at[3 * side + e],
                recv_d.at[3 * side + e],
                device(2 * side - 1, 0, 0),
            )
            copy.start()
            moved_x[order, e] = copy
    middle_grad = dot(onehot_t[...], here_g)
    plane_sum = {e: middle_grad[PLANE * e : PLANE * (e + 1)] for e in range(3)}

    high, low = split_bf16(hidden * readout)
    atom_terms = dot(members, high) + dot(members, low)
    energy = dot(jnp.ones((8, WIDTH), F32), atom_terms, NT, HIGH)

    moved_yz = {}
    for e in (0, 2, 1):
        moved_x[0, e].wait_recv()
        moved_x[1, e].wait_recv()
        plane_sum[e] = plane_sum[e] + grad_recv[0, e].astype(F32) + grad_recv[1, e].astype(F32)
        plane_send[e] = plane_sum[e].astype(BF16)
        for k, (dy, dz) in enumerate(PARTNERS):
            if dy == e - 1:
                rows_send = pl.ds(*ROWS[dz])
                copy = remote(
                    plane_send.at[e, rows_send],
                    plane_recv.at[k, pl.ds(0, ROWS[dz][1])],
                    send_c.at[16 + k],
                    recv_c.at[16 + k],
                    device(0, dy, dz),
                )
                copy.start()
                moved_yz[k] = copy
    for copy in moved_yz.values():
        copy.wait_recv()
    sends.extend(moved_x.values())
    sends.extend(moved_yz.values())
    parts = {0: plane_sum[1][0:128]}
    for k, (dy, dz) in enumerate(PARTNERS):
        got = plane_recv[k, 0 : ROWS[dz][1], :].astype(F32)
        parts[dz] = got if dz not in parts else parts[dz] + got
    owned = parts[0] + jnp.concatenate([parts[1], parts[-1]], axis=0)

    owned_edges = jnp.broadcast_to((owned * (1.0 / NEIGH))[:, None, :], (ATOMS, NEIGH, WIDTH)).reshape(EDGES, WIDTH)
    summed_g = (edge_buf[...] + owned_edges) * upd_d[...]
    edge_buf[...] = summed_g
    summed_b[...] = summed_g.astype(BF16)
    for j in range(GROUPS):
        span = slice(128 * j, 128 * (j + 1))
        placed(values, j, dot(diag_a[j], summed_b[span, :]).astype(BF16))
    for value, weight in zip(values, update_w):
        value[...] = (dot(value[...], weight, NT) * (1.0 / NEIGH)).astype(BF16)
    angular_g = [[] for _ in range(9)]
    for j in range(GROUPS):
        span = slice(128 * j, 128 * (j + 1))
        value_g = gathered(values, j)
        latent_buf[span, :] = dot(diag_at[j], value_g)
        all_g = dot(
            jnp.concatenate([gathered(mixes, j), value_g], axis=1),
            jnp.concatenate([summed_b[span, :], env_buf[span, :]], axis=1),
            NT,
        )
        for m in range(1, 9):
            angular_g[m].append(
                jnp.sum(all_g[GROUP * m : GROUP * (m + 1)] * group_mask, axis=0, keepdims=True)
            )
    latent_g = dot(latent_buf[...].astype(BF16), env_ref[...], NT).astype(BF16).astype(F32)
    mixed_g = ((edge_buf[...] + latent_g) * mix_d[...]).astype(BF16)
    act_g = dot(mixed_g, mix_ref[...], NT).astype(BF16).astype(F32)
    before_g = (act_g * act_d[...]).astype(BF16)
    basis_g = dot(radial_ref[...], before_g, NT).astype(BF16).astype(F32)

    distance_g = jnp.sum(basis_g * basis_d, axis=0, keepdims=True)
    g = [jnp.concatenate(parts_m, axis=1) if parts_m else None for parts_m in angular_g]
    gu_x = g[1] + ROOT3 * (u_y * g[4] + u_z * g[7] + u_x * g[8])
    gu_y = g[2] + ROOT3 * (u_x * g[4] + u_z * g[5] - u_y * g[8])
    gu_z = g[3] + ROOT3 * (u_y * g[5] + u_x * g[7]) + 3.0 * u_z * g[6]
    along = distance_g - inverse * (u_x * gu_x + u_y * gu_y + u_z * gu_z)
    pull = [-(gu * inverse + u * along) for gu, u in ((gu_x, u_x), (gu_y, u_y), (gu_z, u_z))]
    pull4 = jnp.concatenate(pull + [jnp.zeros_like(u_x)], axis=0)
    high = pull4.astype(BF16).astype(F32)
    pull8 = jnp.concatenate([high, pull4 - high], axis=0)

    pulls = jnp.concatenate([jnp.where(level == a, pull8, 0.0) for a in range(3)], axis=0).astype(BF16)
    spread_f = dot(pulls, onehot_t[...], NT)
    for a in range(3):
        level_f = spread_f[8 * a : 8 * a + 4] + spread_f[8 * a + 4 : 8 * a + 8]
        for i in range(6):
            force_tab[3 * a + i // 2, i % 2] = level_f[:, 128 * i : 128 * (i + 1)]
    moved_f = []
    for k, (dx, dy, dz) in enumerate(AROUND):
        copy = remote(
            force_tab.at[3 * dx + dy + 4, 1 if dz else 0],
            force_recv.at[k],
            send_f.at[k],
            recv_f.at[k],
            device(dx, dy, dz),
        )
        copy.start()
        moved_f.append(copy)
    both = dot(pull8.astype(BF16), members, NT)
    own_f = both[0:4] + both[4:8]
    for copy in moved_f:
        copy.wait_recv()
    sends.extend(moved_f)
    total = force_tab[4, 0] - own_f
    ends = {}
    for k, (dx, dy, dz) in enumerate(AROUND):
        got = force_recv[k]
        if dz == 0:
            total = total + got
        else:
            ends[dz] = got if dz not in ends else ends[dz] + got
    total = total + jnp.where(half_lane, ends[1], ends[-1])
    shown = [energy[0:1]] + [total[c : c + 1] for c in range(3)]
    out_ref[0, 0] = jnp.concatenate(
        [
            jnp.concatenate([row[:, SLOTS * z : SLOTS * (z + 1)] for row in shown], axis=1)
            for z in range(CELLS_Z)
        ],
        axis=0,
    )
    for copy in sends:
        copy.wait_send()


def on_device(
    positions,
    species,
    neighbors,
    center_table,
    neighbor_table,
    radial_weight,
    mix_weight,
    env_weight,
    update_weight,
    second_weight,
    readout,
):
    dma = pltpu.SemaphoreType.DMA
    vmem = pltpu.VMEM
    cells = positions.shape[:3]
    args = (
        positions,
        species,
        neighbors,
        center_table,
        neighbor_table,
        radial_weight,
        mix_weight,
        env_weight,
        update_weight,
        second_weight,
        readout.reshape(1, WIDTH),
    )
    both = pl.pallas_call(
        kernel,
        out_shape=jax.ShapeDtypeStruct((*cells, 4 * SLOTS), F32),
        in_specs=[pl.BlockSpec(memory_space=pl.ANY)] * len(args),
        out_specs=pl.BlockSpec(memory_space=pltpu.VMEM),
        scratch_shapes=[
            *(vmem(arg.shape, arg.dtype) for arg in args),
            dma((len(args),)),
            vmem((9, 3, 4, 128), F32),
            vmem((EDGES, LEVEL), BF16),
            vmem((LEVEL, EDGES), BF16),
            vmem((GROUPS, 128, 128), F32),
            vmem((EDGES, 128), F32),
            vmem((9, PLANE, WIDTH), BF16),
            vmem((24, WIDTH), F32),
            vmem((EDGES, WIDTH), F32),
            vmem((EDGES, WIDTH), F32),
            vmem((EDGES, WIDTH), F32),
            vmem((EDGES, WIDTH), BF16),
            vmem((GROUPS, 9 * GROUP, 128), BF16),
            vmem((GROUPS, 128, 9 * GROUP), BF16),
            vmem((1 * ATOMS, WIDTH), BF16),
            vmem((3 * ATOMS, WIDTH), BF16),
            vmem((5 * ATOMS, WIDTH), BF16),
            vmem((1 * ATOMS, WIDTH), BF16),
            vmem((3 * ATOMS, WIDTH), BF16),
            vmem((5 * ATOMS, WIDTH), BF16),
            vmem((EDGES, WIDTH), BF16),
            vmem((EDGES, WIDTH), F32),
            vmem((EDGES, WIDTH), F32),
            vmem((2, 3, PLANE, WIDTH), BF16),
            vmem((2, 3, PLANE, WIDTH), BF16),
            vmem((3, PLANE, WIDTH), BF16),
            vmem((8, 128, WIDTH), BF16),
            vmem((9, 2, 4, 128), F32),
            vmem((26, 4, 128), F32),
            dma((26,)),
            dma((26,)),
            dma((24,)),
            dma((24,)),
            dma((14,)),
            dma((14,)),
            dma((6,)),
            dma((6,)),
            dma((26,)),
            dma((26,)),
        ],
        compiler_params=pltpu.CompilerParams(collective_id=0, has_side_effects=True),
    )(*args)
    return both[..., :SLOTS], both[..., SLOTS:]


def solution(mesh):
    placed = (
        P("gx", "gy", "gz", None),
        P("gx", "gy", "gz", None),
        P("gx", "gy", "gz", None),
        P(),
        P(),
        P(),
        P(),
        P(),
        P(),
        P(),
        P(),
    )
    return jax.shard_map(
        on_device,
        mesh=mesh,
        in_specs=placed,
        out_specs=(P("gx", "gy", "gz", None), P("gx", "gy", "gz", None)),
        check_vma=False,
    )
```

```python
import itertools
import math

import jax
import jax.numpy as jnp
from jax import lax
from jax.experimental import pallas as pl
from jax.experimental.pallas import tpu as pltpu
from jax.sharding import PartitionSpec as P

MESH = pl.DeviceIdType.MESH
F32 = jnp.float32
BF16 = jnp.bfloat16
HIGH = lax.Precision.HIGHEST

NEIGH = 8
SLOTS = 64
CUTOFF = 4.0
SHARPNESS = 2.0
NBASIS = 8
CELLS_Z = 2
ATOMS = CELLS_Z * SLOTS
EDGES = ATOMS * NEIGH
WIDTH = 128
PLANE = 256
LEVEL = 3 * PLANE
GROUP = 16
GROUPS = ATOMS // GROUP
ROOT3 = math.sqrt(3.0)
GRAD_CHUNKS = {0: ((0, PLANE),), 1: ((128, 128), (0, 128)), 2: ((0, PLANE),)}

PARTNERS = ((1, -1), (-1, 1), (1, 1), (-1, -1), (0, 1), (0, -1), (1, 0), (-1, 0))
AROUND = sorted(
    (d for d in itertools.product((-1, 0, 1), repeat=3) if any(d)), key=lambda d: -sum(abs(c) for c in d)
)
ROWS = {0: (0, 128), 1: (128, 64), -1: (192, 64)}
SLOTS_YZ = tuple((64 * k, 64) if dz else (384 + 128 * (k - 6), 128) for k, (dy, dz) in enumerate(PARTNERS))


def split_bf16(value):
    high = value.astype(BF16)
    return high, (value - high.astype(F32)).astype(BF16)


def dot(a, b, dims=((1,), (0,)), precision=None):
    return lax.dot_general(a, b, (dims, ((), ())), preferred_element_type=F32, precision=precision)


NT = ((1,), (1,))


def sigmoid(value):
    return 0.5 + 0.5 * jnp.tanh(0.5 * value)


def kernel(
    pos_in,
    spec_in,
    nbr_in,
    center_in,
    neighbor_in,
    radial_in,
    mix_in,
    env_in,
    update_in,
    second_in,
    readout_in,
    out_ref,
    pos_ref,
    spec_ref,
    nbr_ref,
    center_ref,
    neighbor_ref,
    radial_ref,
    mix_ref,
    env_ref,
    update_ref,
    second_ref,
    readout_ref,
    load_sem,
    tiles,
    onehot,
    onehot_t,
    target_col,
    level_col,
    table,
    weights,
    act_d,
    mix_d,
    upd_d,
    env_buf,
    diag_a,
    diag_at,
    value_0,
    value_1,
    value_2,
    mixed_0,
    mixed_1,
    mixed_2,
    summed_b,
    latent_buf,
    edge_buf,
    grad_send,
    grad_recv,
    plane_send,
    plane_recv,
    force_tab,
    force_recv,
    send_a,
    recv_a,
    send_c,
    recv_c,
    recv_x,
    recv_d,
):
    size_x, size_y, size_z = lax.axis_size("gx"), lax.axis_size("gy"), lax.axis_size("gz")
    my_x, my_y, my_z = lax.axis_index("gx"), lax.axis_index("gy"), lax.axis_index("gz")

    near = []
    for index, size in ((my_x, size_x), (my_y, size_y), (my_z, size_z)):
        near.append(
            (index, jnp.where(index == size - 1, 0, index + 1), jnp.where(index == 0, size - 1, index - 1))
        )

    def device(dx, dy, dz):
        return near[0][dx], near[1][dy], near[2][dz]

    def settle(ref, sem):
        pltpu.make_async_copy(ref, ref, sem).wait()

    def remote(src, dst, send, recv, target):
        return pltpu.make_async_remote_copy(
            src_ref=src, dst_ref=dst, send_sem=send, recv_sem=recv, device_id=target, device_id_type=MESH
        )

    barrier = pltpu.get_barrier_semaphore()
    for step in AROUND:
        pl.semaphore_signal(barrier, inc=1, device_id=device(*step), device_id_type=MESH)

    sources = (
        pos_in, spec_in, nbr_in, center_in, neighbor_in, radial_in, mix_in, env_in, update_in, second_in, readout_in
    )
    places = (
        pos_ref, spec_ref, nbr_ref, center_ref, neighbor_ref, radial_ref, mix_ref, env_ref, update_ref, second_ref,
        readout_ref,
    )
    loads = [pltpu.make_async_copy(src, dst, load_sem.at[k]) for k, (src, dst) in enumerate(zip(sources, places))]
    for load in loads:
        load.start()
    loads[0].wait()
    loads[1].wait()

    coords = pos_ref[0, 0]
    kinds = spec_ref[0, 0].astype(F32)
    rows = [
        jnp.concatenate([coords[z : z + 1, SLOTS * c : SLOTS * (c + 1)] for z in range(CELLS_Z)], axis=1)
        for c in range(3)
    ]
    rows.append(jnp.concatenate([kinds[z : z + 1, :] for z in range(CELLS_Z)], axis=1))
    own_tile = jnp.concatenate(rows, axis=0)
    tiles[13] = own_tile

    pl.semaphore_wait(barrier, len(AROUND))

    far_side = lax.rem(my_x, 2)
    sides = (far_side, 1 - far_side)

    def x_device(side):
        return jnp.where(side == 0, near[0][-1], near[0][1]), my_y, my_z

    def forward(source, dest, send, recv, k):
        copies = []
        for side in sides[::-1]:
            copy = remote(
                source,
                dest(3 * (2 * side)),
                send.at[1],
                recv.at[2 * k + side],
                x_device(1 - side),
            )
            copy.start()
            copies.append(copy)
        return copies

    def tile_of(dx, dy, dz):
        return 9 * (dx + 1) + 3 * (dy + 1) + (dz + 1)

    for dx, dy, dz in AROUND:
        copy = remote(
            tiles.at[13], tiles.at[tile_of(dx, dy, dz)], send_a.at[0], recv_a.at[0], device(-dx, -dy, -dz)
        )
        copy.start()

    loads[2].wait()
    codes = nbr_ref[0, 0]
    offset_code = lax.shift_right_logical(codes, 6)
    slot = jnp.bitwise_and(codes, SLOTS - 1)
    column_code = lax.shift_right_logical(offset_code * 171, 9)
    row_z = offset_code - 3 * column_code
    own_z = lax.broadcasted_iota(jnp.int32, codes.shape, 0)
    place = jnp.bitwise_and(row_z + own_z + 3, 3)
    step_a = lax.shift_right_logical(column_code * 171, 9)
    step_e = column_code - 3 * step_a

    def flat(value):
        return jnp.concatenate([value[z : z + 1, :] for z in range(CELLS_Z)], axis=1)

    target = flat((step_e * 4 + place) * SLOTS + slot)
    level = flat(step_a)
    offsets = [flat(step - 1).astype(F32) for step in (step_a, step_e, row_z)]

    for load in loads[3:]:
        load.wait()
    weights[...] = jnp.zeros_like(weights)
    weights[0:NBASIS, :] = radial_ref[...].astype(F32)
    spec_count = center_ref.shape[0]
    weights[8 : 8 + spec_count, :] = center_ref[...].astype(F32)
    weights[16 : 16 + spec_count, :] = neighbor_ref[...].astype(F32)
    before_w = weights[...].astype(BF16)

    settle(tiles.at[pl.ds(0, len(AROUND))], recv_a.at[0])
    settle(tiles.at[pl.ds(0, len(AROUND))], send_a.at[0])

    half_lane = lax.broadcasted_iota(jnp.int32, (4, 128), 1) < SLOTS
    halves = []
    for p in range(9):
        halves.append(tiles[3 * p + 1])
        halves.append(jnp.where(half_lane, tiles[3 * p + 2], tiles[3 * p]))
    packed = [jnp.concatenate([halves[t], halves[t + 9]], axis=0) for t in range(9)]
    own8 = jnp.concatenate([own_tile, own_tile], axis=0)
    lane8 = lax.broadcasted_iota(jnp.int32, (8, 128), 1)
    others, centers = [], []
    for j in range(8):
        goal = (target + LEVEL * level)[:, 128 * j : 128 * (j + 1)]
        spot = jnp.broadcast_to(jnp.bitwise_and(goal, 127), (8, 128))
        which = lax.shift_right_logical(goal, 7)
        late = which >= 9
        which = jnp.broadcast_to(jnp.where(late, which - 9, which), (8, 128))
        found = jnp.zeros((8, 128), F32)
        for t in range(9):
            picked = jnp.take_along_axis(packed[t], spot, axis=1)
            found = jnp.where(which == t, picked, found)
        others.append(jnp.where(jnp.broadcast_to(late, (4, 128)), found[4:8], found[0:4]))
        mine = jnp.take_along_axis(own8, lax.shift_right_logical(lane8, 3) + GROUP * j, axis=1)
        centers.append(mine[0:4])
    other = jnp.concatenate(others, axis=1)
    center = jnp.concatenate(centers, axis=1)

    d_x, d_y, d_z = (offsets[c] + (other[c : c + 1] - center[c : c + 1]) for c in range(3))
    distance = jnp.sqrt(d_x * d_x + d_y * d_y + d_z * d_z)
    inverse = 1.0 / distance
    u_x, u_y, u_z = d_x * inverse, d_y * inverse, d_z * inverse
    angular = [
        jnp.ones_like(u_x),
        u_x,
        u_y,
        u_z,
        ROOT3 * u_x * u_y,
        ROOT3 * u_y * u_z,
        0.5 * (3.0 * u_z * u_z - 1.0),
        ROOT3 * u_x * u_z,
        0.5 * ROOT3 * (u_x * u_x - u_y * u_y),
    ]
    ratio = distance * (1.0 / CUTOFF)
    inside = 1.0 - ratio * ratio
    index8 = lax.broadcasted_iota(jnp.int32, (8, EDGES), 0)
    mu = (index8.astype(F32) + 0.5) * (CUTOFF / NBASIS)
    apart = distance - mu
    bell = jnp.exp(-SHARPNESS * apart * apart)
    basis = bell * (inside * inside)
    basis_d = bell * (-2.0 * SHARPNESS * apart * (inside * inside) - ratio * inside)
    hot_center = (index8.astype(F32) == center[3:4]).astype(F32)
    hot_other = (index8.astype(F32) == other[3:4]).astype(F32)
    features = jnp.concatenate([basis, hot_center, hot_other], axis=0)
    features = jnp.transpose(features).astype(BF16)

    group_mask = (
        lax.shift_right_logical(lax.broadcasted_iota(jnp.int32, (GROUP, 128), 1), 3)
        == lax.broadcasted_iota(jnp.int32, (GROUP, 128), 0)
    ).astype(F32)
    members = (
        lax.shift_right_logical(lax.broadcasted_iota(jnp.int32, (ATOMS, EDGES), 1), 3)
        == lax.broadcasted_iota(jnp.int32, (ATOMS, EDGES), 0)
    ).astype(F32).astype(BF16)
    levels = ((0, 1), (1, 4), (4, 9))
    update_w = [update_ref[WIDTH * l : WIDTH * (l + 1), :] for l in range(3)]

    def gathered(buffers, j):
        return jnp.concatenate(
            [
                buffer[GROUP * (stop - start) * j : GROUP * (stop - start) * (j + 1), :]
                for buffer, (start, stop) in zip(buffers, levels)
            ],
            axis=0,
        )

    def placed(buffers, j, value):
        for buffer, (start, stop) in zip(buffers, levels):
            rows_l = GROUP * (stop - start)
            buffer[rows_l * j : rows_l * (j + 1), :] = value[GROUP * start : GROUP * stop]

    values = (value_0, value_1, value_2)
    mixes = (mixed_0, mixed_1, mixed_2)
    half_edges = EDGES // CELLS_Z
    half_groups = GROUPS // CELLS_Z
    yz = {}
    moved_c = []
    for z in range(CELLS_Z):
        block = slice(half_edges * z, half_edges * (z + 1))
        before = dot(features[block, :], before_w)
        gate = sigmoid(before)
        act = before * gate
        act_d[block, :] = gate + act * (1.0 - gate)
        mixed = dot(act.astype(BF16), mix_ref[...])
        gate = sigmoid(mixed)
        latent = mixed * gate
        mix_d[block, :] = gate + latent * (1.0 - gate)
        env_buf[block, :] = dot(latent.astype(BF16), env_ref[...]).astype(BF16)
        for j in range(half_groups * z, half_groups * (z + 1)):
            span = slice(128 * j, 128 * (j + 1))
            spread_y = jnp.concatenate([angular[m][:, span] * group_mask for m in range(9)], axis=0)
            diag_a[j] = spread_y.astype(BF16)
            diag_at[j] = jnp.transpose(diag_a[j])
            placed(values, j, (dot(diag_a[j], env_buf[span, :]) * (1.0 / NEIGH)).astype(BF16))
        for value, mixed_l, weight, (start, stop) in zip(values, mixes, update_w, levels):
            rows_l = GROUP * (stop - start) * half_groups
            span = slice(rows_l * z, rows_l * (z + 1))
            mixed_l[span, :] = dot(value[span, :], weight).astype(BF16)
        update = jnp.concatenate(
            [dot(diag_at[j], gathered(mixes, j)) for j in range(half_groups * z, half_groups * (z + 1))], axis=0
        )
        summed = latent + update
        gate = sigmoid(summed)
        edge = summed * gate
        upd_d[block, :] = gate + edge * (1.0 - gate)
        edge_buf[block, :] = edge
        high, low = split_bf16(edge)
        mine = members[0:SLOTS, 0:half_edges]
        own_rows = pl.ds(SLOTS * z, SLOTS)
        table[4, SLOTS * z : SLOTS * (z + 1), :] = ((dot(mine, high) + dot(mine, low)) * (1.0 / NEIGH)).astype(BF16)
        for k, (dy, dz) in enumerate(PARTNERS):
            if dz == (-1 if z == 0 else 1):
                continue
            rows_there = own_rows if dz == 0 else pl.ds(*ROWS[dz])
            copy = remote(
                table.at[4, own_rows],
                table.at[4 + dy, rows_there],
                send_c.at[0],
                recv_c.at[k + 8 * z],
                device(0, -dy, -dz),
            )
            copy.start()
            yz[dy, dz, z] = copy
        moved_c.append(
            forward(
                table.at[4, own_rows], lambda a, own_rows=own_rows: table.at[a + 1, own_rows], send_c, recv_x, z
            )
        )

    row_kinds = [target[:, 128 * j : 128 * (j + 1)].astype(F32) for j in range(8)]
    row_kinds += [level[:, 128 * j : 128 * (j + 1)].astype(F32) for j in range(8)]
    columns = jnp.transpose(jnp.concatenate(row_kinds + [jnp.zeros((112, 128), F32)], axis=0))
    for j in range(8):
        target_col[j] = jnp.broadcast_to(columns[:, j : j + 1], (128, 128))
        level_col[128 * j : 128 * (j + 1), :] = jnp.broadcast_to(columns[:, 8 + j : 9 + j], (128, 128))

    def build(j, carry):
        first = pl.multiple_of(j * 128, 128)
        lane = lax.broadcasted_iota(jnp.int32, (128, 128), 1).astype(F32)
        column = target_col[j]
        for t in range(LEVEL // 128):
            onehot[pl.ds(first, 128), 128 * t : 128 * (t + 1)] = (
                (column == lane + float(128 * t)).astype(F32).astype(BF16)
            )
        return carry

    lax.fori_loop(0, GROUPS, build, 0)

    def build_t(t, carry):
        first = pl.multiple_of(t * 128, 128)
        row = lax.broadcasted_iota(jnp.int32, (128, EDGES), 0) + first
        onehot_t[pl.ds(first, 128), :] = (row == target).astype(F32).astype(BF16)
        return carry

    lax.fori_loop(0, LEVEL // 128, build_t, 0)

    ends = pl.ds(128, 128)
    pair = pl.ds(0, 128)
    yz[0, 1, 0].wait_recv()
    yz[0, -1, 1].wait_recv()
    moved_c.append(forward(table.at[4, ends], lambda a: table.at[a + 1, ends], send_c, recv_x, 2))
    for k, dy in ((3, 1), (5, -1)):
        yz[dy, 0, 0].wait_recv()
        yz[dy, 0, 1].wait_recv()
        moved_c.append(forward(table.at[4 + dy, pair], lambda a, dy=dy: table.at[a + 1 + dy, pair], send_c, recv_x, k))
        yz[dy, 1, 0].wait_recv()
        yz[dy, -1, 1].wait_recv()
        moved_c.append(
            forward(table.at[4 + dy, ends], lambda a, dy=dy: table.at[a + 1 + dy, ends], send_c, recv_x, k + 1)
        )
    here = dot(onehot[...], jnp.concatenate([table[3], table[4], table[5]], axis=0))
    beside = jnp.zeros((EDGES, 2 * WIDTH), F32)
    for e, chunks in ((1, (0, 1, 2)), (2, (3, 4)), (0, (5, 6))):
        for c in chunks:
            for copy in moved_c[c]:
                copy.wait_recv()
        pair_e = jnp.concatenate([table[e], table[6 + e]], axis=1)
        beside = beside + dot(onehot[:, PLANE * e : PLANE * (e + 1)], pair_e)
    levels_e = level_col[...]
    other_latent = jnp.where(
        levels_e == 1.0, here, jnp.where(levels_e == 0.0, beside[:, 0:WIDTH], beside[:, WIDTH : 2 * WIDTH])
    )

    edge = edge_buf[...]
    product = (edge * other_latent).astype(BF16)
    second_w = second_ref[...]
    readout = readout_ref[...]
    hidden_in = dot(product, second_w)
    gate = sigmoid(hidden_in)
    hidden = hidden_in * gate
    hidden_g = (readout * (gate + hidden * (1.0 - gate))).astype(BF16)
    product_g = dot(hidden_g, second_w, NT).astype(BF16).astype(F32)
    other_g = product_g * edge
    none = jnp.zeros_like(other_g)
    beside_g = jnp.concatenate(
        [jnp.where(levels_e == 0.0, other_g, none), jnp.where(levels_e == 2.0, other_g, none)], axis=1
    ).astype(BF16)
    here_g = jnp.where(levels_e == 1.0, other_g, none).astype(BF16)
    edge_buf[...] = product_g * other_latent

    moved_x = {}
    for e in (0, 2, 1):
        grads = dot(onehot_t[PLANE * e : PLANE * (e + 1), :], beside_g).astype(BF16)
        grad_send[0, e] = grads[:, 0:WIDTH]
        grad_send[1, e] = grads[:, WIDTH : 2 * WIDTH]
        for c, (first, count) in enumerate(GRAD_CHUNKS[e]):
            chunk = pl.ds(first, count)
            for order, side in enumerate(sides):
                copy = remote(
                    grad_send.at[side, e, chunk],
                    grad_recv.at[side, e, chunk],
                    send_c.at[2],
                    recv_d.at[4 * side + e + 2 * c],
                    x_device(side),
                )
                copy.start()
                moved_x[order, e, c] = copy
    middle_grad = dot(onehot_t[...], here_g)
    plane_sum = {e: middle_grad[PLANE * e : PLANE * (e + 1)] for e in range(3)}

    high, low = split_bf16(hidden * readout)
    atom_terms = dot(members, high) + dot(members, low)
    energy = dot(jnp.ones((8, WIDTH), F32), atom_terms, NT, HIGH)

    for e in (0, 2, 1):
        moved_x[0, e, 0].wait_recv()
        moved_x[1, e, 0].wait_recv()
        if e == 1:
            arrived = slice(128, 256)
        else:
            arrived = slice(0, 256)
        plane_send[e, arrived, :] = (
            plane_sum[e][arrived] + grad_recv[0, e, arrived, :].astype(F32) + grad_recv[1, e, arrived, :].astype(F32)
        ).astype(BF16)
        for k, (dy, dz) in enumerate(PARTNERS):
            if dy == e - 1:
                copy = remote(
                    plane_send.at[e, pl.ds(*ROWS[dz])],
                    plane_recv.at[pl.ds(*SLOTS_YZ[k])],
                    send_c.at[3],
                    recv_c.at[16],
                    device(0, dy, dz),
                )
                copy.start()
    moved_x[0, 1, 1].wait_recv()
    moved_x[1, 1, 1].wait_recv()
    own_sum = plane_sum[1][0:128] + grad_recv[0, 1, 0:128, :].astype(F32) + grad_recv[1, 1, 0:128, :].astype(F32)
    settle(plane_recv, send_c.at[0])
    settle(table.at[pl.ds(0, 6)], send_c.at[1])
    settle(grad_send, send_c.at[2])
    settle(plane_recv, send_c.at[3])
    settle(plane_recv, recv_c.at[16])
    parts = {0: own_sum}
    for k, (dy, dz) in enumerate(PARTNERS):
        first, count = SLOTS_YZ[k]
        got = plane_recv[first : first + count, :].astype(F32)
        parts[dz] = got if dz not in parts else parts[dz] + got
    owned = parts[0] + jnp.concatenate([parts[1], parts[-1]], axis=0)

    owned_edges = jnp.broadcast_to((owned * (1.0 / NEIGH))[:, None, :], (ATOMS, NEIGH, WIDTH)).reshape(EDGES, WIDTH)
    summed_g = (edge_buf[...] + owned_edges) * upd_d[...]
    edge_buf[...] = summed_g
    summed_b[...] = summed_g.astype(BF16)
    for j in range(GROUPS):
        span = slice(128 * j, 128 * (j + 1))
        placed(values, j, dot(diag_a[j], summed_b[span, :]).astype(BF16))
    for value, weight in zip(values, update_w):
        value[...] = (dot(value[...], weight, NT) * (1.0 / NEIGH)).astype(BF16)
    angular_g = [[] for _ in range(9)]
    for j in range(GROUPS):
        span = slice(128 * j, 128 * (j + 1))
        value_g = gathered(values, j)
        latent_buf[span, :] = dot(diag_at[j], value_g)
        all_g = dot(
            jnp.concatenate([gathered(mixes, j), value_g], axis=1),
            jnp.concatenate([summed_b[span, :], env_buf[span, :]], axis=1),
            NT,
        )
        for m in range(1, 9):
            angular_g[m].append(
                jnp.sum(all_g[GROUP * m : GROUP * (m + 1)] * group_mask, axis=0, keepdims=True)
            )
    latent_g = dot(latent_buf[...].astype(BF16), env_ref[...], NT).astype(BF16).astype(F32)
    mixed_g = ((edge_buf[...] + latent_g) * mix_d[...]).astype(BF16)
    act_g = dot(mixed_g, mix_ref[...], NT).astype(BF16).astype(F32)
    before_g = (act_g * act_d[...]).astype(BF16)
    basis_g = dot(radial_ref[...], before_g, NT).astype(BF16).astype(F32)

    distance_g = jnp.sum(basis_g * basis_d, axis=0, keepdims=True)
    g = [jnp.concatenate(parts_m, axis=1) if parts_m else None for parts_m in angular_g]
    gu_x = g[1] + ROOT3 * (u_y * g[4] + u_z * g[7] + u_x * g[8])
    gu_y = g[2] + ROOT3 * (u_x * g[4] + u_z * g[5] - u_y * g[8])
    gu_z = g[3] + ROOT3 * (u_y * g[5] + u_x * g[7]) + 3.0 * u_z * g[6]
    along = distance_g - inverse * (u_x * gu_x + u_y * gu_y + u_z * gu_z)
    pull = [-(gu * inverse + u * along) for gu, u in ((gu_x, u_x), (gu_y, u_y), (gu_z, u_z))]
    pull4 = jnp.concatenate(pull + [jnp.zeros_like(u_x)], axis=0)
    high = pull4.astype(BF16).astype(F32)
    pull8 = jnp.concatenate([high, pull4 - high], axis=0)

    pulls = jnp.concatenate([jnp.where(level == a, pull8, 0.0) for a in range(3)], axis=0).astype(BF16)
    spread_f = dot(pulls, onehot_t[...], NT)
    for a in range(3):
        level_f = spread_f[8 * a : 8 * a + 4] + spread_f[8 * a + 4 : 8 * a + 8]
        for i in range(6):
            force_tab[3 * a + i // 2, i % 2] = level_f[:, 128 * i : 128 * (i + 1)]
    for k, (dx, dy, dz) in enumerate(AROUND):
        copy = remote(
            force_tab.at[3 * dx + dy + 4, 1 if dz else 0],
            force_recv.at[k],
            send_a.at[1],
            recv_a.at[1],
            device(dx, dy, dz),
        )
        copy.start()
    both = dot(pull8.astype(BF16), members, NT)
    own_f = both[0:4] + both[4:8]
    settle(force_recv, recv_a.at[1])
    total = force_tab[4, 0] - own_f
    ends = {}
    for k, (dx, dy, dz) in enumerate(AROUND):
        got = force_recv[k]
        if dz == 0:
            total = total + got
        else:
            ends[dz] = got if dz not in ends else ends[dz] + got
    total = total + jnp.where(half_lane, ends[1], ends[-1])
    shown = [energy[0:1]] + [total[c : c + 1] for c in range(3)]
    out_ref[0, 0] = jnp.concatenate(
        [
            jnp.concatenate([row[:, SLOTS * z : SLOTS * (z + 1)] for row in shown], axis=1)
            for z in range(CELLS_Z)
        ],
        axis=0,
    )
    settle(force_recv, send_a.at[1])


def on_device(
    positions,
    species,
    neighbors,
    center_table,
    neighbor_table,
    radial_weight,
    mix_weight,
    env_weight,
    update_weight,
    second_weight,
    readout,
):
    dma = pltpu.SemaphoreType.DMA
    vmem = pltpu.VMEM
    cells = positions.shape[:3]
    args = (
        positions,
        species,
        neighbors,
        center_table,
        neighbor_table,
        radial_weight,
        mix_weight,
        env_weight,
        update_weight,
        second_weight,
        readout.reshape(1, WIDTH),
    )
    both = pl.pallas_call(
        kernel,
        out_shape=jax.ShapeDtypeStruct((*cells, 4 * SLOTS), F32),
        in_specs=[pl.BlockSpec(memory_space=pl.ANY)] * len(args),
        out_specs=pl.BlockSpec(memory_space=pltpu.VMEM),
        scratch_shapes=[
            *(vmem(arg.shape, arg.dtype) for arg in args),
            dma((len(args),)),
            vmem((27, 4, 128), F32),
            vmem((EDGES, LEVEL), BF16),
            vmem((LEVEL, EDGES), BF16),
            vmem((GROUPS, 128, 128), F32),
            vmem((EDGES, 128), F32),
            vmem((9, PLANE, WIDTH), BF16),
            vmem((24, WIDTH), F32),
            vmem((EDGES, WIDTH), F32),
            vmem((EDGES, WIDTH), F32),
            vmem((EDGES, WIDTH), F32),
            vmem((EDGES, WIDTH), BF16),
            vmem((GROUPS, 9 * GROUP, 128), BF16),
            vmem((GROUPS, 128, 9 * GROUP), BF16),
            vmem((1 * ATOMS, WIDTH), BF16),
            vmem((3 * ATOMS, WIDTH), BF16),
            vmem((5 * ATOMS, WIDTH), BF16),
            vmem((1 * ATOMS, WIDTH), BF16),
            vmem((3 * ATOMS, WIDTH), BF16),
            vmem((5 * ATOMS, WIDTH), BF16),
            vmem((EDGES, WIDTH), BF16),
            vmem((EDGES, WIDTH), F32),
            vmem((EDGES, WIDTH), F32),
            vmem((2, 3, PLANE, WIDTH), BF16),
            vmem((2, 3, PLANE, WIDTH), BF16),
            vmem((3, PLANE, WIDTH), BF16),
            vmem((640, WIDTH), BF16),
            vmem((9, 2, 4, 128), F32),
            vmem((26, 4, 128), F32),
            dma((2,)),
            dma((2,)),
            dma((4,)),
            dma((17,)),
            dma((14,)),
            dma((8,)),
        ],
        compiler_params=pltpu.CompilerParams(collective_id=0, has_side_effects=True),
    )(*args)
    return both[..., :SLOTS], both[..., SLOTS:]


def solution(mesh):
    placed = (
        P("gx", "gy", "gz", None),
        P("gx", "gy", "gz", None),
        P("gx", "gy", "gz", None),
        P(),
        P(),
        P(),
        P(),
        P(),
        P(),
        P(),
        P(),
    )
    return jax.shard_map(
        on_device,
        mesh=mesh,
        in_specs=placed,
        out_specs=(P("gx", "gy", "gz", None), P("gx", "gy", "gz", None)),
        check_vma=False,
    )
```

```python
import itertools
import math

import jax
import jax.numpy as jnp
from jax import lax
from jax.experimental import pallas as pl
from jax.experimental.pallas import tpu as pltpu
from jax.sharding import PartitionSpec as P

MESH = pl.DeviceIdType.MESH
F32 = jnp.float32
BF16 = jnp.bfloat16
HIGH = lax.Precision.HIGHEST

NEIGH = 8
SLOTS = 64
CUTOFF = 4.0
SHARPNESS = 2.0
NBASIS = 8
CELLS_Z = 2
ATOMS = CELLS_Z * SLOTS
EDGES = ATOMS * NEIGH
WIDTH = 128
PLANE = 256
LEVEL = 3 * PLANE
GROUP = 16
GROUPS = ATOMS // GROUP
ROOT3 = math.sqrt(3.0)
GRAD_CHUNKS = {0: ((0, PLANE),), 1: ((128, 128), (0, 128)), 2: ((0, PLANE),)}

PARTNERS = ((1, -1), (-1, 1), (1, 1), (-1, -1), (0, 1), (0, -1), (1, 0), (-1, 0))
AROUND = sorted(
    (d for d in itertools.product((-1, 0, 1), repeat=3) if any(d)), key=lambda d: -sum(abs(c) for c in d)
)
ROWS = {0: (0, 128), 1: (128, 64), -1: (192, 64)}
SLOTS_YZ = tuple((64 * k, 64) if dz else (384 + 128 * (k - 6), 128) for k, (dy, dz) in enumerate(PARTNERS))


def split_bf16(value):
    high = value.astype(BF16)
    return high, (value - high.astype(F32)).astype(BF16)


def dot(a, b, dims=((1,), (0,)), precision=None):
    return lax.dot_general(a, b, (dims, ((), ())), preferred_element_type=F32, precision=precision)


NT = ((1,), (1,))


def sigmoid(value):
    return 0.5 + 0.5 * jnp.tanh(0.5 * value)


def kernel(
    pos_in,
    spec_in,
    nbr_in,
    center_in,
    neighbor_in,
    radial_in,
    mix_in,
    env_in,
    update_in,
    second_in,
    readout_in,
    energy_ref,
    force_ref,
    pos_ref,
    spec_ref,
    nbr_ref,
    center_ref,
    neighbor_ref,
    radial_ref,
    mix_ref,
    env_ref,
    update_ref,
    second_ref,
    readout_ref,
    load_sem,
    tiles,
    onehot,
    onehot_t,
    target_col,
    level_col,
    level_mask,
    table,
    weights,
    act_d,
    mix_d,
    upd_d,
    env_buf,
    diag_a,
    diag_at,
    value_0,
    value_1,
    value_2,
    mixed_0,
    mixed_1,
    mixed_2,
    summed_b,
    latent_buf,
    edge_buf,
    grad_send,
    grad_recv,
    plane_send,
    plane_recv,
    force_tab,
    force_recv,
    send_a,
    recv_a,
    send_c,
    recv_c,
    recv_x,
    recv_d,
):
    size_x, size_y, size_z = lax.axis_size("gx"), lax.axis_size("gy"), lax.axis_size("gz")
    my_x, my_y, my_z = lax.axis_index("gx"), lax.axis_index("gy"), lax.axis_index("gz")

    near = []
    for index, size in ((my_x, size_x), (my_y, size_y), (my_z, size_z)):
        near.append(
            (index, jnp.where(index == size - 1, 0, index + 1), jnp.where(index == 0, size - 1, index - 1))
        )

    def device(dx, dy, dz):
        return near[0][dx], near[1][dy], near[2][dz]

    def settle(ref, sem):
        pltpu.make_async_copy(ref, ref, sem).wait()

    def remote(src, dst, send, recv, target):
        return pltpu.make_async_remote_copy(
            src_ref=src, dst_ref=dst, send_sem=send, recv_sem=recv, device_id=target, device_id_type=MESH
        )

    barrier = pltpu.get_barrier_semaphore()
    for step in AROUND:
        pl.semaphore_signal(barrier, inc=1, device_id=device(*step), device_id_type=MESH)

    sources = (
        pos_in, spec_in, nbr_in, center_in, neighbor_in, radial_in, mix_in, env_in, update_in, second_in, readout_in
    )
    places = (
        pos_ref, spec_ref, nbr_ref, center_ref, neighbor_ref, radial_ref, mix_ref, env_ref, update_ref, second_ref,
        readout_ref,
    )
    loads = [pltpu.make_async_copy(src, dst, load_sem.at[k]) for k, (src, dst) in enumerate(zip(sources, places))]
    for load in loads:
        load.start()
    loads[0].wait()
    loads[1].wait()

    coords = pos_ref[0, 0]
    kinds = spec_ref[0, 0].astype(F32)
    rows = [
        jnp.concatenate([coords[z : z + 1, SLOTS * c : SLOTS * (c + 1)] for z in range(CELLS_Z)], axis=1)
        for c in range(3)
    ]
    rows.append(jnp.concatenate([kinds[z : z + 1, :] for z in range(CELLS_Z)], axis=1))
    own_tile = jnp.concatenate(rows, axis=0)
    tiles[13] = own_tile

    pl.semaphore_wait(barrier, len(AROUND))

    far_side = lax.rem(my_x, 2)
    sides = (far_side, 1 - far_side)

    def x_device(side):
        return jnp.where(side == 0, near[0][-1], near[0][1]), my_y, my_z

    def forward(source, dest, send, recv, k):
        copies = []
        for side in sides[::-1]:
            copy = remote(
                source,
                dest(3 * (2 * side)),
                send.at[1],
                recv.at[2 * k + side],
                x_device(1 - side),
            )
            copy.start()
            copies.append(copy)
        return copies

    def tile_of(dx, dy, dz):
        return 9 * (dx + 1) + 3 * (dy + 1) + (dz + 1)

    for dx, dy, dz in AROUND:
        copy = remote(
            tiles.at[13], tiles.at[tile_of(dx, dy, dz)], send_a.at[0], recv_a.at[0], device(-dx, -dy, -dz)
        )
        copy.start()

    loads[2].wait()
    codes = nbr_ref[0, 0]
    offset_code = lax.shift_right_logical(codes, 6)
    slot = jnp.bitwise_and(codes, SLOTS - 1)
    column_code = lax.shift_right_logical(offset_code * 171, 9)
    row_z = offset_code - 3 * column_code
    own_z = lax.broadcasted_iota(jnp.int32, codes.shape, 0)
    place = jnp.bitwise_and(row_z + own_z + 3, 3)
    step_a = lax.shift_right_logical(column_code * 171, 9)
    step_e = column_code - 3 * step_a

    def flat(value):
        return jnp.concatenate([value[z : z + 1, :] for z in range(CELLS_Z)], axis=1)

    target = flat((step_e * 4 + place) * SLOTS + slot)
    level = flat(step_a)
    offsets = [flat(step - 1).astype(F32) for step in (step_a, step_e, row_z)]

    row_kinds = [target[:, 128 * j : 128 * (j + 1)].astype(F32) for j in range(8)]
    row_kinds += [level[:, 128 * j : 128 * (j + 1)].astype(F32) for j in range(8)]
    columns = jnp.transpose(jnp.concatenate(row_kinds + [jnp.zeros((112, 128), F32)], axis=0))
    for j in range(8):
        target_col[j] = jnp.broadcast_to(columns[:, j : j + 1], (128, 128))
        level_col[128 * j : 128 * (j + 1), :] = jnp.broadcast_to(columns[:, 8 + j : 9 + j], (128, 128))

    def build(j, carry):
        first = pl.multiple_of(j * 128, 128)
        level_j = level_col[pl.ds(first, 128), :]
        for a in range(3):
            level_mask[a, pl.ds(first, 128), :] = (level_j == float(a)).astype(F32).astype(BF16)
        lane = lax.broadcasted_iota(jnp.int32, (128, 128), 1).astype(F32)
        column = target_col[j]
        for t in range(LEVEL // 128):
            onehot[pl.ds(first, 128), 128 * t : 128 * (t + 1)] = (
                (column == lane + float(128 * t)).astype(F32).astype(BF16)
            )
        return carry

    lax.fori_loop(0, GROUPS, build, 0)

    def build_t(t, carry):
        first = pl.multiple_of(t * 128, 128)
        row = lax.broadcasted_iota(jnp.int32, (128, EDGES), 0) + first
        onehot_t[pl.ds(first, 128), :] = (row == target).astype(F32).astype(BF16)
        return carry

    lax.fori_loop(0, LEVEL // 128, build_t, 0)

    for load in loads[3:]:
        load.wait()
    weights[...] = jnp.zeros_like(weights)
    weights[0:NBASIS, :] = radial_ref[...].astype(F32)
    spec_count = center_ref.shape[0]
    weights[8 : 8 + spec_count, :] = center_ref[...].astype(F32)
    weights[16 : 16 + spec_count, :] = neighbor_ref[...].astype(F32)
    before_w = weights[...].astype(BF16)

    settle(tiles.at[pl.ds(0, len(AROUND))], recv_a.at[0])
    settle(tiles.at[pl.ds(0, len(AROUND))], send_a.at[0])

    half_lane = lax.broadcasted_iota(jnp.int32, (4, 128), 1) < SLOTS
    halves = []
    for p in range(9):
        halves.append(tiles[3 * p + 1])
        halves.append(jnp.where(half_lane, tiles[3 * p + 2], tiles[3 * p]))
    packed = [jnp.concatenate([halves[t], halves[t + 9]], axis=0) for t in range(9)]
    own8 = jnp.concatenate([own_tile, own_tile], axis=0)
    lane8 = lax.broadcasted_iota(jnp.int32, (8, 128), 1)
    others, centers = [], []
    for j in range(8):
        goal = (target + LEVEL * level)[:, 128 * j : 128 * (j + 1)]
        spot = jnp.broadcast_to(jnp.bitwise_and(goal, 127), (8, 128))
        which = lax.shift_right_logical(goal, 7)
        late = which >= 9
        which = jnp.broadcast_to(jnp.where(late, which - 9, which), (8, 128))
        found = jnp.zeros((8, 128), F32)
        for t in range(9):
            picked = jnp.take_along_axis(packed[t], spot, axis=1)
            found = jnp.where(which == t, picked, found)
        others.append(jnp.where(jnp.broadcast_to(late, (4, 128)), found[4:8], found[0:4]))
        mine = jnp.take_along_axis(own8, lax.shift_right_logical(lane8, 3) + GROUP * j, axis=1)
        centers.append(mine[0:4])
    other = jnp.concatenate(others, axis=1)
    center = jnp.concatenate(centers, axis=1)

    d_x, d_y, d_z = (offsets[c] + (other[c : c + 1] - center[c : c + 1]) for c in range(3))
    distance = jnp.sqrt(d_x * d_x + d_y * d_y + d_z * d_z)
    inverse = 1.0 / distance
    u_x, u_y, u_z = d_x * inverse, d_y * inverse, d_z * inverse
    angular = [
        jnp.ones_like(u_x),
        u_x,
        u_y,
        u_z,
        ROOT3 * u_x * u_y,
        ROOT3 * u_y * u_z,
        0.5 * (3.0 * u_z * u_z - 1.0),
        ROOT3 * u_x * u_z,
        0.5 * ROOT3 * (u_x * u_x - u_y * u_y),
    ]
    ratio = distance * (1.0 / CUTOFF)
    inside = 1.0 - ratio * ratio
    index8 = lax.broadcasted_iota(jnp.int32, (8, EDGES), 0)
    mu = (index8.astype(F32) + 0.5) * (CUTOFF / NBASIS)
    apart = distance - mu
    bell = jnp.exp(-SHARPNESS * apart * apart)
    basis = bell * (inside * inside)
    basis_d = bell * (-2.0 * SHARPNESS * apart * (inside * inside) - ratio * inside)
    hot_center = (index8.astype(F32) == center[3:4]).astype(F32)
    hot_other = (index8.astype(F32) == other[3:4]).astype(F32)
    features = jnp.concatenate([basis, hot_center, hot_other], axis=0)
    features = jnp.transpose(features).astype(BF16)

    group_mask = (
        lax.shift_right_logical(lax.broadcasted_iota(jnp.int32, (GROUP, 128), 1), 3)
        == lax.broadcasted_iota(jnp.int32, (GROUP, 128), 0)
    ).astype(F32)
    members = (
        lax.shift_right_logical(lax.broadcasted_iota(jnp.int32, (ATOMS, EDGES), 1), 3)
        == lax.broadcasted_iota(jnp.int32, (ATOMS, EDGES), 0)
    ).astype(F32).astype(BF16)
    levels = ((0, 1), (1, 4), (4, 9))
    update_w = [update_ref[WIDTH * l : WIDTH * (l + 1), :] for l in range(3)]

    def gathered(buffers, j):
        return jnp.concatenate(
            [
                buffer[GROUP * (stop - start) * j : GROUP * (stop - start) * (j + 1), :]
                for buffer, (start, stop) in zip(buffers, levels)
            ],
            axis=0,
        )

    def placed(buffers, j, value):
        for buffer, (start, stop) in zip(buffers, levels):
            rows_l = GROUP * (stop - start)
            buffer[rows_l * j : rows_l * (j + 1), :] = value[GROUP * start : GROUP * stop]

    values = (value_0, value_1, value_2)
    mixes = (mixed_0, mixed_1, mixed_2)
    half_edges = EDGES // CELLS_Z
    half_groups = GROUPS // CELLS_Z
    yz = {}
    moved_c = []
    for z in range(CELLS_Z):
        block = slice(half_edges * z, half_edges * (z + 1))
        before = dot(features[block, :], before_w)
        gate = sigmoid(before)
        act = before * gate
        act_d[block, :] = gate + act * (1.0 - gate)
        mixed = dot(act.astype(BF16), mix_ref[...])
        gate = sigmoid(mixed)
        latent = mixed * gate
        mix_d[block, :] = gate + latent * (1.0 - gate)
        env_buf[block, :] = dot(latent.astype(BF16), env_ref[...]).astype(BF16)
        for j in range(half_groups * z, half_groups * (z + 1)):
            span = slice(128 * j, 128 * (j + 1))
            spread_y = jnp.concatenate([angular[m][:, span] * group_mask for m in range(9)], axis=0)
            diag_a[j] = spread_y.astype(BF16)
            diag_at[j] = jnp.transpose(diag_a[j])
            placed(values, j, (dot(diag_a[j], env_buf[span, :]) * (1.0 / NEIGH)).astype(BF16))
        for value, mixed_l, weight, (start, stop) in zip(values, mixes, update_w, levels):
            rows_l = GROUP * (stop - start) * half_groups
            span = slice(rows_l * z, rows_l * (z + 1))
            mixed_l[span, :] = dot(value[span, :], weight).astype(BF16)
        update = jnp.concatenate(
            [dot(diag_at[j], gathered(mixes, j)) for j in range(half_groups * z, half_groups * (z + 1))], axis=0
        )
        summed = latent + update
        gate = sigmoid(summed)
        edge = summed * gate
        upd_d[block, :] = gate + edge * (1.0 - gate)
        edge_buf[block, :] = edge
        high, low = split_bf16(edge)
        mine = members[0:SLOTS, 0:half_edges]
        own_rows = pl.ds(SLOTS * z, SLOTS)
        table[4, SLOTS * z : SLOTS * (z + 1), :] = ((dot(mine, high) + dot(mine, low)) * (1.0 / NEIGH)).astype(BF16)
        for k, (dy, dz) in enumerate(PARTNERS):
            if dz == (-1 if z == 0 else 1):
                continue
            rows_there = own_rows if dz == 0 else pl.ds(*ROWS[dz])
            copy = remote(
                table.at[4, own_rows],
                table.at[4 + dy, rows_there],
                send_c.at[0],
                recv_c.at[k + 8 * z],
                device(0, -dy, -dz),
            )
            copy.start()
            yz[dy, dz, z] = copy
        moved_c.append(
            forward(
                table.at[4, own_rows], lambda a, own_rows=own_rows: table.at[a + 1, own_rows], send_c, recv_x, z
            )
        )

    ends = pl.ds(128, 128)
    pair = pl.ds(0, 128)
    yz[0, 1, 0].wait_recv()
    yz[0, -1, 1].wait_recv()
    moved_c.append(forward(table.at[4, ends], lambda a: table.at[a + 1, ends], send_c, recv_x, 2))
    for k, dy in ((3, 1), (5, -1)):
        yz[dy, 0, 0].wait_recv()
        yz[dy, 0, 1].wait_recv()
        moved_c.append(forward(table.at[4 + dy, pair], lambda a, dy=dy: table.at[a + 1 + dy, pair], send_c, recv_x, k))
        yz[dy, 1, 0].wait_recv()
        yz[dy, -1, 1].wait_recv()
        moved_c.append(
            forward(table.at[4 + dy, ends], lambda a, dy=dy: table.at[a + 1 + dy, ends], send_c, recv_x, k + 1)
        )
    here = dot(onehot[...], jnp.concatenate([table[3], table[4], table[5]], axis=0))
    beside = jnp.zeros((EDGES, 2 * WIDTH), F32)
    for e, chunks in ((1, (0, 1, 2)), (2, (3, 4)), (0, (5, 6))):
        for c in chunks:
            for copy in moved_c[c]:
                copy.wait_recv()
        pair_e = jnp.concatenate([table[e], table[6 + e]], axis=1)
        beside = beside + dot(onehot[:, PLANE * e : PLANE * (e + 1)], pair_e)
    levels_e = level_col[...]
    other_latent = jnp.where(
        levels_e == 1.0, here, jnp.where(levels_e == 0.0, beside[:, 0:WIDTH], beside[:, WIDTH : 2 * WIDTH])
    )

    edge = edge_buf[...]
    product = (edge * other_latent).astype(BF16)
    second_w = second_ref[...]
    readout = readout_ref[...]
    hidden_in = dot(product, second_w)
    gate = sigmoid(hidden_in)
    hidden = hidden_in * gate
    hidden_g = (readout * (gate + hidden * (1.0 - gate))).astype(BF16)
    product_g = dot(hidden_g, second_w, NT).astype(BF16).astype(F32)
    other_g = (product_g * edge).astype(BF16)
    beside_g = jnp.concatenate([other_g * level_mask[0], other_g * level_mask[2]], axis=1)
    here_g = other_g * level_mask[1]
    edge_buf[...] = product_g * other_latent

    moved_x = {}
    for e in (0, 2, 1):
        grads = dot(onehot_t[PLANE * e : PLANE * (e + 1), :], beside_g).astype(BF16)
        grad_send[0, e] = grads[:, 0:WIDTH]
        grad_send[1, e] = grads[:, WIDTH : 2 * WIDTH]
        for c, (first, count) in enumerate(GRAD_CHUNKS[e]):
            chunk = pl.ds(first, count)
            for order, side in enumerate(sides):
                copy = remote(
                    grad_send.at[side, e, chunk],
                    grad_recv.at[side, e, chunk],
                    send_c.at[2],
                    recv_d.at[4 * side + e + 2 * c],
                    x_device(side),
                )
                copy.start()
                moved_x[order, e, c] = copy
    middle_grad = dot(onehot_t[...], here_g)
    plane_sum = {e: middle_grad[PLANE * e : PLANE * (e + 1)] for e in range(3)}

    high, low = split_bf16(hidden * readout)
    atom_terms = dot(members, high) + dot(members, low)
    energy = dot(jnp.ones((8, WIDTH), F32), atom_terms, NT, HIGH)

    for e in (0, 2, 1):
        moved_x[0, e, 0].wait_recv()
        moved_x[1, e, 0].wait_recv()
        if e == 1:
            arrived = slice(128, 256)
        else:
            arrived = slice(0, 256)
        plane_send[e, arrived, :] = (
            plane_sum[e][arrived] + grad_recv[0, e, arrived, :].astype(F32) + grad_recv[1, e, arrived, :].astype(F32)
        ).astype(BF16)
        for k, (dy, dz) in enumerate(PARTNERS):
            if dy == e - 1:
                copy = remote(
                    plane_send.at[e, pl.ds(*ROWS[dz])],
                    plane_recv.at[pl.ds(*SLOTS_YZ[k])],
                    send_c.at[3],
                    recv_c.at[16],
                    device(0, dy, dz),
                )
                copy.start()
    moved_x[0, 1, 1].wait_recv()
    moved_x[1, 1, 1].wait_recv()
    own_sum = plane_sum[1][0:128] + grad_recv[0, 1, 0:128, :].astype(F32) + grad_recv[1, 1, 0:128, :].astype(F32)
    settle(plane_recv, send_c.at[0])
    settle(table.at[pl.ds(0, 6)], send_c.at[1])
    settle(grad_send, send_c.at[2])
    settle(plane_recv, send_c.at[3])
    settle(plane_recv, recv_c.at[16])
    parts = {0: own_sum}
    for k, (dy, dz) in enumerate(PARTNERS):
        first, count = SLOTS_YZ[k]
        got = plane_recv[first : first + count, :].astype(F32)
        parts[dz] = got if dz not in parts else parts[dz] + got
    owned = parts[0] + jnp.concatenate([parts[1], parts[-1]], axis=0)

    owned_edges = jnp.broadcast_to((owned * (1.0 / NEIGH))[:, None, :], (ATOMS, NEIGH, WIDTH)).reshape(EDGES, WIDTH)
    summed_g = (edge_buf[...] + owned_edges) * upd_d[...]
    edge_buf[...] = summed_g
    summed_b[...] = summed_g.astype(BF16)
    for j in range(GROUPS):
        span = slice(128 * j, 128 * (j + 1))
        placed(values, j, dot(diag_a[j], summed_b[span, :]).astype(BF16))
    for value, weight in zip(values, update_w):
        value[...] = (dot(value[...], weight, NT) * (1.0 / NEIGH)).astype(BF16)
    angular_g = [[] for _ in range(9)]
    for j in range(GROUPS):
        span = slice(128 * j, 128 * (j + 1))
        value_g = gathered(values, j)
        latent_buf[span, :] = dot(diag_at[j], value_g)
        all_g = dot(
            jnp.concatenate([gathered(mixes, j), value_g], axis=1),
            jnp.concatenate([summed_b[span, :], env_buf[span, :]], axis=1),
            NT,
        )
        for m in range(1, 9):
            angular_g[m].append(
                jnp.sum(all_g[GROUP * m : GROUP * (m + 1)] * group_mask, axis=0, keepdims=True)
            )
    latent_g = dot(latent_buf[...].astype(BF16), env_ref[...], NT).astype(BF16).astype(F32)
    mixed_g = ((edge_buf[...] + latent_g) * mix_d[...]).astype(BF16)
    act_g = dot(mixed_g, mix_ref[...], NT).astype(BF16).astype(F32)
    before_g = (act_g * act_d[...]).astype(BF16)
    basis_g = dot(radial_ref[...], before_g, NT).astype(BF16).astype(F32)

    distance_g = jnp.sum(basis_g * basis_d, axis=0, keepdims=True)
    g = [jnp.concatenate(parts_m, axis=1) if parts_m else None for parts_m in angular_g]
    gu_x = g[1] + ROOT3 * (u_y * g[4] + u_z * g[7] + u_x * g[8])
    gu_y = g[2] + ROOT3 * (u_x * g[4] + u_z * g[5] - u_y * g[8])
    gu_z = g[3] + ROOT3 * (u_y * g[5] + u_x * g[7]) + 3.0 * u_z * g[6]
    along = distance_g - inverse * (u_x * gu_x + u_y * gu_y + u_z * gu_z)
    pull = [-(gu * inverse + u * along) for gu, u in ((gu_x, u_x), (gu_y, u_y), (gu_z, u_z))]
    pull4 = jnp.concatenate(pull + [jnp.zeros_like(u_x)], axis=0)
    high = pull4.astype(BF16).astype(F32)
    pull8 = jnp.concatenate([high, pull4 - high], axis=0)

    pulls = jnp.concatenate([jnp.where(level == a, pull8, 0.0) for a in range(3)], axis=0).astype(BF16)
    spread_f = dot(pulls, onehot_t[...], NT)
    for a in range(3):
        level_f = spread_f[8 * a : 8 * a + 4] + spread_f[8 * a + 4 : 8 * a + 8]
        for i in range(6):
            force_tab[3 * a + i // 2, i % 2] = level_f[:, 128 * i : 128 * (i + 1)]
    for k, (dx, dy, dz) in enumerate(AROUND):
        copy = remote(
            force_tab.at[3 * dx + dy + 4, 1 if dz else 0],
            force_recv.at[k],
            send_a.at[1],
            recv_a.at[1],
            device(dx, dy, dz),
        )
        copy.start()
    both = dot(pull8.astype(BF16), members, NT)
    own_f = both[0:4] + both[4:8]
    settle(force_recv, recv_a.at[1])
    total = force_tab[4, 0] - own_f
    ends = {}
    for k, (dx, dy, dz) in enumerate(AROUND):
        got = force_recv[k]
        if dz == 0:
            total = total + got
        else:
            ends[dz] = got if dz not in ends else ends[dz] + got
    total = total + jnp.where(half_lane, ends[1], ends[-1])
    energy_ref[0, 0] = jnp.concatenate(
        [energy[0:1, SLOTS * z : SLOTS * (z + 1)] for z in range(CELLS_Z)], axis=0
    )
    force_ref[0, 0] = jnp.concatenate(
        [
            jnp.concatenate([total[c : c + 1, SLOTS * z : SLOTS * (z + 1)] for c in range(3)], axis=1)
            for z in range(CELLS_Z)
        ],
        axis=0,
    )
    settle(force_recv, send_a.at[1])


def on_device(
    positions,
    species,
    neighbors,
    center_table,
    neighbor_table,
    radial_weight,
    mix_weight,
    env_weight,
    update_weight,
    second_weight,
    readout,
):
    dma = pltpu.SemaphoreType.DMA
    vmem = pltpu.VMEM
    cells = positions.shape[:3]
    args = (
        positions,
        species,
        neighbors,
        center_table,
        neighbor_table,
        radial_weight,
        mix_weight,
        env_weight,
        update_weight,
        second_weight,
        readout.reshape(1, WIDTH),
    )
    energies, forces = pl.pallas_call(
        kernel,
        out_shape=(pltpu.VMEM((*cells, SLOTS), F32), pltpu.VMEM((*cells, 3 * SLOTS), F32)),
        in_specs=[pl.BlockSpec(memory_space=pl.ANY)] * len(args),
        out_specs=[pl.BlockSpec(memory_space=pltpu.VMEM)] * 2,
        scratch_shapes=[
            *(vmem(arg.shape, arg.dtype) for arg in args),
            dma((len(args),)),
            vmem((27, 4, 128), F32),
            vmem((EDGES, LEVEL), BF16),
            vmem((LEVEL, EDGES), BF16),
            vmem((GROUPS, 128, 128), F32),
            vmem((EDGES, 128), F32),
            vmem((3, EDGES, 128), BF16),
            vmem((9, PLANE, WIDTH), BF16),
            vmem((24, WIDTH), F32),
            vmem((EDGES, WIDTH), F32),
            vmem((EDGES, WIDTH), F32),
            vmem((EDGES, WIDTH), F32),
            vmem((EDGES, WIDTH), BF16),
            vmem((GROUPS, 9 * GROUP, 128), BF16),
            vmem((GROUPS, 128, 9 * GROUP), BF16),
            vmem((1 * ATOMS, WIDTH), BF16),
            vmem((3 * ATOMS, WIDTH), BF16),
            vmem((5 * ATOMS, WIDTH), BF16),
            vmem((1 * ATOMS, WIDTH), BF16),
            vmem((3 * ATOMS, WIDTH), BF16),
            vmem((5 * ATOMS, WIDTH), BF16),
            vmem((EDGES, WIDTH), BF16),
            vmem((EDGES, WIDTH), F32),
            vmem((EDGES, WIDTH), F32),
            vmem((2, 3, PLANE, WIDTH), BF16),
            vmem((2, 3, PLANE, WIDTH), BF16),
            vmem((3, PLANE, WIDTH), BF16),
            vmem((640, WIDTH), BF16),
            vmem((9, 2, 4, 128), F32),
            vmem((26, 4, 128), F32),
            dma((2,)),
            dma((2,)),
            dma((4,)),
            dma((17,)),
            dma((14,)),
            dma((8,)),
        ],
        compiler_params=pltpu.CompilerParams(collective_id=0, has_side_effects=True),
    )(*args)
    return energies, forces


def solution(mesh):
    placed = (
        P("gx", "gy", "gz", None),
        P("gx", "gy", "gz", None),
        P("gx", "gy", "gz", None),
        P(),
        P(),
        P(),
        P(),
        P(),
        P(),
        P(),
        P(),
    )
    return jax.shard_map(
        on_device,
        mesh=mesh,
        in_specs=placed,
        out_specs=(P("gx", "gy", "gz", None), P("gx", "gy", "gz", None)),
        check_vma=False,
    )
```

```python
import itertools
import math

import jax
import jax.numpy as jnp
from jax import lax
from jax.experimental import pallas as pl
from jax.experimental.pallas import tpu as pltpu
from jax.sharding import PartitionSpec as P

MESH = pl.DeviceIdType.MESH
F32 = jnp.float32
BF16 = jnp.bfloat16
HIGH = lax.Precision.HIGHEST

NEIGH = 8
SLOTS = 64
CUTOFF = 4.0
SHARPNESS = 2.0
NBASIS = 8
CELLS_Z = 2
ATOMS = CELLS_Z * SLOTS
EDGES = ATOMS * NEIGH
WIDTH = 128
PLANE = 256
LEVEL = 3 * PLANE
GROUP = 16
GROUPS = ATOMS // GROUP
ROOT3 = math.sqrt(3.0)
PIECE_ORDER = {0: 0, 1: 1, -1: 2}
GRAD_ENDS, GRAD_OWN = (128, 128), (0, 128)
GRAD_ORDER = ((0, ((0, 0),)), (2, ((2, 0), (0, 1), (2, 1))), (1, ((1, 0), (1, 1))))

PARTNERS = ((1, -1), (-1, 1), (1, 1), (-1, -1), (0, 1), (0, -1), (1, 0), (-1, 0))
AROUND = sorted(
    (d for d in itertools.product((-1, 0, 1), repeat=3) if any(d)), key=lambda d: -sum(abs(c) for c in d)
)
ROWS = {0: (0, 128), 1: (128, 64), -1: (192, 64)}
SLOTS_YZ = tuple((64 * k, 64) if dz else (384 + 128 * (k - 6), 128) for k, (dy, dz) in enumerate(PARTNERS))


def split_bf16(value):
    high = value.astype(BF16)
    return high, (value - high.astype(F32)).astype(BF16)


def dot(a, b, dims=((1,), (0,)), precision=None):
    return lax.dot_general(a, b, (dims, ((), ())), preferred_element_type=F32, precision=precision)


NT = ((1,), (1,))


def sigmoid(value):
    return 0.5 + 0.5 * jnp.tanh(0.5 * value)


def kernel(
    pos_in,
    spec_in,
    nbr_in,
    center_in,
    neighbor_in,
    radial_in,
    mix_in,
    env_in,
    update_in,
    second_in,
    readout_in,
    energy_ref,
    force_ref,
    pos_ref,
    spec_ref,
    nbr_ref,
    center_ref,
    neighbor_ref,
    radial_ref,
    mix_ref,
    env_ref,
    update_ref,
    second_ref,
    readout_ref,
    load_sem,
    tiles,
    onehot,
    onehot_t,
    target_col,
    level_col,
    level_mask,
    table,
    weights,
    act_d,
    mix_d,
    upd_d,
    env_buf,
    diag_a,
    diag_at,
    value_0,
    value_1,
    value_2,
    mixed_0,
    mixed_1,
    mixed_2,
    summed_b,
    latent_buf,
    edge_buf,
    grad_send,
    grad_recv,
    plane_send,
    plane_recv,
    force_tab,
    force_recv,
    send_a,
    recv_a,
    send_c,
    recv_c,
    recv_x,
    recv_d,
):
    size_x, size_y, size_z = lax.axis_size("gx"), lax.axis_size("gy"), lax.axis_size("gz")
    my_x, my_y, my_z = lax.axis_index("gx"), lax.axis_index("gy"), lax.axis_index("gz")

    near = []
    for index, size in ((my_x, size_x), (my_y, size_y), (my_z, size_z)):
        near.append(
            (index, jnp.where(index == size - 1, 0, index + 1), jnp.where(index == 0, size - 1, index - 1))
        )

    def device(dx, dy, dz):
        return near[0][dx], near[1][dy], near[2][dz]

    def settle(ref, sem):
        pltpu.make_async_copy(ref, ref, sem).wait()

    def remote(src, dst, send, recv, target):
        return pltpu.make_async_remote_copy(
            src_ref=src, dst_ref=dst, send_sem=send, recv_sem=recv, device_id=target, device_id_type=MESH
        )

    sources = (
        pos_in, spec_in, nbr_in, center_in, neighbor_in, radial_in, mix_in, env_in, update_in, second_in, readout_in
    )
    places = (
        pos_ref, spec_ref, nbr_ref, center_ref, neighbor_ref, radial_ref, mix_ref, env_ref, update_ref, second_ref,
        readout_ref,
    )
    loads = [pltpu.make_async_copy(src, dst, load_sem.at[k]) for k, (src, dst) in enumerate(zip(sources, places))]
    for load in loads[:3]:
        load.start()
    barrier = pltpu.get_barrier_semaphore()
    for step in AROUND:
        pl.semaphore_signal(barrier, inc=1, device_id=device(*step), device_id_type=MESH)
    for load in loads[3:]:
        load.start()
    loads[0].wait()
    loads[1].wait()

    coords = pos_ref[0, 0]
    kinds = spec_ref[0, 0].astype(F32)
    rows = [
        jnp.concatenate([coords[z : z + 1, SLOTS * c : SLOTS * (c + 1)] for z in range(CELLS_Z)], axis=1)
        for c in range(3)
    ]
    rows.append(jnp.concatenate([kinds[z : z + 1, :] for z in range(CELLS_Z)], axis=1))
    own_tile = jnp.concatenate(rows, axis=0)
    tiles[13] = own_tile

    pl.semaphore_wait(barrier, len(AROUND))

    far_side = lax.rem(my_x, 2)
    sides = (far_side, 1 - far_side)

    def x_device(side):
        return jnp.where(side == 0, near[0][-1], near[0][1]), my_y, my_z

    def forward(source, dest, send, recv, k):
        copies = []
        for side in sides[::-1]:
            copy = remote(
                source,
                dest(3 * (2 * side)),
                send.at[1],
                recv.at[2 * k + side],
                x_device(1 - side),
            )
            copy.start()
            copies.append(copy)
        return copies

    def tile_of(dx, dy, dz):
        return 9 * (dx + 1) + 3 * (dy + 1) + (dz + 1)

    for dx, dy, dz in AROUND:
        copy = remote(
            tiles.at[13], tiles.at[tile_of(dx, dy, dz)], send_a.at[0], recv_a.at[0], device(-dx, -dy, -dz)
        )
        copy.start()

    loads[2].wait()
    codes = nbr_ref[0, 0]
    offset_code = lax.shift_right_logical(codes, 6)
    slot = jnp.bitwise_and(codes, SLOTS - 1)
    column_code = lax.shift_right_logical(offset_code * 171, 9)
    row_z = offset_code - 3 * column_code
    own_z = lax.broadcasted_iota(jnp.int32, codes.shape, 0)
    place = jnp.bitwise_and(row_z + own_z + 3, 3)
    step_a = lax.shift_right_logical(column_code * 171, 9)
    step_e = column_code - 3 * step_a

    def flat(value):
        return jnp.concatenate([value[z : z + 1, :] for z in range(CELLS_Z)], axis=1)

    target = flat((step_e * 4 + place) * SLOTS + slot)
    level = flat(step_a)
    offsets = [flat(step - 1).astype(F32) for step in (step_a, step_e, row_z)]

    row_kinds = [target[:, 128 * j : 128 * (j + 1)].astype(F32) for j in range(8)]
    row_kinds += [level[:, 128 * j : 128 * (j + 1)].astype(F32) for j in range(8)]
    columns = jnp.transpose(jnp.concatenate(row_kinds + [jnp.zeros((112, 128), F32)], axis=0))
    for j in range(8):
        target_col[j] = jnp.broadcast_to(columns[:, j : j + 1], (128, 128))
        level_col[128 * j : 128 * (j + 1), :] = jnp.broadcast_to(columns[:, 8 + j : 9 + j], (128, 128))

    def build(j, carry):
        first = pl.multiple_of(j * 128, 128)
        level_j = level_col[pl.ds(first, 128), :]
        for a in range(3):
            level_mask[a, pl.ds(first, 128), :] = (level_j == float(a)).astype(F32).astype(BF16)
        lane = lax.broadcasted_iota(jnp.int32, (128, 128), 1).astype(F32)
        column = target_col[j]
        for t in range(LEVEL // 128):
            onehot[pl.ds(first, 128), 128 * t : 128 * (t + 1)] = (
                (column == lane + float(128 * t)).astype(F32).astype(BF16)
            )
        return carry

    lax.fori_loop(0, GROUPS, build, 0)

    def build_t(t, carry):
        first = pl.multiple_of(t * 128, 128)
        row = lax.broadcasted_iota(jnp.int32, (128, EDGES), 0) + first
        onehot_t[pl.ds(first, 128), :] = (row == target).astype(F32).astype(BF16)
        return carry

    lax.fori_loop(0, LEVEL // 128, build_t, 0)

    for load in loads[3:]:
        load.wait()
    weights[...] = jnp.zeros_like(weights)
    weights[0:NBASIS, :] = radial_ref[...].astype(F32)
    spec_count = center_ref.shape[0]
    weights[8 : 8 + spec_count, :] = center_ref[...].astype(F32)
    weights[16 : 16 + spec_count, :] = neighbor_ref[...].astype(F32)
    before_w = weights[...].astype(BF16)

    settle(tiles.at[pl.ds(0, len(AROUND))], recv_a.at[0])
    settle(tiles.at[pl.ds(0, len(AROUND))], send_a.at[0])

    half_lane = lax.broadcasted_iota(jnp.int32, (4, 128), 1) < SLOTS
    halves = []
    for p in range(9):
        halves.append(tiles[3 * p + 1])
        halves.append(jnp.where(half_lane, tiles[3 * p + 2], tiles[3 * p]))
    packed = [jnp.concatenate([halves[t], halves[t + 9]], axis=0) for t in range(9)]
    own8 = jnp.concatenate([own_tile, own_tile], axis=0)
    lane8 = lax.broadcasted_iota(jnp.int32, (8, 128), 1)
    others, centers = [], []
    for j in range(8):
        goal = (target + LEVEL * level)[:, 128 * j : 128 * (j + 1)]
        spot = jnp.broadcast_to(jnp.bitwise_and(goal, 127), (8, 128))
        which = lax.shift_right_logical(goal, 7)
        late = which >= 9
        which = jnp.broadcast_to(jnp.where(late, which - 9, which), (8, 128))
        found = jnp.zeros((8, 128), F32)
        for t in range(9):
            picked = jnp.take_along_axis(packed[t], spot, axis=1)
            found = jnp.where(which == t, picked, found)
        others.append(jnp.where(jnp.broadcast_to(late, (4, 128)), found[4:8], found[0:4]))
        mine = jnp.take_along_axis(own8, lax.shift_right_logical(lane8, 3) + GROUP * j, axis=1)
        centers.append(mine[0:4])
    other = jnp.concatenate(others, axis=1)
    center = jnp.concatenate(centers, axis=1)

    d_x, d_y, d_z = (offsets[c] + (other[c : c + 1] - center[c : c + 1]) for c in range(3))
    distance = jnp.sqrt(d_x * d_x + d_y * d_y + d_z * d_z)
    inverse = 1.0 / distance
    u_x, u_y, u_z = d_x * inverse, d_y * inverse, d_z * inverse
    angular = [
        jnp.ones_like(u_x),
        u_x,
        u_y,
        u_z,
        ROOT3 * u_x * u_y,
        ROOT3 * u_y * u_z,
        0.5 * (3.0 * u_z * u_z - 1.0),
        ROOT3 * u_x * u_z,
        0.5 * ROOT3 * (u_x * u_x - u_y * u_y),
    ]
    ratio = distance * (1.0 / CUTOFF)
    inside = 1.0 - ratio * ratio
    index8 = lax.broadcasted_iota(jnp.int32, (8, EDGES), 0)
    mu = (index8.astype(F32) + 0.5) * (CUTOFF / NBASIS)
    apart = distance - mu
    bell = jnp.exp(-SHARPNESS * apart * apart)
    basis = bell * (inside * inside)
    basis_d = bell * (-2.0 * SHARPNESS * apart * (inside * inside) - ratio * inside)
    hot_center = (index8.astype(F32) == center[3:4]).astype(F32)
    hot_other = (index8.astype(F32) == other[3:4]).astype(F32)
    features = jnp.concatenate([basis, hot_center, hot_other], axis=0)
    features = jnp.transpose(features).astype(BF16)

    group_mask = (
        lax.shift_right_logical(lax.broadcasted_iota(jnp.int32, (GROUP, 128), 1), 3)
        == lax.broadcasted_iota(jnp.int32, (GROUP, 128), 0)
    ).astype(F32)
    members = (
        lax.shift_right_logical(lax.broadcasted_iota(jnp.int32, (ATOMS, EDGES), 1), 3)
        == lax.broadcasted_iota(jnp.int32, (ATOMS, EDGES), 0)
    ).astype(F32).astype(BF16)
    levels = ((0, 1), (1, 4), (4, 9))
    update_w = [update_ref[WIDTH * l : WIDTH * (l + 1), :] for l in range(3)]

    def gathered(buffers, j):
        return jnp.concatenate(
            [
                buffer[GROUP * (stop - start) * j : GROUP * (stop - start) * (j + 1), :]
                for buffer, (start, stop) in zip(buffers, levels)
            ],
            axis=0,
        )

    def placed(buffers, j, value):
        for buffer, (start, stop) in zip(buffers, levels):
            rows_l = GROUP * (stop - start)
            buffer[rows_l * j : rows_l * (j + 1), :] = value[GROUP * start : GROUP * stop]

    values = (value_0, value_1, value_2)
    mixes = (mixed_0, mixed_1, mixed_2)
    half_edges = EDGES // CELLS_Z
    half_groups = GROUPS // CELLS_Z
    yz = {}
    moved_c = {0: [], 1: [], -1: []}
    for z in range(CELLS_Z):
        block = slice(half_edges * z, half_edges * (z + 1))
        before = dot(features[block, :], before_w)
        gate = sigmoid(before)
        act = before * gate
        act_d[block, :] = gate + act * (1.0 - gate)
        mixed = dot(act.astype(BF16), mix_ref[...])
        gate = sigmoid(mixed)
        latent = mixed * gate
        mix_d[block, :] = gate + latent * (1.0 - gate)
        env_buf[block, :] = dot(latent.astype(BF16), env_ref[...]).astype(BF16)
        for j in range(half_groups * z, half_groups * (z + 1)):
            span = slice(128 * j, 128 * (j + 1))
            spread_y = jnp.concatenate([angular[m][:, span] * group_mask for m in range(9)], axis=0)
            diag_a[j] = spread_y.astype(BF16)
            diag_at[j] = jnp.transpose(diag_a[j])
            placed(values, j, (dot(diag_a[j], env_buf[span, :]) * (1.0 / NEIGH)).astype(BF16))
        for value, mixed_l, weight, (start, stop) in zip(values, mixes, update_w, levels):
            rows_l = GROUP * (stop - start) * half_groups
            span = slice(rows_l * z, rows_l * (z + 1))
            mixed_l[span, :] = dot(value[span, :], weight).astype(BF16)
        update = jnp.concatenate(
            [dot(diag_at[j], gathered(mixes, j)) for j in range(half_groups * z, half_groups * (z + 1))], axis=0
        )
        summed = latent + update
        gate = sigmoid(summed)
        edge = summed * gate
        upd_d[block, :] = gate + edge * (1.0 - gate)
        edge_buf[block, :] = edge
        high, low = split_bf16(edge)
        mine = members[0:SLOTS, 0:half_edges]
        own_rows = pl.ds(SLOTS * z, SLOTS)
        table[4, SLOTS * z : SLOTS * (z + 1), :] = ((dot(mine, high) + dot(mine, low)) * (1.0 / NEIGH)).astype(BF16)
        for k, (dy, dz) in enumerate(PARTNERS):
            if dz == (-1 if z == 0 else 1):
                continue
            rows_there = own_rows if dz == 0 else pl.ds(*ROWS[dz])
            copy = remote(
                table.at[4, own_rows],
                table.at[4 + dy, rows_there],
                send_c.at[0],
                recv_c.at[k + 8 * z],
                device(0, -dy, -dz),
            )
            copy.start()
            yz[dy, dz, z] = copy
        moved_c[0] += forward(
            table.at[4, own_rows], lambda a, own_rows=own_rows: table.at[a + 1, own_rows], send_c, recv_x, z
        )

    k = CELLS_Z
    for (dy, dz, z), copy in sorted(yz.items(), key=lambda item: (item[0][2], PIECE_ORDER[item[0][0]])):
        copy.wait_recv()
        rows_here = pl.ds(SLOTS * z, SLOTS) if dz == 0 else pl.ds(*ROWS[dz])
        moved_c[dy] += forward(
            table.at[4 + dy, rows_here],
            lambda a, dy=dy, rows_here=rows_here: table.at[a + 1 + dy, rows_here],
            send_c,
            recv_x,
            k,
        )
        k += 1
    here = dot(onehot[...], jnp.concatenate([table[3], table[4], table[5]], axis=0))
    beside = jnp.zeros((EDGES, 2 * WIDTH), F32)
    for e in (1, 2, 0):
        for copy in moved_c[e - 1]:
            copy.wait_recv()
        pair_e = jnp.concatenate([table[e], table[6 + e]], axis=1)
        beside = beside + dot(onehot[:, PLANE * e : PLANE * (e + 1)], pair_e)
    levels_e = level_col[...]
    other_latent = jnp.where(
        levels_e == 1.0, here, jnp.where(levels_e == 0.0, beside[:, 0:WIDTH], beside[:, WIDTH : 2 * WIDTH])
    )

    edge = edge_buf[...]
    product = (edge * other_latent).astype(BF16)
    second_w = second_ref[...]
    readout = readout_ref[...]
    hidden_in = dot(product, second_w)
    gate = sigmoid(hidden_in)
    hidden = hidden_in * gate
    hidden_g = (readout * (gate + hidden * (1.0 - gate))).astype(BF16)
    product_g = dot(hidden_g, second_w, NT).astype(BF16).astype(F32)
    other_g = (product_g * edge).astype(BF16)
    beside_g = jnp.concatenate([other_g * level_mask[0], other_g * level_mask[2]], axis=1)
    here_g = other_g * level_mask[1]
    edge_buf[...] = product_g * other_latent

    moved_x = {}
    for e, chunks in GRAD_ORDER:
        grads = dot(onehot_t[PLANE * e : PLANE * (e + 1), :], beside_g).astype(BF16)
        grad_send[0, e] = grads[:, 0:WIDTH]
        grad_send[1, e] = grads[:, WIDTH : 2 * WIDTH]
        for e_sent, c in chunks:
            chunk = pl.ds(*(GRAD_OWN if c else GRAD_ENDS))
            for order, side in enumerate(sides):
                copy = remote(
                    grad_send.at[side, e_sent, chunk],
                    grad_recv.at[side, e_sent, chunk],
                    send_c.at[2],
                    recv_d.at[6 * side + 2 * e_sent + c],
                    x_device(side),
                )
                copy.start()
                moved_x[order, e_sent, c] = copy
    middle_grad = dot(onehot_t[...], here_g)
    plane_sum = {e: middle_grad[PLANE * e : PLANE * (e + 1)] for e in range(3)}

    high, low = split_bf16(hidden * readout)
    atom_terms = dot(members, high) + dot(members, low)
    energy = dot(jnp.ones((8, WIDTH), F32), atom_terms, NT, HIGH)

    for e, c in ((0, 0), (2, 0), (0, 1), (2, 1), (1, 0)):
        moved_x[0, e, c].wait_recv()
        moved_x[1, e, c].wait_recv()
        first, count = GRAD_OWN if c else GRAD_ENDS
        arrived = slice(first, first + count)
        plane_send[e, arrived, :] = (
            plane_sum[e][arrived] + grad_recv[0, e, arrived, :].astype(F32) + grad_recv[1, e, arrived, :].astype(F32)
        ).astype(BF16)
        for k, (dy, dz) in enumerate(PARTNERS):
            if dy == e - 1 and (dz == 0) == (c == 1):
                copy = remote(
                    plane_send.at[e, pl.ds(*ROWS[dz])],
                    plane_recv.at[pl.ds(*SLOTS_YZ[k])],
                    send_c.at[3],
                    recv_c.at[16],
                    device(0, dy, dz),
                )
                copy.start()
    moved_x[0, 1, 1].wait_recv()
    moved_x[1, 1, 1].wait_recv()
    own_sum = plane_sum[1][0:128] + grad_recv[0, 1, 0:128, :].astype(F32) + grad_recv[1, 1, 0:128, :].astype(F32)
    settle(plane_recv, send_c.at[0])
    settle(table.at[pl.ds(0, 6)], send_c.at[1])
    settle(grad_send, send_c.at[2])
    settle(plane_recv, send_c.at[3])
    settle(plane_recv, recv_c.at[16])
    parts = {0: own_sum}
    for k, (dy, dz) in enumerate(PARTNERS):
        first, count = SLOTS_YZ[k]
        got = plane_recv[first : first + count, :].astype(F32)
        parts[dz] = got if dz not in parts else parts[dz] + got
    owned = parts[0] + jnp.concatenate([parts[1], parts[-1]], axis=0)

    owned_edges = jnp.broadcast_to((owned * (1.0 / NEIGH))[:, None, :], (ATOMS, NEIGH, WIDTH)).reshape(EDGES, WIDTH)
    summed_g = (edge_buf[...] + owned_edges) * upd_d[...]
    edge_buf[...] = summed_g
    summed_b[...] = summed_g.astype(BF16)
    for j in range(GROUPS):
        span = slice(128 * j, 128 * (j + 1))
        placed(values, j, dot(diag_a[j], summed_b[span, :]).astype(BF16))
    for value, weight in zip(values, update_w):
        value[...] = (dot(value[...], weight, NT) * (1.0 / NEIGH)).astype(BF16)
    angular_g = [[] for _ in range(9)]
    for j in range(GROUPS):
        span = slice(128 * j, 128 * (j + 1))
        value_g = gathered(values, j)
        latent_buf[span, :] = dot(diag_at[j], value_g)
        all_g = dot(
            jnp.concatenate([gathered(mixes, j), value_g], axis=1),
            jnp.concatenate([summed_b[span, :], env_buf[span, :]], axis=1),
            NT,
        )
        for m in range(1, 9):
            angular_g[m].append(
                jnp.sum(all_g[GROUP * m : GROUP * (m + 1)] * group_mask, axis=0, keepdims=True)
            )
    latent_g = dot(latent_buf[...].astype(BF16), env_ref[...], NT).astype(BF16).astype(F32)
    mixed_g = ((edge_buf[...] + latent_g) * mix_d[...]).astype(BF16)
    act_g = dot(mixed_g, mix_ref[...], NT).astype(BF16).astype(F32)
    before_g = (act_g * act_d[...]).astype(BF16)
    basis_g = dot(radial_ref[...], before_g, NT).astype(BF16).astype(F32)

    distance_g = jnp.sum(basis_g * basis_d, axis=0, keepdims=True)
    g = [jnp.concatenate(parts_m, axis=1) if parts_m else None for parts_m in angular_g]
    gu_x = g[1] + ROOT3 * (u_y * g[4] + u_z * g[7] + u_x * g[8])
    gu_y = g[2] + ROOT3 * (u_x * g[4] + u_z * g[5] - u_y * g[8])
    gu_z = g[3] + ROOT3 * (u_y * g[5] + u_x * g[7]) + 3.0 * u_z * g[6]
    along = distance_g - inverse * (u_x * gu_x + u_y * gu_y + u_z * gu_z)
    pull = [-(gu * inverse + u * along) for gu, u in ((gu_x, u_x), (gu_y, u_y), (gu_z, u_z))]
    pull4 = jnp.concatenate(pull + [jnp.zeros_like(u_x)], axis=0)
    high = pull4.astype(BF16).astype(F32)
    pull8 = jnp.concatenate([high, pull4 - high], axis=0)

    pulls = jnp.concatenate([jnp.where(level == a, pull8, 0.0) for a in range(3)], axis=0).astype(BF16)
    spread_f = dot(pulls, onehot_t[...], NT)
    for a in range(3):
        level_f = spread_f[8 * a : 8 * a + 4] + spread_f[8 * a + 4 : 8 * a + 8]
        for i in range(6):
            force_tab[3 * a + i // 2, i % 2] = level_f[:, 128 * i : 128 * (i + 1)]
    for k, (dx, dy, dz) in enumerate(AROUND):
        copy = remote(
            force_tab.at[3 * dx + dy + 4, 1 if dz else 0],
            force_recv.at[k],
            send_a.at[1],
            recv_a.at[1],
            device(dx, dy, dz),
        )
        copy.start()
    both = dot(pull8.astype(BF16), members, NT)
    own_f = both[0:4] + both[4:8]
    settle(force_recv, recv_a.at[1])
    total = force_tab[4, 0] - own_f
    ends = {}
    for k, (dx, dy, dz) in enumerate(AROUND):
        got = force_recv[k]
        if dz == 0:
            total = total + got
        else:
            ends[dz] = got if dz not in ends else ends[dz] + got
    total = total + jnp.where(half_lane, ends[1], ends[-1])
    energy_ref[0, 0] = jnp.concatenate(
        [energy[0:1, SLOTS * z : SLOTS * (z + 1)] for z in range(CELLS_Z)], axis=0
    )
    force_ref[0, 0] = jnp.concatenate(
        [
            jnp.concatenate([total[c : c + 1, SLOTS * z : SLOTS * (z + 1)] for c in range(3)], axis=1)
            for z in range(CELLS_Z)
        ],
        axis=0,
    )
    settle(force_recv, send_a.at[1])


def on_device(
    positions,
    species,
    neighbors,
    center_table,
    neighbor_table,
    radial_weight,
    mix_weight,
    env_weight,
    update_weight,
    second_weight,
    readout,
):
    dma = pltpu.SemaphoreType.DMA
    vmem = pltpu.VMEM
    cells = positions.shape[:3]
    args = (
        positions,
        species,
        neighbors,
        center_table,
        neighbor_table,
        radial_weight,
        mix_weight,
        env_weight,
        update_weight,
        second_weight,
        readout.reshape(1, WIDTH),
    )
    energies, forces = pl.pallas_call(
        kernel,
        out_shape=(pltpu.VMEM((*cells, SLOTS), F32), pltpu.VMEM((*cells, 3 * SLOTS), F32)),
        in_specs=[pl.BlockSpec(memory_space=pl.ANY)] * len(args),
        out_specs=[pl.BlockSpec(memory_space=pltpu.VMEM)] * 2,
        scratch_shapes=[
            *(vmem(arg.shape, arg.dtype) for arg in args),
            dma((len(args),)),
            vmem((27, 4, 128), F32),
            vmem((EDGES, LEVEL), BF16),
            vmem((LEVEL, EDGES), BF16),
            vmem((GROUPS, 128, 128), F32),
            vmem((EDGES, 128), F32),
            vmem((3, EDGES, 128), BF16),
            vmem((9, PLANE, WIDTH), BF16),
            vmem((24, WIDTH), F32),
            vmem((EDGES, WIDTH), F32),
            vmem((EDGES, WIDTH), F32),
            vmem((EDGES, WIDTH), F32),
            vmem((EDGES, WIDTH), BF16),
            vmem((GROUPS, 9 * GROUP, 128), BF16),
            vmem((GROUPS, 128, 9 * GROUP), BF16),
            vmem((1 * ATOMS, WIDTH), BF16),
            vmem((3 * ATOMS, WIDTH), BF16),
            vmem((5 * ATOMS, WIDTH), BF16),
            vmem((1 * ATOMS, WIDTH), BF16),
            vmem((3 * ATOMS, WIDTH), BF16),
            vmem((5 * ATOMS, WIDTH), BF16),
            vmem((EDGES, WIDTH), BF16),
            vmem((EDGES, WIDTH), F32),
            vmem((EDGES, WIDTH), F32),
            vmem((2, 3, PLANE, WIDTH), BF16),
            vmem((2, 3, PLANE, WIDTH), BF16),
            vmem((3, PLANE, WIDTH), BF16),
            vmem((640, WIDTH), BF16),
            vmem((9, 2, 4, 128), F32),
            vmem((26, 4, 128), F32),
            dma((2,)),
            dma((2,)),
            dma((4,)),
            dma((17,)),
            dma((24,)),
            dma((12,)),
        ],
        compiler_params=pltpu.CompilerParams(collective_id=0, has_side_effects=True),
    )(*args)
    return energies, forces


def solution(mesh):
    placed = (
        P("gx", "gy", "gz", None),
        P("gx", "gy", "gz", None),
        P("gx", "gy", "gz", None),
        P(),
        P(),
        P(),
        P(),
        P(),
        P(),
        P(),
        P(),
    )
    return jax.shard_map(
        on_device,
        mesh=mesh,
        in_specs=placed,
        out_specs=(P("gx", "gy", "gz", None), P("gx", "gy", "gz", None)),
        check_vma=False,
    )
```

```python
import itertools
import math

import jax
import jax.numpy as jnp
from jax import lax
from jax.experimental import pallas as pl
from jax.experimental.pallas import tpu as pltpu
from jax.sharding import PartitionSpec as P

MESH = pl.DeviceIdType.MESH
F32 = jnp.float32
BF16 = jnp.bfloat16
HIGH = lax.Precision.HIGHEST

NEIGH = 8
SLOTS = 64
CUTOFF = 4.0
SHARPNESS = 2.0
NBASIS = 8
CELLS_Z = 2
ATOMS = CELLS_Z * SLOTS
EDGES = ATOMS * NEIGH
WIDTH = 128
PLANE = 256
LEVEL = 3 * PLANE
GROUP = 16
GROUPS = ATOMS // GROUP
ROOT3 = math.sqrt(3.0)
PIECE_ORDER = {0: 0, 1: 1, -1: 2}
GRAD_ENDS, GRAD_OWN = (128, 128), (0, 128)
GRAD_ORDER = ((0, ((0, 0),)), (2, ((2, 0), (0, 1), (2, 1))), (1, ((1, 0), (1, 1))))

PARTNERS = ((1, -1), (-1, 1), (1, 1), (-1, -1), (0, 1), (0, -1), (1, 0), (-1, 0))
AROUND = sorted(
    (d for d in itertools.product((-1, 0, 1), repeat=3) if any(d)), key=lambda d: -sum(abs(c) for c in d)
)
ROWS = {0: (0, 128), 1: (128, 64), -1: (192, 64)}
SLOTS_YZ = tuple((64 * k, 64) if dz else (384 + 128 * (k - 6), 128) for k, (dy, dz) in enumerate(PARTNERS))


def split_bf16(value):
    high = value.astype(BF16)
    return high, (value - high.astype(F32)).astype(BF16)


def dot(a, b, dims=((1,), (0,)), precision=None):
    return lax.dot_general(a, b, (dims, ((), ())), preferred_element_type=F32, precision=precision)


NT = ((1,), (1,))


def sigmoid(value):
    return 0.5 + 0.5 * jnp.tanh(0.5 * value)


def kernel(
    pos_in,
    spec_in,
    nbr_in,
    center_in,
    neighbor_in,
    radial_in,
    mix_in,
    env_in,
    update_in,
    second_in,
    readout_in,
    energy_ref,
    force_ref,
    pos_ref,
    spec_ref,
    nbr_ref,
    center_ref,
    neighbor_ref,
    radial_ref,
    mix_ref,
    env_ref,
    update_ref,
    second_ref,
    readout_ref,
    load_sem,
    tiles,
    onehot,
    onehot_t,
    target_col,
    level_col,
    level_mask,
    table,
    weights,
    act_d,
    mix_d,
    upd_d,
    env_buf,
    diag_a,
    diag_at,
    value_0,
    value_1,
    value_2,
    mixed_0,
    mixed_1,
    mixed_2,
    summed_b,
    latent_buf,
    edge_buf,
    grad_send,
    grad_recv,
    plane_send,
    plane_recv,
    force_tab,
    force_recv,
    send_a,
    recv_a,
    send_c,
    recv_c,
    recv_x,
    recv_d,
):
    size_x, size_y, size_z = lax.axis_size("gx"), lax.axis_size("gy"), lax.axis_size("gz")
    my_x, my_y, my_z = lax.axis_index("gx"), lax.axis_index("gy"), lax.axis_index("gz")

    near = []
    for index, size in ((my_x, size_x), (my_y, size_y), (my_z, size_z)):
        near.append(
            (index, jnp.where(index == size - 1, 0, index + 1), jnp.where(index == 0, size - 1, index - 1))
        )

    def device(dx, dy, dz):
        return near[0][dx], near[1][dy], near[2][dz]

    def settle(ref, sem):
        pltpu.make_async_copy(ref, ref, sem).wait()

    def remote(src, dst, send, recv, target):
        return pltpu.make_async_remote_copy(
            src_ref=src, dst_ref=dst, send_sem=send, recv_sem=recv, device_id=target, device_id_type=MESH
        )

    sources = (
        pos_in, spec_in, nbr_in, center_in, neighbor_in, radial_in, mix_in, env_in, update_in, second_in, readout_in
    )
    places = (
        pos_ref, spec_ref, nbr_ref, center_ref, neighbor_ref, radial_ref, mix_ref, env_ref, update_ref, second_ref,
        readout_ref,
    )
    loads = [pltpu.make_async_copy(src, dst, load_sem.at[k]) for k, (src, dst) in enumerate(zip(sources, places))]
    for load in loads[:3]:
        load.start()
    barrier = pltpu.get_barrier_semaphore()
    for step in AROUND:
        pl.semaphore_signal(barrier, inc=1, device_id=device(*step), device_id_type=MESH)
    for load in loads[3:]:
        load.start()
    loads[0].wait()
    loads[1].wait()

    coords = pos_ref[0, 0]
    kinds = spec_ref[0, 0].astype(F32)
    rows = [
        jnp.concatenate([coords[z : z + 1, SLOTS * c : SLOTS * (c + 1)] for z in range(CELLS_Z)], axis=1)
        for c in range(3)
    ]
    rows.append(jnp.concatenate([kinds[z : z + 1, :] for z in range(CELLS_Z)], axis=1))
    own_tile = jnp.concatenate(rows, axis=0)
    tiles[13] = own_tile

    pl.semaphore_wait(barrier, len(AROUND))

    far_side = lax.rem(my_x, 2)
    sides = (far_side, 1 - far_side)

    def x_device(side):
        return jnp.where(side == 0, near[0][-1], near[0][1]), my_y, my_z

    def forward(source, dest, send, recv, k):
        copies = []
        for side in sides[::-1]:
            copy = remote(
                source,
                dest(3 * (2 * side)),
                send.at[1],
                recv.at[2 * k + side],
                x_device(1 - side),
            )
            copy.start()
            copies.append(copy)
        return copies

    def tile_of(dx, dy, dz):
        return 9 * (dx + 1) + 3 * (dy + 1) + (dz + 1)

    for dx, dy, dz in AROUND:
        copy = remote(
            tiles.at[13], tiles.at[tile_of(dx, dy, dz)], send_a.at[0], recv_a.at[0], device(-dx, -dy, -dz)
        )
        copy.start()

    loads[2].wait()
    codes = nbr_ref[0, 0]
    offset_code = lax.shift_right_logical(codes, 6)
    slot = jnp.bitwise_and(codes, SLOTS - 1)
    column_code = lax.shift_right_logical(offset_code * 171, 9)
    row_z = offset_code - 3 * column_code
    own_z = lax.broadcasted_iota(jnp.int32, codes.shape, 0)
    place = jnp.bitwise_and(row_z + own_z + 3, 3)
    step_a = lax.shift_right_logical(column_code * 171, 9)
    step_e = column_code - 3 * step_a

    def flat(value):
        return jnp.concatenate([value[z : z + 1, :] for z in range(CELLS_Z)], axis=1)

    target = flat((step_e * 4 + place) * SLOTS + slot)
    level = flat(step_a)
    offsets = [flat(step - 1).astype(F32) for step in (step_a, step_e, row_z)]

    row_kinds = [target[:, 128 * j : 128 * (j + 1)].astype(F32) for j in range(8)]
    row_kinds += [level[:, 128 * j : 128 * (j + 1)].astype(F32) for j in range(8)]
    columns = jnp.transpose(jnp.concatenate(row_kinds + [jnp.zeros((112, 128), F32)], axis=0))
    for j in range(8):
        target_col[j] = jnp.broadcast_to(columns[:, j : j + 1], (128, 128))
        level_col[128 * j : 128 * (j + 1), :] = jnp.broadcast_to(columns[:, 8 + j : 9 + j], (128, 128))

    def build(j, carry):
        first = pl.multiple_of(j * 128, 128)
        level_j = level_col[pl.ds(first, 128), :]
        for a in range(3):
            level_mask[a, pl.ds(first, 128), :] = (level_j == float(a)).astype(F32).astype(BF16)
        lane = lax.broadcasted_iota(jnp.int32, (128, 128), 1).astype(F32)
        column = target_col[j]
        for t in range(LEVEL // 128):
            onehot[pl.ds(first, 128), 128 * t : 128 * (t + 1)] = (
                (column == lane + float(128 * t)).astype(F32).astype(BF16)
            )
        return carry

    lax.fori_loop(0, GROUPS, build, 0)

    def build_t(t, carry):
        first = pl.multiple_of(t * 128, 128)
        row = lax.broadcasted_iota(jnp.int32, (128, EDGES), 0) + first
        onehot_t[pl.ds(first, 128), :] = (row == target).astype(F32).astype(BF16)
        return carry

    lax.fori_loop(0, LEVEL // 128, build_t, 0)

    for load in loads[3:]:
        load.wait()
    weights[...] = jnp.zeros_like(weights)
    weights[0:NBASIS, :] = radial_ref[...].astype(F32)
    spec_count = center_ref.shape[0]
    weights[8 : 8 + spec_count, :] = center_ref[...].astype(F32)
    weights[16 : 16 + spec_count, :] = neighbor_ref[...].astype(F32)
    before_w = weights[...].astype(BF16)

    settle(tiles.at[pl.ds(0, len(AROUND))], recv_a.at[0])
    settle(tiles.at[pl.ds(0, len(AROUND))], send_a.at[0])

    half_lane = lax.broadcasted_iota(jnp.int32, (4, 128), 1) < SLOTS
    halves = []
    for p in range(9):
        halves.append(tiles[3 * p + 1])
        halves.append(jnp.where(half_lane, tiles[3 * p + 2], tiles[3 * p]))
    packed = [jnp.concatenate([halves[t], halves[t + 9]], axis=0) for t in range(9)]
    own8 = jnp.concatenate([own_tile, own_tile], axis=0)
    lane8 = lax.broadcasted_iota(jnp.int32, (8, 128), 1)
    others, centers = [], []
    for j in range(8):
        goal = (target + LEVEL * level)[:, 128 * j : 128 * (j + 1)]
        spot = jnp.broadcast_to(jnp.bitwise_and(goal, 127), (8, 128))
        which = lax.shift_right_logical(goal, 7)
        late = which >= 9
        which = jnp.broadcast_to(jnp.where(late, which - 9, which), (8, 128))
        found = jnp.zeros((8, 128), F32)
        for t in range(9):
            picked = jnp.take_along_axis(packed[t], spot, axis=1)
            found = jnp.where(which == t, picked, found)
        others.append(jnp.where(jnp.broadcast_to(late, (4, 128)), found[4:8], found[0:4]))
        mine = jnp.take_along_axis(own8, lax.shift_right_logical(lane8, 3) + GROUP * j, axis=1)
        centers.append(mine[0:4])
    other = jnp.concatenate(others, axis=1)
    center = jnp.concatenate(centers, axis=1)

    d_x, d_y, d_z = (offsets[c] + (other[c : c + 1] - center[c : c + 1]) for c in range(3))
    distance = jnp.sqrt(d_x * d_x + d_y * d_y + d_z * d_z)
    inverse = 1.0 / distance
    u_x, u_y, u_z = d_x * inverse, d_y * inverse, d_z * inverse
    angular = [
        jnp.ones_like(u_x),
        u_x,
        u_y,
        u_z,
        ROOT3 * u_x * u_y,
        ROOT3 * u_y * u_z,
        0.5 * (3.0 * u_z * u_z - 1.0),
        ROOT3 * u_x * u_z,
        0.5 * ROOT3 * (u_x * u_x - u_y * u_y),
    ]
    ratio = distance * (1.0 / CUTOFF)
    inside = 1.0 - ratio * ratio
    index8 = lax.broadcasted_iota(jnp.int32, (8, EDGES), 0)
    mu = (index8.astype(F32) + 0.5) * (CUTOFF / NBASIS)
    apart = distance - mu
    bell = jnp.exp(-SHARPNESS * apart * apart)
    basis = bell * (inside * inside)
    basis_d = bell * (-2.0 * SHARPNESS * apart * (inside * inside) - ratio * inside)
    hot_center = (index8.astype(F32) == center[3:4]).astype(F32)
    hot_other = (index8.astype(F32) == other[3:4]).astype(F32)
    features = jnp.concatenate([basis, hot_center, hot_other], axis=0)
    features = jnp.transpose(features).astype(BF16)

    group_mask = (
        lax.shift_right_logical(lax.broadcasted_iota(jnp.int32, (GROUP, 128), 1), 3)
        == lax.broadcasted_iota(jnp.int32, (GROUP, 128), 0)
    ).astype(F32)
    members = (
        lax.shift_right_logical(lax.broadcasted_iota(jnp.int32, (ATOMS, EDGES), 1), 3)
        == lax.broadcasted_iota(jnp.int32, (ATOMS, EDGES), 0)
    ).astype(F32).astype(BF16)
    levels = ((0, 1), (1, 4), (4, 9))
    update_w = [update_ref[WIDTH * l : WIDTH * (l + 1), :] for l in range(3)]

    def gathered(buffers, j):
        return jnp.concatenate(
            [
                buffer[GROUP * (stop - start) * j : GROUP * (stop - start) * (j + 1), :]
                for buffer, (start, stop) in zip(buffers, levels)
            ],
            axis=0,
        )

    def placed(buffers, j, value):
        for buffer, (start, stop) in zip(buffers, levels):
            rows_l = GROUP * (stop - start)
            buffer[rows_l * j : rows_l * (j + 1), :] = value[GROUP * start : GROUP * stop]

    values = (value_0, value_1, value_2)
    mixes = (mixed_0, mixed_1, mixed_2)
    half_edges = EDGES // CELLS_Z
    half_groups = GROUPS // CELLS_Z
    yz = {}
    moved_c = {0: [], 1: [], -1: []}
    for z in range(CELLS_Z):
        block = slice(half_edges * z, half_edges * (z + 1))
        before = dot(features[block, :], before_w)
        gate = sigmoid(before)
        act = before * gate
        act_d[block, :] = gate + act * (1.0 - gate)
        mixed = dot(act.astype(BF16), mix_ref[...])
        gate = sigmoid(mixed)
        latent = mixed * gate
        mix_d[block, :] = gate + latent * (1.0 - gate)
        env_buf[block, :] = dot(latent.astype(BF16), env_ref[...]).astype(BF16)
        for j in range(half_groups * z, half_groups * (z + 1)):
            span = slice(128 * j, 128 * (j + 1))
            spread_y = jnp.concatenate([angular[m][:, span] * group_mask for m in range(9)], axis=0)
            diag_a[j] = spread_y.astype(BF16)
            diag_at[j] = jnp.transpose(diag_a[j])
            placed(values, j, (dot(diag_a[j], env_buf[span, :]) * (1.0 / NEIGH)).astype(BF16))
        for value, mixed_l, weight, (start, stop) in zip(values, mixes, update_w, levels):
            rows_l = GROUP * (stop - start) * half_groups
            span = slice(rows_l * z, rows_l * (z + 1))
            mixed_l[span, :] = dot(value[span, :], weight).astype(BF16)
        update = jnp.concatenate(
            [dot(diag_at[j], gathered(mixes, j)) for j in range(half_groups * z, half_groups * (z + 1))], axis=0
        )
        summed = latent + update
        gate = sigmoid(summed)
        edge = summed * gate
        upd_d[block, :] = gate + edge * (1.0 - gate)
        edge_buf[block, :] = edge
        high, low = split_bf16(edge)
        mine = members[0:SLOTS, 0:half_edges]
        own_rows = pl.ds(SLOTS * z, SLOTS)
        table[4, SLOTS * z : SLOTS * (z + 1), :] = ((dot(mine, high) + dot(mine, low)) * (1.0 / NEIGH)).astype(BF16)
        for k, (dy, dz) in enumerate(PARTNERS):
            if dz == (-1 if z == 0 else 1):
                continue
            rows_there = own_rows if dz == 0 else pl.ds(*ROWS[dz])
            copy = remote(
                table.at[4, own_rows],
                table.at[4 + dy, rows_there],
                send_c.at[0],
                recv_c.at[k + 8 * z],
                device(0, -dy, -dz),
            )
            copy.start()
            yz[dy, dz, z] = copy
        moved_c[0] += forward(
            table.at[4, own_rows], lambda a, own_rows=own_rows: table.at[a + 1, own_rows], send_c, recv_x, z
        )

    k = CELLS_Z
    for (dy, dz, z), copy in sorted(yz.items(), key=lambda item: (item[0][2], PIECE_ORDER[item[0][0]])):
        copy.wait_recv()
        rows_here = pl.ds(SLOTS * z, SLOTS) if dz == 0 else pl.ds(*ROWS[dz])
        moved_c[dy] += forward(
            table.at[4 + dy, rows_here],
            lambda a, dy=dy, rows_here=rows_here: table.at[a + 1 + dy, rows_here],
            send_c,
            recv_x,
            k,
        )
        k += 1
    here = dot(onehot[...], jnp.concatenate([table[3], table[4], table[5]], axis=0))
    beside = jnp.zeros((EDGES, 2 * WIDTH), F32)
    for e in (1, 2, 0):
        for copy in moved_c[e - 1]:
            copy.wait_recv()
        pair_e = jnp.concatenate([table[e], table[6 + e]], axis=1)
        beside = beside + dot(onehot[:, PLANE * e : PLANE * (e + 1)], pair_e)
    levels_e = level_col[...]
    other_latent = jnp.where(
        levels_e == 1.0, here, jnp.where(levels_e == 0.0, beside[:, 0:WIDTH], beside[:, WIDTH : 2 * WIDTH])
    )

    edge = edge_buf[...]
    product = (edge * other_latent).astype(BF16)
    second_w = second_ref[...]
    readout = readout_ref[...]
    hidden_in = dot(product, second_w)
    gate = sigmoid(hidden_in)
    hidden = hidden_in * gate
    hidden_g = (readout * (gate + hidden * (1.0 - gate))).astype(BF16)
    product_g = dot(hidden_g, second_w, NT).astype(BF16).astype(F32)
    other_g = (product_g * edge).astype(BF16)
    beside_g = jnp.concatenate([other_g * level_mask[0], other_g * level_mask[2]], axis=1)
    here_g = other_g * level_mask[1]
    edge_buf[...] = product_g * other_latent

    moved_x = {}
    for e, chunks in GRAD_ORDER:
        grads = dot(onehot_t[PLANE * e : PLANE * (e + 1), :], beside_g).astype(BF16)
        grad_send[0, e] = grads[:, 0:WIDTH]
        grad_send[1, e] = grads[:, WIDTH : 2 * WIDTH]
        for e_sent, c in chunks:
            chunk = pl.ds(*(GRAD_OWN if c else GRAD_ENDS))
            for order, side in enumerate(sides):
                copy = remote(
                    grad_send.at[side, e_sent, chunk],
                    grad_recv.at[side, e_sent, chunk],
                    send_c.at[2],
                    recv_d.at[6 * side + 2 * e_sent + c],
                    x_device(side),
                )
                copy.start()
                moved_x[order, e_sent, c] = copy
    middle_grad = dot(onehot_t[...], here_g)
    plane_sum = {e: middle_grad[PLANE * e : PLANE * (e + 1)] for e in range(3)}

    high, low = split_bf16(hidden * readout)
    atom_terms = dot(members, high) + dot(members, low)
    energy = dot(jnp.ones((8, WIDTH), F32), atom_terms, NT, HIGH)

    for e, c in ((0, 0), (2, 0), (0, 1), (2, 1), (1, 0)):
        moved_x[0, e, c].wait_recv()
        moved_x[1, e, c].wait_recv()
        first, count = GRAD_OWN if c else GRAD_ENDS
        arrived = slice(first, first + count)
        plane_send[e, arrived, :] = (
            plane_sum[e][arrived] + grad_recv[0, e, arrived, :].astype(F32) + grad_recv[1, e, arrived, :].astype(F32)
        ).astype(BF16)
        for k, (dy, dz) in enumerate(PARTNERS):
            if dy == e - 1 and (dz == 0) == (c == 1):
                copy = remote(
                    plane_send.at[e, pl.ds(*ROWS[dz])],
                    plane_recv.at[pl.ds(*SLOTS_YZ[k])],
                    send_c.at[3],
                    recv_c.at[16],
                    device(0, dy, dz),
                )
                copy.start()
    moved_x[0, 1, 1].wait_recv()
    moved_x[1, 1, 1].wait_recv()
    own_sum = plane_sum[1][0:128] + grad_recv[0, 1, 0:128, :].astype(F32) + grad_recv[1, 1, 0:128, :].astype(F32)
    settle(plane_recv, send_c.at[0])
    settle(table.at[pl.ds(0, 6)], send_c.at[1])
    settle(grad_send, send_c.at[2])
    settle(plane_recv, send_c.at[3])
    settle(plane_recv, recv_c.at[16])
    parts = {0: own_sum}
    for k, (dy, dz) in enumerate(PARTNERS):
        first, count = SLOTS_YZ[k]
        got = plane_recv[first : first + count, :].astype(F32)
        parts[dz] = got if dz not in parts else parts[dz] + got
    owned = parts[0] + jnp.concatenate([parts[1], parts[-1]], axis=0)

    owned_edges = jnp.broadcast_to((owned * (1.0 / NEIGH))[:, None, :], (ATOMS, NEIGH, WIDTH)).reshape(EDGES, WIDTH)
    summed_g = (edge_buf[...] + owned_edges) * upd_d[...]
    edge_buf[...] = summed_g
    summed_b[...] = summed_g.astype(BF16)
    for j in range(GROUPS):
        span = slice(128 * j, 128 * (j + 1))
        placed(values, j, dot(diag_a[j], summed_b[span, :]).astype(BF16))
    for value, weight in zip(values, update_w):
        value[...] = (dot(value[...], weight, NT) * (1.0 / NEIGH)).astype(BF16)
    angular_g = [[] for _ in range(9)]
    for j in range(GROUPS):
        span = slice(128 * j, 128 * (j + 1))
        value_g = gathered(values, j)
        latent_buf[span, :] = dot(diag_at[j], value_g)
        all_g = dot(
            jnp.concatenate([gathered(mixes, j), value_g], axis=1),
            jnp.concatenate([summed_b[span, :], env_buf[span, :]], axis=1),
            NT,
        )
        for m in range(1, 9):
            angular_g[m].append(
                jnp.sum(all_g[GROUP * m : GROUP * (m + 1)] * group_mask, axis=0, keepdims=True)
            )
    latent_g = dot(latent_buf[...].astype(BF16), env_ref[...], NT).astype(BF16).astype(F32)
    mixed_g = ((edge_buf[...] + latent_g) * mix_d[...]).astype(BF16)
    act_g = dot(mixed_g, mix_ref[...], NT).astype(BF16).astype(F32)
    before_g = (act_g * act_d[...]).astype(BF16)
    basis_g = dot(radial_ref[...], before_g, NT).astype(BF16).astype(F32)

    distance_g = jnp.sum(basis_g * basis_d, axis=0, keepdims=True)
    g = [jnp.concatenate(parts_m, axis=1) if parts_m else None for parts_m in angular_g]
    gu_x = g[1] + ROOT3 * (u_y * g[4] + u_z * g[7] + u_x * g[8])
    gu_y = g[2] + ROOT3 * (u_x * g[4] + u_z * g[5] - u_y * g[8])
    gu_z = g[3] + ROOT3 * (u_y * g[5] + u_x * g[7]) + 3.0 * u_z * g[6]
    along = distance_g - inverse * (u_x * gu_x + u_y * gu_y + u_z * gu_z)
    pull = [-(gu * inverse + u * along) for gu, u in ((gu_x, u_x), (gu_y, u_y), (gu_z, u_z))]
    pull4 = jnp.concatenate(pull + [jnp.zeros_like(u_x)], axis=0)
    high = pull4.astype(BF16).astype(F32)
    pull8 = jnp.concatenate([high, pull4 - high], axis=0)

    pulls = jnp.concatenate([jnp.where(level == a, pull8, 0.0) for a in range(3)], axis=0).astype(BF16)
    spread_f = dot(pulls, onehot_t[...], NT)
    for a in range(3):
        level_f = spread_f[8 * a : 8 * a + 4] + spread_f[8 * a + 4 : 8 * a + 8]
        for i in range(6):
            force_tab[3 * a + i // 2, i % 2] = level_f[:, 128 * i : 128 * (i + 1)]
    for k, (dx, dy, dz) in enumerate(AROUND):
        copy = remote(
            force_tab.at[3 * dx + dy + 4, 1 if dz else 0],
            force_recv.at[k],
            send_a.at[1],
            recv_a.at[1],
            device(dx, dy, dz),
        )
        copy.start()
    both = dot(pull8.astype(BF16), members, NT)
    own_f = both[0:4] + both[4:8]
    settle(force_recv, recv_a.at[1])
    total = force_tab[4, 0] - own_f
    ends = {}
    for k, (dx, dy, dz) in enumerate(AROUND):
        got = force_recv[k]
        if dz == 0:
            total = total + got
        else:
            ends[dz] = got if dz not in ends else ends[dz] + got
    total = total + jnp.where(half_lane, ends[1], ends[-1])
    energy_ref[0, 0] = jnp.concatenate(
        [energy[0:1, SLOTS * z : SLOTS * (z + 1)] for z in range(CELLS_Z)], axis=0
    )
    force_ref[0, 0] = jnp.concatenate(
        [
            jnp.concatenate([total[c : c + 1, SLOTS * z : SLOTS * (z + 1)] for c in range(3)], axis=1)
            for z in range(CELLS_Z)
        ],
        axis=0,
    )
    settle(force_recv, send_a.at[1])


def copy_out(energy_in, force_in, energy_out, force_out, sem):
    copies = [
        pltpu.make_async_copy(energy_in, energy_out, sem.at[0]),
        pltpu.make_async_copy(force_in, force_out, sem.at[1]),
    ]
    for copy in copies:
        copy.start()
    for copy in copies:
        copy.wait()


def on_device(
    positions,
    species,
    neighbors,
    center_table,
    neighbor_table,
    radial_weight,
    mix_weight,
    env_weight,
    update_weight,
    second_weight,
    readout,
):
    dma = pltpu.SemaphoreType.DMA
    vmem = pltpu.VMEM
    cells = positions.shape[:3]
    args = (
        positions,
        species,
        neighbors,
        center_table,
        neighbor_table,
        radial_weight,
        mix_weight,
        env_weight,
        update_weight,
        second_weight,
        readout.reshape(1, WIDTH),
    )
    energies, forces = pl.pallas_call(
        kernel,
        out_shape=(pltpu.VMEM((*cells, SLOTS), F32), pltpu.VMEM((*cells, 3 * SLOTS), F32)),
        in_specs=[pl.BlockSpec(memory_space=pl.ANY)] * len(args),
        out_specs=[pl.BlockSpec(memory_space=pltpu.VMEM)] * 2,
        scratch_shapes=[
            *(vmem(arg.shape, arg.dtype) for arg in args),
            dma((len(args),)),
            vmem((27, 4, 128), F32),
            vmem((EDGES, LEVEL), BF16),
            vmem((LEVEL, EDGES), BF16),
            vmem((GROUPS, 128, 128), F32),
            vmem((EDGES, 128), F32),
            vmem((3, EDGES, 128), BF16),
            vmem((9, PLANE, WIDTH), BF16),
            vmem((24, WIDTH), F32),
            vmem((EDGES, WIDTH), F32),
            vmem((EDGES, WIDTH), F32),
            vmem((EDGES, WIDTH), F32),
            vmem((EDGES, WIDTH), BF16),
            vmem((GROUPS, 9 * GROUP, 128), BF16),
            vmem((GROUPS, 128, 9 * GROUP), BF16),
            vmem((1 * ATOMS, WIDTH), BF16),
            vmem((3 * ATOMS, WIDTH), BF16),
            vmem((5 * ATOMS, WIDTH), BF16),
            vmem((1 * ATOMS, WIDTH), BF16),
            vmem((3 * ATOMS, WIDTH), BF16),
            vmem((5 * ATOMS, WIDTH), BF16),
            vmem((EDGES, WIDTH), BF16),
            vmem((EDGES, WIDTH), F32),
            vmem((EDGES, WIDTH), F32),
            vmem((2, 3, PLANE, WIDTH), BF16),
            vmem((2, 3, PLANE, WIDTH), BF16),
            vmem((3, PLANE, WIDTH), BF16),
            vmem((640, WIDTH), BF16),
            vmem((9, 2, 4, 128), F32),
            vmem((26, 4, 128), F32),
            dma((2,)),
            dma((2,)),
            dma((4,)),
            dma((17,)),
            dma((24,)),
            dma((12,)),
        ],
        compiler_params=pltpu.CompilerParams(collective_id=0, has_side_effects=True),
    )(*args)
    return pl.pallas_call(
        copy_out,
        out_shape=(jax.ShapeDtypeStruct((*cells, SLOTS), F32), jax.ShapeDtypeStruct((*cells, 3 * SLOTS), F32)),
        in_specs=[pl.BlockSpec(memory_space=pl.ANY)] * 2,
        out_specs=[pl.BlockSpec(memory_space=pl.ANY)] * 2,
        scratch_shapes=[dma((2,))],
    )(
        pltpu.with_memory_space_constraint(energies, pltpu.VMEM),
        pltpu.with_memory_space_constraint(forces, pltpu.VMEM),
    )


def solution(mesh):
    placed = (
        P("gx", "gy", "gz", None),
        P("gx", "gy", "gz", None),
        P("gx", "gy", "gz", None),
        P(),
        P(),
        P(),
        P(),
        P(),
        P(),
        P(),
        P(),
    )
    return jax.shard_map(
        on_device,
        mesh=mesh,
        in_specs=placed,
        out_specs=(P("gx", "gy", "gz", None), P("gx", "gy", "gz", None)),
        check_vma=False,
    )
```

```python
import itertools
import math

import jax
import jax.numpy as jnp
from jax import lax
from jax.experimental import pallas as pl
from jax.experimental.pallas import tpu as pltpu
from jax.sharding import PartitionSpec as P

MESH = pl.DeviceIdType.MESH
F32 = jnp.float32
BF16 = jnp.bfloat16
HIGH = lax.Precision.HIGHEST

NEIGH = 8
SLOTS = 64
CUTOFF = 4.0
SHARPNESS = 2.0
NBASIS = 8
CELLS_Z = 2
ATOMS = CELLS_Z * SLOTS
EDGES = ATOMS * NEIGH
WIDTH = 128
PLANE = 256
LEVEL = 3 * PLANE
GROUP = 16
GROUPS = ATOMS // GROUP
ROOT3 = math.sqrt(3.0)
PIECE_ORDER = {0: 0, 1: 1, -1: 2}
GRAD_ENDS, GRAD_OWN = (128, 128), (0, 128)
GRAD_ORDER = ((0, ((0, 0),)), (2, ((2, 0), (0, 1), (2, 1))), (1, ((1, 0), (1, 1))))

PARTNERS = ((1, -1), (-1, 1), (1, 1), (-1, -1), (0, 1), (0, -1), (1, 0), (-1, 0))
AROUND = sorted(
    (d for d in itertools.product((-1, 0, 1), repeat=3) if any(d)), key=lambda d: -sum(abs(c) for c in d)
)
ROWS = {0: (0, 128), 1: (128, 64), -1: (192, 64)}
SLOTS_YZ = tuple((64 * k, 64) if dz else (384 + 128 * (k - 6), 128) for k, (dy, dz) in enumerate(PARTNERS))


def split_bf16(value):
    high = value.astype(BF16)
    return high, (value - high.astype(F32)).astype(BF16)


def dot(a, b, dims=((1,), (0,)), precision=None):
    return lax.dot_general(a, b, (dims, ((), ())), preferred_element_type=F32, precision=precision)


NT = ((1,), (1,))


def sigmoid(value):
    return 0.5 + 0.5 * jnp.tanh(0.5 * value)


def kernel(
    pos_in,
    spec_in,
    nbr_in,
    center_in,
    neighbor_in,
    radial_in,
    mix_in,
    env_in,
    update_in,
    second_in,
    readout_in,
    energy_ref,
    force_ref,
    pos_ref,
    spec_ref,
    nbr_ref,
    center_ref,
    neighbor_ref,
    radial_ref,
    mix_ref,
    env_ref,
    update_ref,
    second_ref,
    readout_ref,
    load_sem,
    tiles,
    onehot,
    onehot_t,
    target_col,
    level_col,
    level_mask,
    table,
    weights,
    act_d,
    mix_d,
    upd_d,
    env_buf,
    diag_a,
    diag_at,
    value_0,
    value_1,
    value_2,
    mixed_0,
    mixed_1,
    mixed_2,
    summed_b,
    latent_buf,
    edge_buf,
    grad_send,
    grad_recv,
    plane_send,
    plane_recv,
    force_tab,
    force_recv,
    send_a,
    recv_a,
    send_c,
    recv_c,
    recv_x,
    recv_d,
):
    size_x, size_y, size_z = lax.axis_size("gx"), lax.axis_size("gy"), lax.axis_size("gz")
    my_x, my_y, my_z = lax.axis_index("gx"), lax.axis_index("gy"), lax.axis_index("gz")

    near = []
    for index, size in ((my_x, size_x), (my_y, size_y), (my_z, size_z)):
        near.append(
            (index, jnp.where(index == size - 1, 0, index + 1), jnp.where(index == 0, size - 1, index - 1))
        )

    def device(dx, dy, dz):
        return near[0][dx], near[1][dy], near[2][dz]

    def settle(ref, sem):
        pltpu.make_async_copy(ref, ref, sem).wait()

    def remote(src, dst, send, recv, target):
        return pltpu.make_async_remote_copy(
            src_ref=src, dst_ref=dst, send_sem=send, recv_sem=recv, device_id=target, device_id_type=MESH
        )

    sources = (
        pos_in, spec_in, nbr_in, center_in, neighbor_in, radial_in, mix_in, env_in, update_in, second_in, readout_in
    )
    places = (
        pos_ref, spec_ref, nbr_ref, center_ref, neighbor_ref, radial_ref, mix_ref, env_ref, update_ref, second_ref,
        readout_ref,
    )
    loads = [pltpu.make_async_copy(src, dst, load_sem.at[k]) for k, (src, dst) in enumerate(zip(sources, places))]
    for load in loads[:3]:
        load.start()
    barrier = pltpu.get_barrier_semaphore()
    for step in AROUND:
        pl.semaphore_signal(barrier, inc=1, device_id=device(*step), device_id_type=MESH)
    for load in loads[3:]:
        load.start()
    loads[0].wait()
    loads[1].wait()

    coords = pos_ref[0, 0]
    kinds = spec_ref[0, 0].astype(F32)
    rows = [
        jnp.concatenate([coords[z : z + 1, SLOTS * c : SLOTS * (c + 1)] for z in range(CELLS_Z)], axis=1)
        for c in range(3)
    ]
    rows.append(jnp.concatenate([kinds[z : z + 1, :] for z in range(CELLS_Z)], axis=1))
    own_tile = jnp.concatenate(rows, axis=0)
    tiles[13] = own_tile

    pl.semaphore_wait(barrier, len(AROUND))

    far_side = lax.rem(my_x, 2)
    sides = (far_side, 1 - far_side)

    def x_device(side):
        return jnp.where(side == 0, near[0][-1], near[0][1]), my_y, my_z

    def forward(source, dest, send, recv, k):
        copies = []
        for side in sides[::-1]:
            copy = remote(
                source,
                dest(3 * (2 * side)),
                send.at[1],
                recv.at[2 * k + side],
                x_device(1 - side),
            )
            copy.start()
            copies.append(copy)
        return copies

    def tile_of(dx, dy, dz):
        return 9 * (dx + 1) + 3 * (dy + 1) + (dz + 1)

    for dx, dy, dz in AROUND:
        copy = remote(
            tiles.at[13], tiles.at[tile_of(dx, dy, dz)], send_a.at[0], recv_a.at[0], device(-dx, -dy, -dz)
        )
        copy.start()

    loads[2].wait()
    codes = nbr_ref[0, 0]
    offset_code = lax.shift_right_logical(codes, 6)
    slot = jnp.bitwise_and(codes, SLOTS - 1)
    column_code = lax.shift_right_logical(offset_code * 171, 9)
    row_z = offset_code - 3 * column_code
    own_z = lax.broadcasted_iota(jnp.int32, codes.shape, 0)
    place = jnp.bitwise_and(row_z + own_z + 3, 3)
    step_a = lax.shift_right_logical(column_code * 171, 9)
    step_e = column_code - 3 * step_a

    def flat(value):
        return jnp.concatenate([value[z : z + 1, :] for z in range(CELLS_Z)], axis=1)

    target = flat((step_e * 4 + place) * SLOTS + slot)
    level = flat(step_a)
    offsets = [flat(step - 1).astype(F32) for step in (step_a, step_e, row_z)]

    row_kinds = [target[:, 128 * j : 128 * (j + 1)].astype(F32) for j in range(8)]
    row_kinds += [level[:, 128 * j : 128 * (j + 1)].astype(F32) for j in range(8)]
    columns = jnp.transpose(jnp.concatenate(row_kinds + [jnp.zeros((112, 128), F32)], axis=0))
    for j in range(8):
        target_col[j] = jnp.broadcast_to(columns[:, j : j + 1], (128, 128))
        level_col[128 * j : 128 * (j + 1), :] = jnp.broadcast_to(columns[:, 8 + j : 9 + j], (128, 128))

    def build(j, carry):
        first = pl.multiple_of(j * 128, 128)
        level_j = level_col[pl.ds(first, 128), :]
        for a in range(3):
            level_mask[a, pl.ds(first, 128), :] = (level_j == float(a)).astype(F32).astype(BF16)
        lane = lax.broadcasted_iota(jnp.int32, (128, 128), 1).astype(F32)
        column = target_col[j]
        for t in range(LEVEL // 128):
            onehot[pl.ds(first, 128), 128 * t : 128 * (t + 1)] = (
                (column == lane + float(128 * t)).astype(F32).astype(BF16)
            )
        return carry

    lax.fori_loop(0, GROUPS, build, 0)

    def build_t(t, carry):
        first = pl.multiple_of(t * 128, 128)
        row = lax.broadcasted_iota(jnp.int32, (128, EDGES), 0) + first
        onehot_t[pl.ds(first, 128), :] = (row == target).astype(F32).astype(BF16)
        return carry

    lax.fori_loop(0, LEVEL // 128, build_t, 0)

    for load in loads[3:]:
        load.wait()
    weights[...] = jnp.zeros_like(weights)
    weights[0:NBASIS, :] = radial_ref[...].astype(F32)
    spec_count = center_ref.shape[0]
    weights[8 : 8 + spec_count, :] = center_ref[...].astype(F32)
    weights[16 : 16 + spec_count, :] = neighbor_ref[...].astype(F32)
    before_w = weights[...].astype(BF16)

    settle(tiles.at[pl.ds(0, len(AROUND))], recv_a.at[0])
    settle(tiles.at[pl.ds(0, len(AROUND))], send_a.at[0])

    half_lane = lax.broadcasted_iota(jnp.int32, (4, 128), 1) < SLOTS
    halves = []
    for p in range(9):
        halves.append(tiles[3 * p + 1])
        halves.append(jnp.where(half_lane, tiles[3 * p + 2], tiles[3 * p]))
    packed = [jnp.concatenate([halves[t], halves[t + 9]], axis=0) for t in range(9)]
    own8 = jnp.concatenate([own_tile, own_tile], axis=0)
    lane8 = lax.broadcasted_iota(jnp.int32, (8, 128), 1)
    others, centers = [], []
    for j in range(8):
        goal = (target + LEVEL * level)[:, 128 * j : 128 * (j + 1)]
        spot = jnp.broadcast_to(jnp.bitwise_and(goal, 127), (8, 128))
        which = lax.shift_right_logical(goal, 7)
        late = which >= 9
        which = jnp.broadcast_to(jnp.where(late, which - 9, which), (8, 128))
        found = jnp.zeros((8, 128), F32)
        for t in range(9):
            picked = jnp.take_along_axis(packed[t], spot, axis=1)
            found = jnp.where(which == t, picked, found)
        others.append(jnp.where(jnp.broadcast_to(late, (4, 128)), found[4:8], found[0:4]))
        mine = jnp.take_along_axis(own8, lax.shift_right_logical(lane8, 3) + GROUP * j, axis=1)
        centers.append(mine[0:4])
    other = jnp.concatenate(others, axis=1)
    center = jnp.concatenate(centers, axis=1)

    d_x, d_y, d_z = (offsets[c] + (other[c : c + 1] - center[c : c + 1]) for c in range(3))
    distance = jnp.sqrt(d_x * d_x + d_y * d_y + d_z * d_z)
    inverse = 1.0 / distance
    u_x, u_y, u_z = d_x * inverse, d_y * inverse, d_z * inverse
    angular = [
        jnp.ones_like(u_x),
        u_x,
        u_y,
        u_z,
        ROOT3 * u_x * u_y,
        ROOT3 * u_y * u_z,
        0.5 * (3.0 * u_z * u_z - 1.0),
        ROOT3 * u_x * u_z,
        0.5 * ROOT3 * (u_x * u_x - u_y * u_y),
    ]
    ratio = distance * (1.0 / CUTOFF)
    inside = 1.0 - ratio * ratio
    index8 = lax.broadcasted_iota(jnp.int32, (8, EDGES), 0)
    mu = (index8.astype(F32) + 0.5) * (CUTOFF / NBASIS)
    apart = distance - mu
    bell = jnp.exp(-SHARPNESS * apart * apart)
    basis = bell * (inside * inside)
    basis_d = bell * (-2.0 * SHARPNESS * apart * (inside * inside) - ratio * inside)
    hot_center = (index8.astype(F32) == center[3:4]).astype(F32)
    hot_other = (index8.astype(F32) == other[3:4]).astype(F32)
    features = jnp.concatenate([basis, hot_center, hot_other], axis=0)
    features = jnp.transpose(features).astype(BF16)

    group_mask = (
        lax.shift_right_logical(lax.broadcasted_iota(jnp.int32, (GROUP, 128), 1), 3)
        == lax.broadcasted_iota(jnp.int32, (GROUP, 128), 0)
    ).astype(F32)
    members = (
        lax.shift_right_logical(lax.broadcasted_iota(jnp.int32, (ATOMS, EDGES), 1), 3)
        == lax.broadcasted_iota(jnp.int32, (ATOMS, EDGES), 0)
    ).astype(F32).astype(BF16)
    levels = ((0, 1), (1, 4), (4, 9))
    update_w = [update_ref[WIDTH * l : WIDTH * (l + 1), :] for l in range(3)]

    def gathered(buffers, j):
        return jnp.concatenate(
            [
                buffer[GROUP * (stop - start) * j : GROUP * (stop - start) * (j + 1), :]
                for buffer, (start, stop) in zip(buffers, levels)
            ],
            axis=0,
        )

    def placed(buffers, j, value):
        for buffer, (start, stop) in zip(buffers, levels):
            rows_l = GROUP * (stop - start)
            buffer[rows_l * j : rows_l * (j + 1), :] = value[GROUP * start : GROUP * stop]

    values = (value_0, value_1, value_2)
    mixes = (mixed_0, mixed_1, mixed_2)
    half_edges = EDGES // CELLS_Z
    half_groups = GROUPS // CELLS_Z
    yz = {}
    moved_c = {0: [], 1: [], -1: []}
    for z in range(CELLS_Z):
        block = slice(half_edges * z, half_edges * (z + 1))
        before = dot(features[block, :], before_w)
        gate = sigmoid(before)
        act = before * gate
        act_d[block, :] = gate + act * (1.0 - gate)
        mixed = dot(act.astype(BF16), mix_ref[...])
        gate = sigmoid(mixed)
        latent = mixed * gate
        mix_d[block, :] = gate + latent * (1.0 - gate)
        env_buf[block, :] = dot(latent.astype(BF16), env_ref[...]).astype(BF16)
        for j in range(half_groups * z, half_groups * (z + 1)):
            span = slice(128 * j, 128 * (j + 1))
            spread_y = jnp.concatenate([angular[m][:, span] * group_mask for m in range(9)], axis=0)
            diag_a[j] = spread_y.astype(BF16)
            diag_at[j] = jnp.transpose(diag_a[j])
            placed(values, j, (dot(diag_a[j], env_buf[span, :]) * (1.0 / NEIGH)).astype(BF16))
        for value, mixed_l, weight, (start, stop) in zip(values, mixes, update_w, levels):
            rows_l = GROUP * (stop - start) * half_groups
            span = slice(rows_l * z, rows_l * (z + 1))
            mixed_l[span, :] = dot(value[span, :], weight).astype(BF16)
        update = jnp.concatenate(
            [dot(diag_at[j], gathered(mixes, j)) for j in range(half_groups * z, half_groups * (z + 1))], axis=0
        )
        summed = latent + update
        gate = sigmoid(summed)
        edge = summed * gate
        upd_d[block, :] = gate + edge * (1.0 - gate)
        edge_buf[block, :] = edge
        mine = members[0:SLOTS, 0:half_edges]
        own_rows = pl.ds(SLOTS * z, SLOTS)
        table[4, SLOTS * z : SLOTS * (z + 1), :] = (dot(mine, edge.astype(BF16)) * (1.0 / NEIGH)).astype(BF16)
        for k, (dy, dz) in enumerate(PARTNERS):
            if dz == (-1 if z == 0 else 1):
                continue
            rows_there = own_rows if dz == 0 else pl.ds(*ROWS[dz])
            copy = remote(
                table.at[4, own_rows],
                table.at[4 + dy, rows_there],
                send_c.at[0],
                recv_c.at[k + 8 * z],
                device(0, -dy, -dz),
            )
            copy.start()
            yz[dy, dz, z] = copy
        moved_c[0] += forward(
            table.at[4, own_rows], lambda a, own_rows=own_rows: table.at[a + 1, own_rows], send_c, recv_x, z
        )

    k = CELLS_Z
    for (dy, dz, z), copy in sorted(yz.items(), key=lambda item: (item[0][2], PIECE_ORDER[item[0][0]])):
        copy.wait_recv()
        rows_here = pl.ds(SLOTS * z, SLOTS) if dz == 0 else pl.ds(*ROWS[dz])
        moved_c[dy] += forward(
            table.at[4 + dy, rows_here],
            lambda a, dy=dy, rows_here=rows_here: table.at[a + 1 + dy, rows_here],
            send_c,
            recv_x,
            k,
        )
        k += 1
    here = dot(onehot[...], jnp.concatenate([table[3], table[4], table[5]], axis=0))
    beside = jnp.zeros((EDGES, 2 * WIDTH), F32)
    for e in (1, 2, 0):
        for copy in moved_c[e - 1]:
            copy.wait_recv()
        pair_e = jnp.concatenate([table[e], table[6 + e]], axis=1)
        beside = beside + dot(onehot[:, PLANE * e : PLANE * (e + 1)], pair_e)
    levels_e = level_col[...]
    other_latent = jnp.where(
        levels_e == 1.0, here, jnp.where(levels_e == 0.0, beside[:, 0:WIDTH], beside[:, WIDTH : 2 * WIDTH])
    )

    edge = edge_buf[...]
    product = (edge * other_latent).astype(BF16)
    second_w = second_ref[...]
    readout = readout_ref[...]
    hidden_in = dot(product, second_w)
    gate = sigmoid(hidden_in)
    hidden = hidden_in * gate
    hidden_g = (readout * (gate + hidden * (1.0 - gate))).astype(BF16)
    product_g = dot(hidden_g, second_w, NT).astype(BF16).astype(F32)
    other_g = (product_g * edge).astype(BF16)
    beside_g = jnp.concatenate([other_g * level_mask[0], other_g * level_mask[2]], axis=1)
    here_g = other_g * level_mask[1]
    edge_buf[...] = product_g * other_latent

    moved_x = {}
    for e, chunks in GRAD_ORDER:
        grads = dot(onehot_t[PLANE * e : PLANE * (e + 1), :], beside_g).astype(BF16)
        grad_send[0, e] = grads[:, 0:WIDTH]
        grad_send[1, e] = grads[:, WIDTH : 2 * WIDTH]
        for e_sent, c in chunks:
            chunk = pl.ds(*(GRAD_OWN if c else GRAD_ENDS))
            for order, side in enumerate(sides):
                copy = remote(
                    grad_send.at[side, e_sent, chunk],
                    grad_recv.at[side, e_sent, chunk],
                    send_c.at[2],
                    recv_d.at[6 * side + 2 * e_sent + c],
                    x_device(side),
                )
                copy.start()
                moved_x[order, e_sent, c] = copy
    middle_grad = dot(onehot_t[...], here_g)
    plane_sum = {e: middle_grad[PLANE * e : PLANE * (e + 1)] for e in range(3)}

    high, low = split_bf16(hidden * readout)
    atom_terms = dot(members, high) + dot(members, low)
    energy = dot(jnp.ones((8, WIDTH), F32), atom_terms, NT, HIGH)

    for e, c in ((0, 0), (2, 0), (0, 1), (2, 1), (1, 0)):
        moved_x[0, e, c].wait_recv()
        moved_x[1, e, c].wait_recv()
        first, count = GRAD_OWN if c else GRAD_ENDS
        arrived = slice(first, first + count)
        plane_send[e, arrived, :] = (
            plane_sum[e][arrived] + grad_recv[0, e, arrived, :].astype(F32) + grad_recv[1, e, arrived, :].astype(F32)
        ).astype(BF16)
        for k, (dy, dz) in enumerate(PARTNERS):
            if dy == e - 1 and (dz == 0) == (c == 1):
                copy = remote(
                    plane_send.at[e, pl.ds(*ROWS[dz])],
                    plane_recv.at[pl.ds(*SLOTS_YZ[k])],
                    send_c.at[3],
                    recv_c.at[16],
                    device(0, dy, dz),
                )
                copy.start()
    moved_x[0, 1, 1].wait_recv()
    moved_x[1, 1, 1].wait_recv()
    own_sum = plane_sum[1][0:128] + grad_recv[0, 1, 0:128, :].astype(F32) + grad_recv[1, 1, 0:128, :].astype(F32)
    settle(plane_recv, send_c.at[0])
    settle(table.at[pl.ds(0, 6)], send_c.at[1])
    settle(grad_send, send_c.at[2])
    settle(plane_recv, send_c.at[3])
    settle(plane_recv, recv_c.at[16])
    parts = {0: own_sum}
    for k, (dy, dz) in enumerate(PARTNERS):
        first, count = SLOTS_YZ[k]
        got = plane_recv[first : first + count, :].astype(F32)
        parts[dz] = got if dz not in parts else parts[dz] + got
    owned = parts[0] + jnp.concatenate([parts[1], parts[-1]], axis=0)

    owned_edges = jnp.broadcast_to((owned * (1.0 / NEIGH))[:, None, :], (ATOMS, NEIGH, WIDTH)).reshape(EDGES, WIDTH)
    summed_g = (edge_buf[...] + owned_edges) * upd_d[...]
    edge_buf[...] = summed_g
    summed_b[...] = summed_g.astype(BF16)
    for j in range(GROUPS):
        span = slice(128 * j, 128 * (j + 1))
        placed(values, j, dot(diag_a[j], summed_b[span, :]).astype(BF16))
    for value, weight in zip(values, update_w):
        value[...] = (dot(value[...], weight, NT) * (1.0 / NEIGH)).astype(BF16)
    angular_g = [[] for _ in range(9)]
    for j in range(GROUPS):
        span = slice(128 * j, 128 * (j + 1))
        value_g = gathered(values, j)
        latent_buf[span, :] = dot(diag_at[j], value_g)
        all_g = dot(
            jnp.concatenate([gathered(mixes, j)[GROUP:], value_g[GROUP:]], axis=1),
            jnp.concatenate([summed_b[span, :], env_buf[span, :]], axis=1),
            NT,
        )
        for m in range(1, 9):
            angular_g[m].append(
                jnp.sum(all_g[GROUP * (m - 1) : GROUP * m] * group_mask, axis=0, keepdims=True)
            )
    latent_g = dot(latent_buf[...].astype(BF16), env_ref[...], NT).astype(BF16).astype(F32)
    mixed_g = ((edge_buf[...] + latent_g) * mix_d[...]).astype(BF16)
    act_g = dot(mixed_g, mix_ref[...], NT).astype(BF16).astype(F32)
    before_g = (act_g * act_d[...]).astype(BF16)
    basis_g = dot(radial_ref[...], before_g, NT).astype(BF16).astype(F32)

    distance_g = jnp.sum(basis_g * basis_d, axis=0, keepdims=True)
    g = [jnp.concatenate(parts_m, axis=1) if parts_m else None for parts_m in angular_g]
    gu_x = g[1] + ROOT3 * (u_y * g[4] + u_z * g[7] + u_x * g[8])
    gu_y = g[2] + ROOT3 * (u_x * g[4] + u_z * g[5] - u_y * g[8])
    gu_z = g[3] + ROOT3 * (u_y * g[5] + u_x * g[7]) + 3.0 * u_z * g[6]
    along = distance_g - inverse * (u_x * gu_x + u_y * gu_y + u_z * gu_z)
    pull = [-(gu * inverse + u * along) for gu, u in ((gu_x, u_x), (gu_y, u_y), (gu_z, u_z))]
    pull4 = jnp.concatenate(pull + [jnp.zeros_like(u_x)], axis=0)
    high = pull4.astype(BF16).astype(F32)
    pull8 = jnp.concatenate([high, pull4 - high], axis=0)

    pulls = jnp.concatenate([jnp.where(level == a, pull8, 0.0) for a in range(3)], axis=0).astype(BF16)
    spread_f = dot(pulls, onehot_t[...], NT)
    for a in range(3):
        level_f = spread_f[8 * a : 8 * a + 4] + spread_f[8 * a + 4 : 8 * a + 8]
        for i in range(6):
            force_tab[3 * a + i // 2, i % 2] = level_f[:, 128 * i : 128 * (i + 1)]
    for k, (dx, dy, dz) in enumerate(AROUND):
        copy = remote(
            force_tab.at[3 * dx + dy + 4, 1 if dz else 0],
            force_recv.at[k],
            send_a.at[1],
            recv_a.at[1],
            device(dx, dy, dz),
        )
        copy.start()
    both = dot(pull8.astype(BF16), members, NT)
    own_f = both[0:4] + both[4:8]
    settle(force_recv, recv_a.at[1])
    total = force_tab[4, 0] - own_f
    ends = {}
    for k, (dx, dy, dz) in enumerate(AROUND):
        got = force_recv[k]
        if dz == 0:
            total = total + got
        else:
            ends[dz] = got if dz not in ends else ends[dz] + got
    total = total + jnp.where(half_lane, ends[1], ends[-1])
    energy_ref[0, 0] = jnp.concatenate(
        [energy[0:1, SLOTS * z : SLOTS * (z + 1)] for z in range(CELLS_Z)], axis=0
    )
    force_ref[0, 0] = jnp.concatenate(
        [
            jnp.concatenate([total[c : c + 1, SLOTS * z : SLOTS * (z + 1)] for c in range(3)], axis=1)
            for z in range(CELLS_Z)
        ],
        axis=0,
    )
    settle(force_recv, send_a.at[1])


def copy_out(energy_in, force_in, energy_out, force_out, sem):
    copies = [
        pltpu.make_async_copy(energy_in, energy_out, sem.at[0]),
        pltpu.make_async_copy(force_in, force_out, sem.at[1]),
    ]
    for copy in copies:
        copy.start()
    for copy in copies:
        copy.wait()


def on_device(
    positions,
    species,
    neighbors,
    center_table,
    neighbor_table,
    radial_weight,
    mix_weight,
    env_weight,
    update_weight,
    second_weight,
    readout,
):
    dma = pltpu.SemaphoreType.DMA
    vmem = pltpu.VMEM
    cells = positions.shape[:3]
    args = (
        positions,
        species,
        neighbors,
        center_table,
        neighbor_table,
        radial_weight,
        mix_weight,
        env_weight,
        update_weight,
        second_weight,
        readout.reshape(1, WIDTH),
    )
    energies, forces = pl.pallas_call(
        kernel,
        out_shape=(pltpu.VMEM((*cells, SLOTS), F32), pltpu.VMEM((*cells, 3 * SLOTS), F32)),
        in_specs=[pl.BlockSpec(memory_space=pl.ANY)] * len(args),
        out_specs=[pl.BlockSpec(memory_space=pltpu.VMEM)] * 2,
        scratch_shapes=[
            *(vmem(arg.shape, arg.dtype) for arg in args),
            dma((len(args),)),
            vmem((27, 4, 128), F32),
            vmem((EDGES, LEVEL), BF16),
            vmem((LEVEL, EDGES), BF16),
            vmem((GROUPS, 128, 128), F32),
            vmem((EDGES, 128), F32),
            vmem((3, EDGES, 128), BF16),
            vmem((9, PLANE, WIDTH), BF16),
            vmem((24, WIDTH), F32),
            vmem((EDGES, WIDTH), F32),
            vmem((EDGES, WIDTH), F32),
            vmem((EDGES, WIDTH), F32),
            vmem((EDGES, WIDTH), BF16),
            vmem((GROUPS, 9 * GROUP, 128), BF16),
            vmem((GROUPS, 128, 9 * GROUP), BF16),
            vmem((1 * ATOMS, WIDTH), BF16),
            vmem((3 * ATOMS, WIDTH), BF16),
            vmem((5 * ATOMS, WIDTH), BF16),
            vmem((1 * ATOMS, WIDTH), BF16),
            vmem((3 * ATOMS, WIDTH), BF16),
            vmem((5 * ATOMS, WIDTH), BF16),
            vmem((EDGES, WIDTH), BF16),
            vmem((EDGES, WIDTH), F32),
            vmem((EDGES, WIDTH), F32),
            vmem((2, 3, PLANE, WIDTH), BF16),
            vmem((2, 3, PLANE, WIDTH), BF16),
            vmem((3, PLANE, WIDTH), BF16),
            vmem((640, WIDTH), BF16),
            vmem((9, 2, 4, 128), F32),
            vmem((26, 4, 128), F32),
            dma((2,)),
            dma((2,)),
            dma((4,)),
            dma((17,)),
            dma((24,)),
            dma((12,)),
        ],
        compiler_params=pltpu.CompilerParams(collective_id=0, has_side_effects=True),
    )(*args)
    return pl.pallas_call(
        copy_out,
        out_shape=(jax.ShapeDtypeStruct((*cells, SLOTS), F32), jax.ShapeDtypeStruct((*cells, 3 * SLOTS), F32)),
        in_specs=[pl.BlockSpec(memory_space=pl.ANY)] * 2,
        out_specs=[pl.BlockSpec(memory_space=pl.ANY)] * 2,
        scratch_shapes=[dma((2,))],
    )(
        pltpu.with_memory_space_constraint(energies, pltpu.VMEM),
        pltpu.with_memory_space_constraint(forces, pltpu.VMEM),
    )


def solution(mesh):
    placed = (
        P("gx", "gy", "gz", None),
        P("gx", "gy", "gz", None),
        P("gx", "gy", "gz", None),
        P(),
        P(),
        P(),
        P(),
        P(),
        P(),
        P(),
        P(),
    )
    return jax.shard_map(
        on_device,
        mesh=mesh,
        in_specs=placed,
        out_specs=(P("gx", "gy", "gz", None), P("gx", "gy", "gz", None)),
        check_vma=False,
    )
```
